512 devices in a mesh: axial: 64 (over z, x), azim: 8 (over y, core).
Axes of the slice: x: 4, y: 4, z: 16, core: 2. Of those that a mesh axis runs over, the one named last changes fastest.
Arguments:
- state: float32 [14, 512, 64, 128], P(None, 'axial', 'azim'), may hold values from -18 to 18, as said below
- diff_coef: float32 [10], replicated, may hold values from 0.1 to 1
- parcel_state: float32 [8, 1048576], P(None, ('axial', 'azim')), may hold values from -6 to 6, as said below
- parcel_cell: int32 [1048576], P(('axial', 'azim')), may hold values from 0 to 8191
- parcel_dest: int32 [1048576], P(('axial', 'azim')), may hold values from 0 to 4, as said below
- live_count: int32 [512], P(('axial', 'azim')), may hold values from 256 to 2048, as said below
Outputs:
- scalars_new: float32 [10, 512, 64, 128], P(None, 'axial', 'azim')
- velocity_new: float32 [3, 512, 64, 128], P(None, 'axial', 'azim')
- kept_parcels: float32 [8, 1048576], P(None, ('axial', 'azim'))
- arrived: float32 [4, 8, 32768], P(None, None, ('axial', 'azim'))
The draws below stay inside these ranges and needn't reach their ends.
Inputs may be any that keep to these rules, and one draw needn't show every extreme that they name: `state`: component 0 (density) lies in [0.5, 2] and components 5 to 13 (species fractions) in [0, 1]. `parcel_state`: row 0 (mass) lies in [0.2, 2], rows 5 to 7 (offsets) in [0, 1]. Live parcels of a box fill its first live_count slots; boxes at axial index 0 are full. `parcel_dest`: among the live parcels of one box at most 64 have any one destination 1 to 4, and in every box one destination has exactly 64. Entries of slots that are not live are ignored. `parcel_cell`: x * 8 * 128 + y * 128 + z for box-local cell (x, y, z).
All inputs are finite; a program needn't handle non-finite values. Where the reference program divides by a largest or mean magnitude, that divisor is 1e-20 or more.
Results may differ from the reference program's by a relative error of at most 0.0003.
Values sent between devices are 32-bit elements; how exact they have to be, the bound alone decides.
A program may use at most 64 MiB of HBM per device.

```python
import math
import jax
import jax.numpy as jnp
from jax import lax

CX = 8
CY = 8
CZ = 128
NSPEC = 9
NSCAL = 10
PATTR = 8
NPAR = 2048
CAP = 64
ITERS = 4
NX = 512
NY = 64
PARCELS = 1048576
N_AXIAL = 64
N_AZIM = 8
DEVICES = 512


def draw_state(key, part):
    subkeys = jax.random.split(key, 6)
    grid_shape = (NX, NY, CZ)
    axial_pos = lax.broadcasted_iota(jnp.float32, grid_shape, 0) / NX
    growth = 1.0 + 2.0 * axial_pos
    density = jax.random.uniform(subkeys[0], grid_shape, jnp.float32, 0.5, 2.0)
    species = jax.random.uniform(subkeys[3], (NSPEC,) + grid_shape, jnp.float32, 0.0, 1.0)
    cell_x = lax.broadcasted_iota(jnp.float32, grid_shape, 0)
    cell_y = lax.broadcasted_iota(jnp.float32, grid_shape, 1)
    cell_z = lax.broadcasted_iota(jnp.float32, grid_shape, 2)
    wave = 2.0 * math.pi * (cell_x / 10.0 + cell_y / 13.0 + cell_z / 16.0)
    phases = jax.random.uniform(subkeys[5], (3, 1, 1, 1), jnp.float32, 0.0, 2.0 * math.pi)
    box_table = jnp.exp(jax.random.uniform(subkeys[4], (NX // CX, NY // CY), jnp.float32, math.log(0.1), math.log(1.2)))
    rough = jnp.clip(jax.random.normal(subkeys[1], (3,) + grid_shape, jnp.float32), -4.0, 4.0)
    smooth_amp = 2.0
    enthalpy = jnp.clip(jax.random.normal(subkeys[2], grid_shape, jnp.float32), -6.0, 6.0)
    box_scale = jnp.repeat(jnp.repeat(box_table, CX, axis=0), CY, axis=1)[:, :, None]
    smooth = smooth_amp * jnp.sin(wave[None] + phases)
    speeds = rough * growth[None] * box_scale[None] + smooth
    return jnp.concatenate([density[None], speeds, enthalpy[None], species], axis=0)


def draw_parcel_state(key, part):
    subkeys = jax.random.split(key, 3)
    parcel_mass = jnp.exp(jax.random.uniform(subkeys[0], (1, PARCELS), jnp.float32, jnp.log(0.2), jnp.log(2.0)))
    moving = jnp.clip(jax.random.normal(subkeys[1], (4, PARCELS), jnp.float32), -6.0, 6.0)
    offsets = jax.random.uniform(subkeys[2], (3, PARCELS), jnp.float32, 0.0, 1.0)
    return jnp.concatenate([parcel_mass, moving, offsets], axis=0)


def live_slots(key):
    axial_of = jnp.arange(DEVICES) // N_AZIM
    drawn = jax.random.randint(key, (DEVICES,), NPAR // 8, NPAR // 2 + 1)
    return jnp.where(axial_of == 0, NPAR, drawn).astype(jnp.int32)


def draw_live_count(key, part):
    return live_slots(jax.random.fold_in(key, 11))


def draw_parcel_dest(key, part):
    live_now = live_slots(jax.random.fold_in(key, 11))
    subkeys = jax.random.split(jax.random.fold_in(key, 12), 3)
    counts = jax.random.randint(subkeys[0], (DEVICES, 4), CAP // 4, CAP + 1)
    fullest = jax.random.randint(subkeys[1], (DEVICES,), 0, 4)
    counts = jnp.where(jnp.arange(4)[None, :] == fullest[:, None], CAP, counts)
    bounds = jnp.cumsum(counts, axis=1)
    scores = jax.random.randint(subkeys[2], (DEVICES, NPAR), 0, 1048576)
    scores = jnp.where(jnp.arange(NPAR)[None, :] < live_now[:, None], scores, scores + 2097152)
    order = jnp.argsort(scores, axis=1, stable=True)
    ranks = jnp.argsort(order, axis=1, stable=True)
    beyond = jnp.sum((ranks[:, :, None] >= bounds[:, None, :3]).astype(jnp.int32), axis=2)
    chosen = jnp.where(ranks < bounds[:, 3:4], 1 + beyond, 0)
    return chosen.reshape(PARCELS).astype(jnp.int32)


def plant(values, stream_key, smallest, largest):
    dims = values.shape
    index_at = [jax.random.randint(jax.random.fold_in(stream_key, axis), (), 0, dims[axis]) for axis in range(len(dims))]
    values = values.at[tuple(index_at)].set(smallest)
    longest = dims.index(max(dims))
    index_at[longest] = (index_at[longest] + 1) % dims[longest]
    return values.at[tuple(index_at)].set(largest)


def setup_inputs(seed: int = 0) -> dict:
    key_list = jax.random.split(jax.random.key(seed), 7)
    return {
        "state": draw_state(jax.random.fold_in(key_list[6], 71), 0),
        "diff_coef": jnp.clip(jnp.exp(jax.random.uniform(key_list[1], (NSCAL,), jnp.float32, math.log(0.1), math.log(1.0))), 0.1, 1.0),
        "parcel_state": draw_parcel_state(jax.random.fold_in(key_list[6], 71), 0),
        "parcel_cell": plant(jax.random.randint(key_list[3], (PARCELS,), 0, CX * CY * CZ), jax.random.fold_in(key_list[3], 1), 0, (CX * CY * CZ) - 1).astype(jnp.int32),
        "parcel_dest": draw_parcel_dest(jax.random.fold_in(key_list[6], 71), 0),
        "live_count": draw_live_count(jax.random.fold_in(key_list[6], 71), 0),
    }


CFL = 0.4
SHIFT_PRESSURE = 0.25
EVAP = 8.0
RELAX = 4.0
DRAG = 6.0
LATENT = 0.5
HEAT_CAP = 0.8


def shifted(padded, rim_width, direction, step_by):
    selector = []
    total_dims = padded.ndim
    for dim_index in range(total_dims):
        extent = padded.shape[dim_index]
        if dim_index == total_dims - 3 + direction:
            selector.append(slice(rim_width + step_by, extent - rim_width + step_by))
        elif dim_index >= total_dims - 3:
            selector.append(slice(rim_width, extent - rim_width))
        else:
            selector.append(slice(None))
    return padded[tuple(selector)]


def pad_grid(values, rim_width, radial_mode):
    lead_dims = [(0, 0)] * (values.ndim - 3)
    padded = jnp.pad(values, lead_dims + [(rim_width, rim_width), (0, 0), (0, 0)])
    padded = jnp.pad(padded, lead_dims + [(0, 0), (rim_width, rim_width), (0, 0)], mode="wrap")
    return jnp.pad(padded, lead_dims + [(0, 0), (0, 0), (rim_width, rim_width)], mode=radial_mode)


def transport(scalar_pad, vel_pad, density_pad, density_rim, diffusion, step_size):
    center = shifted(scalar_pad, 2, 0, 0)
    density = shifted(density_pad, density_rim, 0, 0)
    change = jnp.zeros_like(center)
    for direction in range(3):
        carried = vel_pad[direction] * scalar_pad
        advect = (-shifted(carried, 2, direction, 2) + 8.0 * shifted(carried, 2, direction, 1)
                  - 8.0 * shifted(carried, 2, direction, -1) + shifted(carried, 2, direction, -2)) / 12.0
        upper_flux = 0.5 * diffusion * (density + shifted(density_pad, density_rim, direction, 1)) * (shifted(scalar_pad, 2, direction, 1) - center)
        lower_flux = 0.5 * diffusion * (density + shifted(density_pad, density_rim, direction, -1)) * (center - shifted(scalar_pad, 2, direction, -1))
        change = change - advect + upper_flux - lower_flux
    return center + step_size * change


def evaporate(attrs, gas_values, alive_mask, step_size):
    parcel_mass = attrs[0]
    parcel_temp = attrs[1]
    parcel_vel = attrs[2:5]
    offsets = attrs[5:8]
    gas_heat = gas_values[3]
    gas_fuel = gas_values[4]
    evap_rate = EVAP * jax.nn.softplus(gas_heat - parcel_temp) * (1.0 - gas_fuel)
    new_mass = parcel_mass * jnp.exp(-step_size * evap_rate)
    lost_mass = parcel_mass - new_mass
    new_temp = parcel_temp + step_size * RELAX * (gas_heat - parcel_temp)
    new_vel = parcel_vel + step_size * DRAG * (gas_values[0:3] - parcel_vel)
    new_offsets = offsets + step_size * new_vel
    heat_source = -LATENT * lost_mass - HEAT_CAP * new_mass * (new_temp - parcel_temp)
    new_attrs = jnp.concatenate([new_mass[None], new_temp[None], new_vel, new_offsets], axis=0) * alive_mask[None]
    sources = jnp.stack([heat_source * alive_mask, lost_mass * alive_mask])
    return new_attrs, sources


def operate(values):
    padded = pad_grid(values, 1, "constant")
    beside = shifted(padded, 1, 0, 1) + shifted(padded, 1, 0, -1)
    beside = beside + shifted(padded, 1, 1, 1) + shifted(padded, 1, 1, -1)
    beside = beside + shifted(padded, 1, 2, 1) + shifted(padded, 1, 2, -1)
    return (6.0 + SHIFT_PRESSURE) * values - beside


def reference(state, diff_coef, parcel_state, parcel_cell, parcel_dest, live_count):
    velocity = state[1:4]
    fastest = jnp.max(jnp.abs(velocity))
    step_size = CFL / (fastest + 1e-6)
    padded = pad_grid(state, 2, "edge")
    vel_pad = padded[1:4]
    density_pad = padded[0]

    def one_scalar(pair):
        return transport(pair[0], vel_pad, density_pad, 2, pair[1], step_size)

    transported = lax.map(one_scalar, (padded[4:], diff_coef))

    slot_index = jnp.arange(PARCELS).astype(jnp.int32)
    owner = slot_index // NPAR
    owner_axial = owner // N_AZIM
    owner_azim = owner % N_AZIM
    slot_alive = (slot_index % NPAR) < live_count[owner]
    alive_mask = slot_alive.astype(jnp.float32)
    local_x = parcel_cell // (CY * CZ)
    local_y = (parcel_cell // CZ) % CY
    radial = parcel_cell % CZ
    grid_x = owner_axial * CX + local_x
    grid_y = owner_azim * CY + local_y
    gas_values = state[1:6][:, grid_x, grid_y, radial]
    updated, sources = evaporate(parcel_state, gas_values, alive_mask, step_size)
    flat_cell = ((grid_x * NY + grid_y) * CZ + radial).astype(jnp.int32)
    deposit = jax.ops.segment_sum(sources.T, flat_cell, num_segments=NX * NY * CZ).T.reshape(2, NX, NY, CZ)
    scalars_new = jnp.concatenate([transported[:2] + deposit / state[0][None], transported[2:]], axis=0)

    dest_masks = jnp.stack([((parcel_dest == d + 1) & slot_alive) for d in range(4)], axis=1).astype(jnp.int32)
    ranks = jnp.cumsum(dest_masks.reshape(DEVICES, NPAR, 4), axis=1).reshape(PARCELS, 4) - 1
    rank_of = jnp.sum(dest_masks * ranks, axis=1)
    direction = parcel_dest - 1
    to_axial = owner_axial + jnp.where(direction == 0, -1, jnp.where(direction == 1, 1, 0))
    to_azim = (owner_azim + jnp.where(direction == 2, -1, jnp.where(direction == 3, 1, 0)) + N_AZIM) % N_AZIM
    receiver = to_axial * N_AZIM + to_azim
    moving_ok = (jnp.sum(dest_masks, axis=1) > 0) & (to_axial >= 0) & (to_axial < N_AXIAL)
    target = jnp.where(moving_ok, direction * (DEVICES * CAP) + receiver * CAP + rank_of, 4 * DEVICES * CAP).astype(jnp.int32)
    landed = jax.ops.segment_sum(updated.T, target, num_segments=4 * DEVICES * CAP + 1)[:-1]
    arrived = jnp.transpose(landed.reshape(4, DEVICES * CAP, PATTR), (0, 2, 1))
    kept_parcels = jnp.where((parcel_dest == 0)[None], updated, jnp.float32(0.0))

    divergence = jnp.zeros_like(state[0])
    for direction_dim in range(3):
        divergence = divergence + 0.5 * (shifted(vel_pad[direction_dim], 2, direction_dim, 1) - shifted(vel_pad[direction_dim], 2, direction_dim, -1))
    pressure = jnp.zeros_like(divergence)
    residual = divergence
    search = divergence
    norm_now = jnp.sum(residual * residual)
    for iteration in range(ITERS):
        image = operate(search)
        alpha = norm_now / jnp.sum(search * image)
        pressure = pressure + alpha * search
        residual = residual - alpha * image
        norm_next = jnp.sum(residual * residual)
        search = residual + (norm_next / norm_now) * search
        norm_now = norm_next
    pressure_pad = pad_grid(pressure, 1, "constant")
    velocity_new = jnp.stack([velocity[d] - 0.5 * (shifted(pressure_pad, 1, d, 1) - shifted(pressure_pad, 1, d, -1)) for d in range(3)])
    return scalars_new, velocity_new, kept_parcels, arrived
```

```python
import jax
import jax.numpy as jnp
from jax import lax
from jax.sharding import PartitionSpec as P

CAP = 64
ITERS = 4


CFL = 0.4
SHIFT_PRESSURE = 0.25
EVAP = 8.0
RELAX = 4.0
DRAG = 6.0
LATENT = 0.5
HEAT_CAP = 0.8
HIGHEST = lax.Precision.HIGHEST


def extended(block, sides, width):
    for axis, dim in sides:
        count = lax.axis_size(axis)
        forward = [(i, i + 1) for i in range(count - 1)]
        forward.append((count - 1, 0))
        backward = [(target, source) for source, target in forward]
        low = lax.ppermute(
            lax.slice_in_dim(block, block.shape[dim] - width, None, axis=dim), axis, forward
        )
        high = lax.ppermute(lax.slice_in_dim(block, 0, width, axis=dim), axis, backward)
        block = jnp.concatenate([low, block, high], axis=dim)
    return block


def shifted_2(shard, axis, by):
    length = lax.axis_size(axis)
    pairs = [(i, i + by) for i in range(length) if 0 <= i + by < length]
    return lax.ppermute(shard, axis, pairs)


def shifted_3(shard, axis, by):
    length = lax.axis_size(axis)
    return lax.ppermute(shard, axis, [(i, (i + by) % length) for i in range(length)])


def shifted(padded, rim_width, direction, step_by):
    selector = []
    total_dims = padded.ndim
    for dim_index in range(total_dims):
        extent = padded.shape[dim_index]
        if dim_index == total_dims - 3 + direction:
            selector.append(slice(rim_width + step_by, extent - rim_width + step_by))
        elif dim_index >= total_dims - 3:
            selector.append(slice(rim_width, extent - rim_width))
        else:
            selector.append(slice(None))
    return padded[tuple(selector)]


def clear_ends(padded, rim_width, axial_dim):
    extent = padded.shape[axial_dim]
    at_first = lax.axis_index("axial") == 0
    at_last = lax.axis_index("axial") == lax.axis_size("axial") - 1
    shape_list = [1] * padded.ndim
    shape_list[axial_dim] = extent
    position = lax.broadcasted_iota(jnp.int32, tuple(shape_list), axial_dim)
    dropped = at_first & (position < rim_width) | at_last & (position >= extent - rim_width)
    return jnp.where(dropped, jnp.float32(0.0), padded)


def radial_pad(values, rim_width, radial_mode):
    return jnp.pad(
        values, [(0, 0)] * (values.ndim - 1) + [(rim_width, rim_width)], mode=radial_mode
    )


def transport(scalar_pad, vel_pad, density_pad, density_rim, diffusion, step_size):
    center = shifted(scalar_pad, 2, 0, 0)
    density = shifted(density_pad, density_rim, 0, 0)
    change = jnp.zeros_like(center)
    for direction in range(3):
        carried = vel_pad[direction] * scalar_pad
        advect = (
            -shifted(carried, 2, direction, 2)
            + 8.0 * shifted(carried, 2, direction, 1)
            - 8.0 * shifted(carried, 2, direction, -1)
            + shifted(carried, 2, direction, -2)
        ) / 12.0
        upper_flux = (
            0.5
            * diffusion
            * (density + shifted(density_pad, density_rim, direction, 1))
            * (shifted(scalar_pad, 2, direction, 1) - center)
        )
        lower_flux = (
            0.5
            * diffusion
            * (density + shifted(density_pad, density_rim, direction, -1))
            * (center - shifted(scalar_pad, 2, direction, -1))
        )
        change = change - advect + upper_flux - lower_flux
    return center + step_size * change


def evaporate(attrs, gas_values, alive_mask, step_size):
    parcel_mass = attrs[0]
    parcel_temp = attrs[1]
    parcel_vel = attrs[2:5]
    offsets = attrs[5:8]
    gas_heat = gas_values[3]
    gas_fuel = gas_values[4]
    evap_rate = EVAP * jax.nn.softplus(gas_heat - parcel_temp) * (1.0 - gas_fuel)
    new_mass = parcel_mass * jnp.exp(-step_size * evap_rate)
    lost_mass = parcel_mass - new_mass
    new_temp = parcel_temp + step_size * RELAX * (gas_heat - parcel_temp)
    new_vel = parcel_vel + step_size * DRAG * (gas_values[0:3] - parcel_vel)
    new_offsets = offsets + step_size * new_vel
    heat_source = -LATENT * lost_mass - HEAT_CAP * new_mass * (new_temp - parcel_temp)
    new_attrs = (
        jnp.concatenate([new_mass[None], new_temp[None], new_vel, new_offsets], axis=0)
        * alive_mask[None]
    )
    sources = jnp.stack([heat_source * alive_mask, lost_mass * alive_mask])
    return (new_attrs, sources)


def pressure_pad(values):
    padded = extended(values, (("axial", 0), ("azim", 1)), 1)
    return radial_pad(clear_ends(padded, 1, 0), 1, "constant")


def operate(values):
    padded = pressure_pad(values)
    beside = shifted(padded, 1, 0, 1) + shifted(padded, 1, 0, -1)
    beside = beside + shifted(padded, 1, 1, 1) + shifted(padded, 1, 1, -1)
    beside = beside + shifted(padded, 1, 2, 1) + shifted(padded, 1, 2, -1)
    return (6.0 + SHIFT_PRESSURE) * values - beside


def neighbour_sum(padded):
    beside = shifted(padded, 1, 0, 1) + shifted(padded, 1, 0, -1)
    beside = beside + shifted(padded, 1, 1, 1) + shifted(padded, 1, 1, -1)
    return beside + shifted(padded, 1, 2, 1) + shifted(padded, 1, 2, -1)


def solve_pressure(divergence):
    half_width = 6.0
    basis = [divergence]
    padded_basis = []
    for j in range(ITERS):
        padded = pressure_pad(basis[j])
        padded_basis.append(padded)
        scaled = neighbour_sum(padded) * (-1.0 / half_width)
        if j == 0:
            basis.append(scaled)
        else:
            basis.append(2.0 * scaled - basis[j - 1])
    size = ITERS + 1
    pairs = [(i, j) for i in range(size) for j in range(i, size)]
    local = jnp.stack([jnp.sum(basis[i] * basis[j]) for i, j in pairs])
    total = lax.psum(local, ("axial", "azim"))
    gram = [[None] * size for _ in range(size)]
    for n, (i, j) in enumerate(pairs):
        gram[i][j] = total[n]
        gram[j][i] = total[n]
    shift = 6.0 + SHIFT_PRESSURE

    def apply_a(c):
        out = [shift * c[j] for j in range(size)]
        for j in range(size - 1):
            if j == 0:
                out[1] = out[1] + half_width * c[0]
            else:
                out[j + 1] = out[j + 1] + 0.5 * half_width * c[j]
                out[j - 1] = out[j - 1] + 0.5 * half_width * c[j]
        return out

    def inner(a, b):
        acc = None
        for i in range(size):
            for j in range(size):
                if isinstance(a[i], float) and a[i] == 0.0:
                    continue
                if isinstance(b[j], float) and b[j] == 0.0:
                    continue
                term = a[i] * gram[i][j] * b[j]
                acc = term if acc is None else acc + term
        return acc

    zero = 0.0
    solution_c = [zero] * size
    residual = [1.0] + [zero] * (size - 1)
    search = list(residual)
    norm_now = inner(residual, residual)
    for iteration in range(ITERS):
        image = apply_a(search)
        alpha = norm_now / inner(search, image)
        solution_c = [solution_c[j] + alpha * search[j] for j in range(size)]
        residual = [residual[j] - alpha * image[j] for j in range(size)]
        if iteration == ITERS - 1:
            break
        norm_next = inner(residual, residual)
        search = [residual[j] + norm_next / norm_now * search[j] for j in range(size)]
        norm_now = norm_next
    pressure = solution_c[0] * basis[0]
    padded_pressure = solution_c[0] * padded_basis[0]
    for j in range(1, ITERS):
        pressure = pressure + solution_c[j] * basis[j]
        padded_pressure = padded_pressure + solution_c[j] * padded_basis[j]
    return pressure, padded_pressure


def along_axial(buffer, step_by):
    return shifted_2(buffer, "axial", step_by)


def along_azim(buffer, step_by):
    return shifted_3(buffer, "azim", step_by)


def on_device(state, diff_coef, parcel_state, parcel_cell, parcel_dest, live_count):
    velocity = state[1:4]
    fastest = lax.pmax(jnp.max(jnp.abs(velocity)), ("axial", "azim"))
    step_size = CFL / (fastest + 1e-06)
    whole_pad = extended(state, (("axial", 1), ("azim", 2)), 2)
    whole_pad = radial_pad(clear_ends(whole_pad, 2, 1), 2, "edge")
    moving = whole_pad[1:]
    density_pad = whole_pad[0]
    density_rim = 2
    vel_pad = moving[0:3]
    transported = transport(
        moving[3:], vel_pad, density_pad, density_rim, diff_coef[:, None, None, None], step_size
    )
    npar_local = parcel_cell.shape[0]
    block_rows = 512
    cells_x, cells_y, cells_z = (state.shape[1], state.shape[2], state.shape[3])
    plane_count = cells_x * cells_y
    gas_table = jnp.transpose(state[1:6].reshape(5, plane_count, cells_z), (1, 0, 2)).reshape(
        plane_count, 5 * cells_z
    )
    live_now = live_count[0]

    def one_block(block_index, carried_pair):
        deposit, updated = carried_pair
        first_slot = block_index * block_rows
        cell_ids = lax.dynamic_slice_in_dim(parcel_cell, first_slot, block_rows)
        attrs = lax.dynamic_slice_in_dim(parcel_state, first_slot, block_rows, 1)
        alive_mask = (first_slot + jnp.arange(block_rows) < live_now).astype(jnp.float32)
        plane_ids = cell_ids // cells_z
        radial_ids = cell_ids % cells_z
        plane_hot = (plane_ids[:, None] == jnp.arange(plane_count)[None, :]).astype(jnp.float32)
        radial_hot = (radial_ids[:, None] == jnp.arange(cells_z)[None, :]).astype(jnp.float32)
        gas_rows = jnp.dot(plane_hot, gas_table, precision=HIGHEST).reshape(block_rows, 5, cells_z)
        gas_values = jnp.sum(gas_rows * radial_hot[:, None, :], axis=2).T
        new_attrs, sources = evaporate(attrs, gas_values, alive_mask, step_size)
        spread = (sources.T[:, :, None] * radial_hot[:, None, :]).reshape(block_rows, 2 * cells_z)
        deposit = deposit + lax.dot_general(
            plane_hot, spread, (((0,), (0,)), ((), ())), precision=HIGHEST
        )
        updated = lax.dynamic_update_slice_in_dim(updated, new_attrs, first_slot, 1)
        return (deposit, updated)

    initial = (jnp.zeros((plane_count, 2 * cells_z), jnp.float32), jnp.zeros_like(parcel_state))
    block_count = npar_local // block_rows
    deposit, updated = lax.fori_loop(0, block_count, one_block, initial)
    deposit = jnp.transpose(deposit.reshape(cells_x, cells_y, 2, cells_z), (2, 0, 1, 3))
    scalars_new = jnp.concatenate(
        [transported[:2] + deposit / state[0][None], transported[2:]], axis=0
    )
    slot_alive = jnp.arange(npar_local) < live_now
    stacked = jnp.stack([(parcel_dest == d + 1) & slot_alive for d in range(4)]).astype(jnp.int32)
    ranks = jnp.cumsum(stacked, axis=1) - 1
    mover = jnp.sum(stacked, axis=0) > 0
    target = jnp.where(mover, jnp.sum(stacked * (jnp.arange(4)[:, None] * CAP + ranks), axis=0), -1)
    select = (target[:, None] == jnp.arange(4 * CAP)[None, :]).astype(jnp.float32)
    buffers = jnp.transpose(
        jnp.dot(updated, select, precision=HIGHEST).reshape(updated.shape[0], 4, CAP), (1, 0, 2)
    )
    arrived = jnp.stack(
        [
            along_axial(buffers[0], -1),
            along_axial(buffers[1], 1),
            along_azim(buffers[2], -1),
            along_azim(buffers[3], 1),
        ]
    )
    kept_parcels = jnp.where((parcel_dest == 0)[None], updated, jnp.float32(0.0))
    divergence = jnp.zeros_like(state[0])
    for direction in range(3):
        divergence = divergence + 0.5 * (
            shifted(vel_pad[direction], 2, direction, 1)
            - shifted(vel_pad[direction], 2, direction, -1)
        )
    pressure, padded_pressure = solve_pressure(divergence)
    velocity_new = jnp.stack(
        [
            velocity[d]
            - 0.5 * (shifted(padded_pressure, 1, d, 1) - shifted(padded_pressure, 1, d, -1))
            for d in range(3)
        ]
    )
    return (scalars_new, velocity_new, kept_parcels, arrived)


def solution(mesh):
    in_specs = (
        P(None, "axial", "azim", None),
        P(),
        P(None, ("axial", "azim")),
        P(("axial", "azim")),
        P(("axial", "azim")),
        P(("axial", "azim")),
    )
    out_specs = (
        P(None, "axial", "azim", None),
        P(None, "axial", "azim", None),
        P(None, ("axial", "azim")),
        P(None, None, ("axial", "azim")),
    )
    return jax.shard_map(
        on_device, mesh=mesh, in_specs=in_specs, out_specs=out_specs, check_vma=False
    )
```

```python
import jax
import jax.numpy as jnp
from jax import lax
from jax.sharding import PartitionSpec as P
from jax.experimental import pallas as pl
from jax.experimental.pallas import tpu as pltpu

CAP = 64
ITERS = 4


CFL = 0.4
SHIFT_PRESSURE = 0.25
EVAP = 8.0
RELAX = 4.0
DRAG = 6.0
LATENT = 0.5
HEAT_CAP = 0.8
HIGHEST = lax.Precision.HIGHEST


def extended(block, sides, width):
    for axis, dim in sides:
        count = lax.axis_size(axis)
        forward = [(i, i + 1) for i in range(count - 1)]
        forward.append((count - 1, 0))
        backward = [(target, source) for source, target in forward]
        low = lax.ppermute(
            lax.slice_in_dim(block, block.shape[dim] - width, None, axis=dim), axis, forward
        )
        high = lax.ppermute(lax.slice_in_dim(block, 0, width, axis=dim), axis, backward)
        block = jnp.concatenate([low, block, high], axis=dim)
    return block


def shifted_2(shard, axis, by):
    length = lax.axis_size(axis)
    pairs = [(i, i + by) for i in range(length) if 0 <= i + by < length]
    return lax.ppermute(shard, axis, pairs)


def shifted_3(shard, axis, by):
    length = lax.axis_size(axis)
    return lax.ppermute(shard, axis, [(i, (i + by) % length) for i in range(length)])


def shifted(padded, rim_width, direction, step_by):
    selector = []
    total_dims = padded.ndim
    for dim_index in range(total_dims):
        extent = padded.shape[dim_index]
        if dim_index == total_dims - 3 + direction:
            selector.append(slice(rim_width + step_by, extent - rim_width + step_by))
        elif dim_index >= total_dims - 3:
            selector.append(slice(rim_width, extent - rim_width))
        else:
            selector.append(slice(None))
    return padded[tuple(selector)]


def clear_ends(padded, rim_width, axial_dim):
    extent = padded.shape[axial_dim]
    at_first = lax.axis_index("axial") == 0
    at_last = lax.axis_index("axial") == lax.axis_size("axial") - 1
    shape_list = [1] * padded.ndim
    shape_list[axial_dim] = extent
    position = lax.broadcasted_iota(jnp.int32, tuple(shape_list), axial_dim)
    dropped = at_first & (position < rim_width) | at_last & (position >= extent - rim_width)
    return jnp.where(dropped, jnp.float32(0.0), padded)


def radial_pad(values, rim_width, radial_mode):
    return jnp.pad(
        values, [(0, 0)] * (values.ndim - 1) + [(rim_width, rim_width)], mode=radial_mode
    )


def transport(scalar_pad, vel_pad, density_pad, density_rim, diffusion, step_size):
    center = shifted(scalar_pad, 2, 0, 0)
    density = shifted(density_pad, density_rim, 0, 0)
    change = jnp.zeros_like(center)
    for direction in range(3):
        carried = vel_pad[direction] * scalar_pad
        advect = (
            -shifted(carried, 2, direction, 2)
            + 8.0 * shifted(carried, 2, direction, 1)
            - 8.0 * shifted(carried, 2, direction, -1)
            + shifted(carried, 2, direction, -2)
        ) / 12.0
        upper_flux = (
            0.5
            * diffusion
            * (density + shifted(density_pad, density_rim, direction, 1))
            * (shifted(scalar_pad, 2, direction, 1) - center)
        )
        lower_flux = (
            0.5
            * diffusion
            * (density + shifted(density_pad, density_rim, direction, -1))
            * (center - shifted(scalar_pad, 2, direction, -1))
        )
        change = change - advect + upper_flux - lower_flux
    return center + step_size * change


def evaporate(attrs, gas_values, alive_mask, step_size):
    parcel_mass = attrs[0]
    parcel_temp = attrs[1]
    parcel_vel = attrs[2:5]
    offsets = attrs[5:8]
    gas_heat = gas_values[3]
    gas_fuel = gas_values[4]
    evap_rate = EVAP * jax.nn.softplus(gas_heat - parcel_temp) * (1.0 - gas_fuel)
    new_mass = parcel_mass * jnp.exp(-step_size * evap_rate)
    lost_mass = parcel_mass - new_mass
    new_temp = parcel_temp + step_size * RELAX * (gas_heat - parcel_temp)
    new_vel = parcel_vel + step_size * DRAG * (gas_values[0:3] - parcel_vel)
    new_offsets = offsets + step_size * new_vel
    heat_source = -LATENT * lost_mass - HEAT_CAP * new_mass * (new_temp - parcel_temp)
    new_attrs = (
        jnp.concatenate([new_mass[None], new_temp[None], new_vel, new_offsets], axis=0)
        * alive_mask[None]
    )
    sources = jnp.stack([heat_source * alive_mask, lost_mass * alive_mask])
    return (new_attrs, sources)


def pressure_pad(values):
    padded = extended(values, (("axial", 0), ("azim", 1)), 1)
    return radial_pad(clear_ends(padded, 1, 0), 1, "constant")


def operate(values):
    padded = pressure_pad(values)
    beside = shifted(padded, 1, 0, 1) + shifted(padded, 1, 0, -1)
    beside = beside + shifted(padded, 1, 1, 1) + shifted(padded, 1, 1, -1)
    beside = beside + shifted(padded, 1, 2, 1) + shifted(padded, 1, 2, -1)
    return (6.0 + SHIFT_PRESSURE) * values - beside


def butterfly_partners():
    rounds = []
    for axis in ("azim", "axial"):
        step = 1
        while step < lax.axis_size(axis):
            rounds.append((axis, step))
            step *= 2
    return rounds


def reduce_kernel(rounds, x_ref, o_ref, send_buf, recv_buf, send_sems, recv_sems):
    here = {"axial": lax.axis_index("axial"), "azim": lax.axis_index("azim")}

    def partner(axis, step):
        index = here[axis]
        other = index + step - 2 * step * ((index // step) % 2)
        coords = dict(here)
        coords[axis] = other
        return (coords["axial"], coords["azim"])

    barrier = pltpu.get_barrier_semaphore()
    for axis, step in rounds:
        pl.semaphore_signal(
            barrier, inc=1, device_id=partner(axis, step), device_id_type=pl.DeviceIdType.MESH
        )
    pl.semaphore_wait(barrier, len(rounds))
    row = lax.broadcasted_iota(jnp.int32, x_ref.shape, 0)
    lane = lax.broadcasted_iota(jnp.int32, x_ref.shape, 1)
    is_max = (row == 0) & (lane == 0)
    acc = x_ref[...]
    for r, (axis, step) in enumerate(rounds):
        send_buf[r] = acc
        copy = pltpu.make_async_remote_copy(
            src_ref=send_buf.at[r],
            dst_ref=recv_buf.at[r],
            send_sem=send_sems.at[r],
            recv_sem=recv_sems.at[r],
            device_id=partner(axis, step),
            device_id_type=pl.DeviceIdType.MESH,
        )
        copy.start()
        copy.wait()
        other = recv_buf[r]
        acc = jnp.where(is_max, jnp.maximum(acc, other), acc + other)
    o_ref[...] = acc


def global_reduce(values):
    rounds = butterfly_partners()
    tile = jnp.zeros((8, 128), jnp.float32).at[0, : values.shape[0]].set(values)
    out = pl.pallas_call(
        lambda *refs: reduce_kernel(rounds, *refs),
        out_shape=jax.ShapeDtypeStruct((8, 128), jnp.float32),
        in_specs=[pl.BlockSpec(memory_space=pltpu.VMEM)],
        out_specs=pl.BlockSpec(memory_space=pltpu.VMEM),
        scratch_shapes=[
            pltpu.VMEM((len(rounds), 8, 128), jnp.float32),
            pltpu.VMEM((len(rounds), 8, 128), jnp.float32),
            pltpu.SemaphoreType.DMA((len(rounds),)),
            pltpu.SemaphoreType.DMA((len(rounds),)),
        ],
        compiler_params=pltpu.CompilerParams(collective_id=0, has_side_effects=True),
    )(tile)
    return out[0, : values.shape[0]]


def neighbour_sum(padded):
    beside = shifted(padded, 1, 0, 1) + shifted(padded, 1, 0, -1)
    beside = beside + shifted(padded, 1, 1, 1) + shifted(padded, 1, 1, -1)
    return beside + shifted(padded, 1, 2, 1) + shifted(padded, 1, 2, -1)


def solve_pressure(divergence, local_fastest):
    half_width = 6.0
    basis = [divergence]
    padded_basis = []
    for j in range(ITERS):
        padded = pressure_pad(basis[j])
        padded_basis.append(padded)
        scaled = neighbour_sum(padded) * (-1.0 / half_width)
        if j == 0:
            basis.append(scaled)
        else:
            basis.append(2.0 * scaled - basis[j - 1])
    size = ITERS + 1
    pairs = [(i, j) for i in range(size) for j in range(i, size)]
    local = jnp.stack([local_fastest] + [jnp.sum(basis[i] * basis[j]) for i, j in pairs])
    reduced = global_reduce(local)
    fastest = reduced[0]
    total = reduced[1:]
    gram = [[None] * size for _ in range(size)]
    for n, (i, j) in enumerate(pairs):
        gram[i][j] = total[n]
        gram[j][i] = total[n]
    shift = 6.0 + SHIFT_PRESSURE

    def apply_a(c):
        out = [shift * c[j] for j in range(size)]
        for j in range(size - 1):
            if j == 0:
                out[1] = out[1] + half_width * c[0]
            else:
                out[j + 1] = out[j + 1] + 0.5 * half_width * c[j]
                out[j - 1] = out[j - 1] + 0.5 * half_width * c[j]
        return out

    def inner(a, b):
        acc = None
        for i in range(size):
            for j in range(size):
                if isinstance(a[i], float) and a[i] == 0.0:
                    continue
                if isinstance(b[j], float) and b[j] == 0.0:
                    continue
                term = a[i] * gram[i][j] * b[j]
                acc = term if acc is None else acc + term
        return acc

    zero = 0.0
    solution_c = [zero] * size
    residual = [1.0] + [zero] * (size - 1)
    search = list(residual)
    norm_now = inner(residual, residual)
    for iteration in range(ITERS):
        image = apply_a(search)
        alpha = norm_now / inner(search, image)
        solution_c = [solution_c[j] + alpha * search[j] for j in range(size)]
        residual = [residual[j] - alpha * image[j] for j in range(size)]
        if iteration == ITERS - 1:
            break
        norm_next = inner(residual, residual)
        search = [residual[j] + norm_next / norm_now * search[j] for j in range(size)]
        norm_now = norm_next
    padded_pressure = solution_c[0] * padded_basis[0]
    for j in range(1, ITERS):
        padded_pressure = padded_pressure + solution_c[j] * padded_basis[j]
    return padded_pressure, fastest


def along_axial(buffer, step_by):
    return shifted_2(buffer, "axial", step_by)


def along_azim(buffer, step_by):
    return shifted_3(buffer, "azim", step_by)


def on_device(state, diff_coef, parcel_state, parcel_cell, parcel_dest, live_count):
    velocity = state[1:4]
    local_fastest = jnp.max(jnp.abs(velocity))
    whole_pad = extended(state, (("axial", 1), ("azim", 2)), 2)
    whole_pad = radial_pad(clear_ends(whole_pad, 2, 1), 2, "edge")
    moving = whole_pad[1:]
    density_pad = whole_pad[0]
    density_rim = 2
    vel_pad = moving[0:3]
    divergence = jnp.zeros_like(state[0])
    for direction in range(3):
        divergence = divergence + 0.5 * (
            shifted(vel_pad[direction], 2, direction, 1)
            - shifted(vel_pad[direction], 2, direction, -1)
        )
    padded_pressure, fastest = solve_pressure(divergence, local_fastest)
    step_size = CFL / (fastest + 1e-06)
    transported = transport(
        moving[3:], vel_pad, density_pad, density_rim, diff_coef[:, None, None, None], step_size
    )
    npar_local = parcel_cell.shape[0]
    block_rows = 512
    cells_x, cells_y, cells_z = (state.shape[1], state.shape[2], state.shape[3])
    plane_count = cells_x * cells_y
    gas_table = jnp.transpose(state[1:6].reshape(5, plane_count, cells_z), (1, 0, 2)).reshape(
        plane_count, 5 * cells_z
    )
    live_now = live_count[0]

    def one_block(block_index, carried_pair):
        deposit, updated = carried_pair
        first_slot = block_index * block_rows
        cell_ids = lax.dynamic_slice_in_dim(parcel_cell, first_slot, block_rows)
        attrs = lax.dynamic_slice_in_dim(parcel_state, first_slot, block_rows, 1)
        alive_mask = (first_slot + jnp.arange(block_rows) < live_now).astype(jnp.float32)
        plane_ids = cell_ids // cells_z
        radial_ids = cell_ids % cells_z
        plane_hot = (plane_ids[:, None] == jnp.arange(plane_count)[None, :]).astype(jnp.float32)
        radial_hot = (radial_ids[:, None] == jnp.arange(cells_z)[None, :]).astype(jnp.float32)
        gas_rows = jnp.dot(plane_hot, gas_table, precision=HIGHEST).reshape(block_rows, 5, cells_z)
        gas_values = jnp.sum(gas_rows * radial_hot[:, None, :], axis=2).T
        new_attrs, sources = evaporate(attrs, gas_values, alive_mask, step_size)
        spread = (sources.T[:, :, None] * radial_hot[:, None, :]).reshape(block_rows, 2 * cells_z)
        deposit = deposit + lax.dot_general(
            plane_hot, spread, (((0,), (0,)), ((), ())), precision=HIGHEST
        )
        updated = lax.dynamic_update_slice_in_dim(updated, new_attrs, first_slot, 1)
        return (deposit, updated)

    initial = (jnp.zeros((plane_count, 2 * cells_z), jnp.float32), jnp.zeros_like(parcel_state))
    block_count = npar_local // block_rows
    deposit, updated = lax.fori_loop(0, block_count, one_block, initial)
    deposit = jnp.transpose(deposit.reshape(cells_x, cells_y, 2, cells_z), (2, 0, 1, 3))
    scalars_new = jnp.concatenate(
        [transported[:2] + deposit / state[0][None], transported[2:]], axis=0
    )
    slot_alive = jnp.arange(npar_local) < live_now
    stacked = jnp.stack([(parcel_dest == d + 1) & slot_alive for d in range(4)]).astype(jnp.int32)
    ranks = jnp.cumsum(stacked, axis=1) - 1
    mover = jnp.sum(stacked, axis=0) > 0
    target = jnp.where(mover, jnp.sum(stacked * (jnp.arange(4)[:, None] * CAP + ranks), axis=0), -1)
    select = (target[:, None] == jnp.arange(4 * CAP)[None, :]).astype(jnp.float32)
    buffers = jnp.transpose(
        jnp.dot(updated, select, precision=HIGHEST).reshape(updated.shape[0], 4, CAP), (1, 0, 2)
    )
    arrived = jnp.stack(
        [
            along_axial(buffers[0], -1),
            along_axial(buffers[1], 1),
            along_azim(buffers[2], -1),
            along_azim(buffers[3], 1),
        ]
    )
    kept_parcels = jnp.where((parcel_dest == 0)[None], updated, jnp.float32(0.0))
    velocity_new = jnp.stack(
        [
            velocity[d]
            - 0.5 * (shifted(padded_pressure, 1, d, 1) - shifted(padded_pressure, 1, d, -1))
            for d in range(3)
        ]
    )
    return (scalars_new, velocity_new, kept_parcels, arrived)


def solution(mesh):
    in_specs = (
        P(None, "axial", "azim", None),
        P(),
        P(None, ("axial", "azim")),
        P(("axial", "azim")),
        P(("axial", "azim")),
        P(("axial", "azim")),
    )
    out_specs = (
        P(None, "axial", "azim", None),
        P(None, "axial", "azim", None),
        P(None, ("axial", "azim")),
        P(None, None, ("axial", "azim")),
    )
    return jax.shard_map(
        on_device, mesh=mesh, in_specs=in_specs, out_specs=out_specs, check_vma=False
    )
```

```python
import jax
import jax.numpy as jnp
from jax import lax
from jax.sharding import PartitionSpec as P
from jax.experimental import pallas as pl
from jax.experimental.pallas import tpu as pltpu

CAP = 64
ITERS = 4


CFL = 0.4
SHIFT_PRESSURE = 0.25
EVAP = 8.0
RELAX = 4.0
DRAG = 6.0
LATENT = 0.5
HEAT_CAP = 0.8
HIGHEST = lax.Precision.HIGHEST


def extended(block, sides, width):
    for axis, dim in sides:
        count = lax.axis_size(axis)
        forward = [(i, i + 1) for i in range(count - 1)]
        forward.append((count - 1, 0))
        backward = [(target, source) for source, target in forward]
        low = lax.ppermute(
            lax.slice_in_dim(block, block.shape[dim] - width, None, axis=dim), axis, forward
        )
        high = lax.ppermute(lax.slice_in_dim(block, 0, width, axis=dim), axis, backward)
        block = jnp.concatenate([low, block, high], axis=dim)
    return block


def shifted_2(shard, axis, by):
    length = lax.axis_size(axis)
    pairs = [(i, i + by) for i in range(length) if 0 <= i + by < length]
    return lax.ppermute(shard, axis, pairs)


def shifted_3(shard, axis, by):
    length = lax.axis_size(axis)
    return lax.ppermute(shard, axis, [(i, (i + by) % length) for i in range(length)])


def shifted(padded, rim_width, direction, step_by):
    selector = []
    total_dims = padded.ndim
    for dim_index in range(total_dims):
        extent = padded.shape[dim_index]
        if dim_index == total_dims - 3 + direction:
            selector.append(slice(rim_width + step_by, extent - rim_width + step_by))
        elif dim_index >= total_dims - 3:
            selector.append(slice(rim_width, extent - rim_width))
        else:
            selector.append(slice(None))
    return padded[tuple(selector)]


def clear_ends(padded, rim_width, axial_dim):
    extent = padded.shape[axial_dim]
    at_first = lax.axis_index("axial") == 0
    at_last = lax.axis_index("axial") == lax.axis_size("axial") - 1
    shape_list = [1] * padded.ndim
    shape_list[axial_dim] = extent
    position = lax.broadcasted_iota(jnp.int32, tuple(shape_list), axial_dim)
    dropped = at_first & (position < rim_width) | at_last & (position >= extent - rim_width)
    return jnp.where(dropped, jnp.float32(0.0), padded)


def radial_pad(values, rim_width, radial_mode):
    return jnp.pad(
        values, [(0, 0)] * (values.ndim - 1) + [(rim_width, rim_width)], mode=radial_mode
    )


def transport(scalar_pad, vel_pad, density_pad, density_rim, diffusion, step_size):
    center = shifted(scalar_pad, 2, 0, 0)
    density = shifted(density_pad, density_rim, 0, 0)
    change = jnp.zeros_like(center)
    for direction in range(3):
        carried = vel_pad[direction] * scalar_pad
        advect = (
            -shifted(carried, 2, direction, 2)
            + 8.0 * shifted(carried, 2, direction, 1)
            - 8.0 * shifted(carried, 2, direction, -1)
            + shifted(carried, 2, direction, -2)
        ) / 12.0
        upper_flux = (
            0.5
            * diffusion
            * (density + shifted(density_pad, density_rim, direction, 1))
            * (shifted(scalar_pad, 2, direction, 1) - center)
        )
        lower_flux = (
            0.5
            * diffusion
            * (density + shifted(density_pad, density_rim, direction, -1))
            * (center - shifted(scalar_pad, 2, direction, -1))
        )
        change = change - advect + upper_flux - lower_flux
    return center + step_size * change


def evaporate(attrs, gas_values, alive_mask, step_size):
    parcel_mass = attrs[0]
    parcel_temp = attrs[1]
    parcel_vel = attrs[2:5]
    offsets = attrs[5:8]
    gas_heat = gas_values[3]
    gas_fuel = gas_values[4]
    evap_rate = EVAP * jax.nn.softplus(gas_heat - parcel_temp) * (1.0 - gas_fuel)
    new_mass = parcel_mass * jnp.exp(-step_size * evap_rate)
    lost_mass = parcel_mass - new_mass
    new_temp = parcel_temp + step_size * RELAX * (gas_heat - parcel_temp)
    new_vel = parcel_vel + step_size * DRAG * (gas_values[0:3] - parcel_vel)
    new_offsets = offsets + step_size * new_vel
    heat_source = -LATENT * lost_mass - HEAT_CAP * new_mass * (new_temp - parcel_temp)
    new_attrs = (
        jnp.concatenate([new_mass[None], new_temp[None], new_vel, new_offsets], axis=0)
        * alive_mask[None]
    )
    sources = jnp.stack([heat_source * alive_mask, lost_mass * alive_mask])
    return (new_attrs, sources)


def pressure_pad(values):
    padded = extended(values, (("axial", 0), ("azim", 1)), 1)
    return radial_pad(clear_ends(padded, 1, 0), 1, "constant")


def operate(values):
    padded = pressure_pad(values)
    beside = shifted(padded, 1, 0, 1) + shifted(padded, 1, 0, -1)
    beside = beside + shifted(padded, 1, 1, 1) + shifted(padded, 1, 1, -1)
    beside = beside + shifted(padded, 1, 2, 1) + shifted(padded, 1, 2, -1)
    return (6.0 + SHIFT_PRESSURE) * values - beside


def butterfly_partners():
    rounds = []
    for axis in ("azim", "axial"):
        step = 1
        while step < lax.axis_size(axis):
            rounds.append((axis, step))
            step *= 2
    return rounds


def coefficient_cg(gram, size, shift, half_width):
    def apply_a(c):
        out = [shift * c[j] for j in range(size)]
        for j in range(size - 1):
            if j == 0:
                out[1] = out[1] + half_width * c[0]
            else:
                out[j + 1] = out[j + 1] + 0.5 * half_width * c[j]
                out[j - 1] = out[j - 1] + 0.5 * half_width * c[j]
        return out

    def inner(a, b):
        acc = None
        for i in range(size):
            for j in range(size):
                if isinstance(a[i], float) and a[i] == 0.0:
                    continue
                if isinstance(b[j], float) and b[j] == 0.0:
                    continue
                term = a[i] * gram[i][j] * b[j]
                acc = term if acc is None else acc + term
        return acc

    solution_c = [0.0] * size
    residual = [1.0] + [0.0] * (size - 1)
    search = list(residual)
    norm_now = inner(residual, residual)
    for iteration in range(ITERS):
        image = apply_a(search)
        alpha = norm_now / inner(search, image)
        solution_c = [solution_c[j] + alpha * search[j] for j in range(size)]
        residual = [residual[j] - alpha * image[j] for j in range(size)]
        if iteration == ITERS - 1:
            break
        norm_next = inner(residual, residual)
        search = [residual[j] + norm_next / norm_now * search[j] for j in range(size)]
        norm_now = norm_next
    return solution_c


def reduce_kernel(rounds, shift, half_width, vel_ref, *refs):
    size = ITERS + 1
    basis_refs = refs[:size]
    o_ref, send_buf, recv_buf, send_sems, recv_sems = refs[size:]
    here = {"axial": lax.axis_index("axial"), "azim": lax.axis_index("azim")}

    def partner(axis, step):
        index = here[axis]
        other = index + step - 2 * step * ((index // step) % 2)
        coords = dict(here)
        coords[axis] = other
        return (coords["axial"], coords["azim"])

    barrier = pltpu.get_barrier_semaphore()
    for axis, step in rounds:
        pl.semaphore_signal(
            barrier, inc=1, device_id=partner(axis, step), device_id_type=pl.DeviceIdType.MESH
        )
    pl.semaphore_wait(barrier, len(rounds))
    row = lax.broadcasted_iota(jnp.int32, o_ref.shape, 0)
    lane = lax.broadcasted_iota(jnp.int32, o_ref.shape, 1)
    is_max = (row == 0) & (lane == 0)

    def total(x):
        return jnp.sum(jnp.sum(x, axis=0, keepdims=True), axis=1, keepdims=True)

    basis = [ref[...] for ref in basis_refs]
    pairs = [(i, j) for i in range(size) for j in range(i, size)]
    entries = [jnp.max(jnp.max(jnp.abs(vel_ref[...]), axis=0, keepdims=True), axis=1, keepdims=True)]
    entries += [total(basis[i] * basis[j]) for i, j in pairs]
    acc = jnp.zeros(o_ref.shape, jnp.float32)
    for n, entry in enumerate(entries):
        acc = jnp.where((row == 0) & (lane == n), entry, acc)
    for r, (axis, step) in enumerate(rounds):
        send_buf[r] = acc
        copy = pltpu.make_async_remote_copy(
            src_ref=send_buf.at[r],
            dst_ref=recv_buf.at[r],
            send_sem=send_sems.at[r],
            recv_sem=recv_sems.at[r],
            device_id=partner(axis, step),
            device_id_type=pl.DeviceIdType.MESH,
        )
        copy.start()
        copy.wait()
        other = recv_buf[r]
        acc = jnp.where(is_max, jnp.maximum(acc, other), acc + other)
    first = acc[0:1, :]
    first_lane = lax.broadcasted_iota(jnp.int32, first.shape, 1)

    def entry_at(n):
        return jnp.sum(jnp.where(first_lane == n, first, 0.0), axis=1, keepdims=True)

    gram = [[None] * size for _ in range(size)]
    for n, (i, j) in enumerate(pairs):
        gram[i][j] = entry_at(n + 1)
        gram[j][i] = gram[i][j]
    coefficients = coefficient_cg(gram, size, shift, half_width)
    out = jnp.where(lane == ITERS, entry_at(0), 0.0)
    for j in range(ITERS):
        out = jnp.where((lane == j), coefficients[j], out)
    o_ref[...] = out


def pressure_coefficients(velocity, basis, shift, half_width):
    rounds = butterfly_partners()
    flat = [v.reshape(-1, v.shape[-1]) for v in basis]
    out = pl.pallas_call(
        lambda *refs: reduce_kernel(rounds, shift, half_width, *refs),
        out_shape=jax.ShapeDtypeStruct((8, 128), jnp.float32),
        in_specs=[pl.BlockSpec(memory_space=pltpu.VMEM)] * (1 + len(flat)),
        out_specs=pl.BlockSpec(memory_space=pltpu.VMEM),
        scratch_shapes=[
            pltpu.VMEM((len(rounds), 8, 128), jnp.float32),
            pltpu.VMEM((len(rounds), 8, 128), jnp.float32),
            pltpu.SemaphoreType.DMA((len(rounds),)),
            pltpu.SemaphoreType.DMA((len(rounds),)),
        ],
        compiler_params=pltpu.CompilerParams(collective_id=0, has_side_effects=True),
    )(velocity.reshape(-1, velocity.shape[-1]), *flat)
    return [out[0, j] for j in range(ITERS)], out[0, ITERS]


def neighbour_sum(padded):
    beside = shifted(padded, 1, 0, 1) + shifted(padded, 1, 0, -1)
    beside = beside + shifted(padded, 1, 1, 1) + shifted(padded, 1, 1, -1)
    return beside + shifted(padded, 1, 2, 1) + shifted(padded, 1, 2, -1)


def solve_pressure(divergence, velocity):
    half_width = 6.0
    basis = [divergence]
    padded_basis = []
    for j in range(ITERS):
        padded = pressure_pad(basis[j])
        padded_basis.append(padded)
        scaled = neighbour_sum(padded) * (-1.0 / half_width)
        if j == 0:
            basis.append(scaled)
        else:
            basis.append(2.0 * scaled - basis[j - 1])
    coefficients, fastest = pressure_coefficients(
        velocity, basis, 6.0 + SHIFT_PRESSURE, half_width
    )
    padded_pressure = coefficients[0] * padded_basis[0]
    for j in range(1, ITERS):
        padded_pressure = padded_pressure + coefficients[j] * padded_basis[j]
    return padded_pressure, fastest


def along_axial(buffer, step_by):
    return shifted_2(buffer, "axial", step_by)


def along_azim(buffer, step_by):
    return shifted_3(buffer, "azim", step_by)


def on_device(state, diff_coef, parcel_state, parcel_cell, parcel_dest, live_count):
    velocity = state[1:4]
    whole_pad = extended(state, (("axial", 1), ("azim", 2)), 2)
    whole_pad = radial_pad(clear_ends(whole_pad, 2, 1), 2, "edge")
    moving = whole_pad[1:]
    density_pad = whole_pad[0]
    density_rim = 2
    vel_pad = moving[0:3]
    divergence = jnp.zeros_like(state[0])
    for direction in range(3):
        divergence = divergence + 0.5 * (
            shifted(vel_pad[direction], 2, direction, 1)
            - shifted(vel_pad[direction], 2, direction, -1)
        )
    padded_pressure, fastest = solve_pressure(divergence, velocity)
    step_size = CFL / (fastest + 1e-06)
    transported = transport(
        moving[3:], vel_pad, density_pad, density_rim, diff_coef[:, None, None, None], step_size
    )
    npar_local = parcel_cell.shape[0]
    block_rows = 512
    cells_x, cells_y, cells_z = (state.shape[1], state.shape[2], state.shape[3])
    plane_count = cells_x * cells_y
    gas_table = jnp.transpose(state[1:6].reshape(5, plane_count, cells_z), (1, 0, 2)).reshape(
        plane_count, 5 * cells_z
    )
    live_now = live_count[0]

    def one_block(block_index, carried_pair):
        deposit, updated = carried_pair
        first_slot = block_index * block_rows
        cell_ids = lax.dynamic_slice_in_dim(parcel_cell, first_slot, block_rows)
        attrs = lax.dynamic_slice_in_dim(parcel_state, first_slot, block_rows, 1)
        alive_mask = (first_slot + jnp.arange(block_rows) < live_now).astype(jnp.float32)
        plane_ids = cell_ids // cells_z
        radial_ids = cell_ids % cells_z
        plane_hot = (plane_ids[:, None] == jnp.arange(plane_count)[None, :]).astype(jnp.float32)
        radial_hot = (radial_ids[:, None] == jnp.arange(cells_z)[None, :]).astype(jnp.float32)
        gas_rows = jnp.dot(plane_hot, gas_table, precision=HIGHEST).reshape(block_rows, 5, cells_z)
        gas_values = jnp.sum(gas_rows * radial_hot[:, None, :], axis=2).T
        new_attrs, sources = evaporate(attrs, gas_values, alive_mask, step_size)
        spread = (sources.T[:, :, None] * radial_hot[:, None, :]).reshape(block_rows, 2 * cells_z)
        deposit = deposit + lax.dot_general(
            plane_hot, spread, (((0,), (0,)), ((), ())), precision=HIGHEST
        )
        updated = lax.dynamic_update_slice_in_dim(updated, new_attrs, first_slot, 1)
        return (deposit, updated)

    initial = (jnp.zeros((plane_count, 2 * cells_z), jnp.float32), jnp.zeros_like(parcel_state))
    block_count = npar_local // block_rows
    deposit, updated = lax.fori_loop(0, block_count, one_block, initial)
    deposit = jnp.transpose(deposit.reshape(cells_x, cells_y, 2, cells_z), (2, 0, 1, 3))
    scalars_new = jnp.concatenate(
        [transported[:2] + deposit / state[0][None], transported[2:]], axis=0
    )
    slot_alive = jnp.arange(npar_local) < live_now
    stacked = jnp.stack([(parcel_dest == d + 1) & slot_alive for d in range(4)]).astype(jnp.int32)
    ranks = jnp.cumsum(stacked, axis=1) - 1
    mover = jnp.sum(stacked, axis=0) > 0
    target = jnp.where(mover, jnp.sum(stacked * (jnp.arange(4)[:, None] * CAP + ranks), axis=0), -1)
    select = (target[:, None] == jnp.arange(4 * CAP)[None, :]).astype(jnp.float32)
    buffers = jnp.transpose(
        jnp.dot(updated, select, precision=HIGHEST).reshape(updated.shape[0], 4, CAP), (1, 0, 2)
    )
    arrived = jnp.stack(
        [
            along_axial(buffers[0], -1),
            along_axial(buffers[1], 1),
            along_azim(buffers[2], -1),
            along_azim(buffers[3], 1),
        ]
    )
    kept_parcels = jnp.where((parcel_dest == 0)[None], updated, jnp.float32(0.0))
    velocity_new = jnp.stack(
        [
            velocity[d]
            - 0.5 * (shifted(padded_pressure, 1, d, 1) - shifted(padded_pressure, 1, d, -1))
            for d in range(3)
        ]
    )
    return (scalars_new, velocity_new, kept_parcels, arrived)


def solution(mesh):
    in_specs = (
        P(None, "axial", "azim", None),
        P(),
        P(None, ("axial", "azim")),
        P(("axial", "azim")),
        P(("axial", "azim")),
        P(("axial", "azim")),
    )
    out_specs = (
        P(None, "axial", "azim", None),
        P(None, "axial", "azim", None),
        P(None, ("axial", "azim")),
        P(None, None, ("axial", "azim")),
    )
    return jax.shard_map(
        on_device, mesh=mesh, in_specs=in_specs, out_specs=out_specs, check_vma=False
    )
```

```python
import jax
import jax.numpy as jnp
from jax import lax
from jax.sharding import PartitionSpec as P
from jax.experimental import pallas as pl
from jax.experimental.pallas import tpu as pltpu

CAP = 64
ITERS = 4


CFL = 0.4
SHIFT_PRESSURE = 0.25
EVAP = 8.0
RELAX = 4.0
DRAG = 6.0
LATENT = 0.5
HEAT_CAP = 0.8
HIGHEST = lax.Precision.HIGHEST


def extended(block, sides, width):
    for axis, dim in sides:
        count = lax.axis_size(axis)
        forward = [(i, i + 1) for i in range(count - 1)]
        forward.append((count - 1, 0))
        backward = [(target, source) for source, target in forward]
        low = lax.ppermute(
            lax.slice_in_dim(block, block.shape[dim] - width, None, axis=dim), axis, forward
        )
        high = lax.ppermute(lax.slice_in_dim(block, 0, width, axis=dim), axis, backward)
        block = jnp.concatenate([low, block, high], axis=dim)
    return block


def shifted_2(shard, axis, by):
    length = lax.axis_size(axis)
    pairs = [(i, i + by) for i in range(length) if 0 <= i + by < length]
    return lax.ppermute(shard, axis, pairs)


def shifted_3(shard, axis, by):
    length = lax.axis_size(axis)
    return lax.ppermute(shard, axis, [(i, (i + by) % length) for i in range(length)])


def shifted(padded, rim_width, direction, step_by):
    selector = []
    total_dims = padded.ndim
    for dim_index in range(total_dims):
        extent = padded.shape[dim_index]
        if dim_index == total_dims - 3 + direction:
            selector.append(slice(rim_width + step_by, extent - rim_width + step_by))
        elif dim_index >= total_dims - 3:
            selector.append(slice(rim_width, extent - rim_width))
        else:
            selector.append(slice(None))
    return padded[tuple(selector)]


def clear_ends(padded, rim_width, axial_dim):
    extent = padded.shape[axial_dim]
    at_first = lax.axis_index("axial") == 0
    at_last = lax.axis_index("axial") == lax.axis_size("axial") - 1
    shape_list = [1] * padded.ndim
    shape_list[axial_dim] = extent
    position = lax.broadcasted_iota(jnp.int32, tuple(shape_list), axial_dim)
    dropped = at_first & (position < rim_width) | at_last & (position >= extent - rim_width)
    return jnp.where(dropped, jnp.float32(0.0), padded)


def radial_pad(values, rim_width, radial_mode):
    return jnp.pad(
        values, [(0, 0)] * (values.ndim - 1) + [(rim_width, rim_width)], mode=radial_mode
    )


def transport(scalar_pad, vel_pad, density_pad, density_rim, diffusion, step_size):
    center = shifted(scalar_pad, 2, 0, 0)
    density = shifted(density_pad, density_rim, 0, 0)
    change = jnp.zeros_like(center)
    for direction in range(3):
        carried = vel_pad[direction] * scalar_pad
        advect = (
            -shifted(carried, 2, direction, 2)
            + 8.0 * shifted(carried, 2, direction, 1)
            - 8.0 * shifted(carried, 2, direction, -1)
            + shifted(carried, 2, direction, -2)
        ) / 12.0
        upper_flux = (
            0.5
            * diffusion
            * (density + shifted(density_pad, density_rim, direction, 1))
            * (shifted(scalar_pad, 2, direction, 1) - center)
        )
        lower_flux = (
            0.5
            * diffusion
            * (density + shifted(density_pad, density_rim, direction, -1))
            * (center - shifted(scalar_pad, 2, direction, -1))
        )
        change = change - advect + upper_flux - lower_flux
    return center + step_size * change


def evaporate(attrs, gas_values, alive_mask, step_size):
    parcel_mass = attrs[0]
    parcel_temp = attrs[1]
    parcel_vel = attrs[2:5]
    offsets = attrs[5:8]
    gas_heat = gas_values[3]
    gas_fuel = gas_values[4]
    evap_rate = EVAP * jax.nn.softplus(gas_heat - parcel_temp) * (1.0 - gas_fuel)
    new_mass = parcel_mass * jnp.exp(-step_size * evap_rate)
    lost_mass = parcel_mass - new_mass
    new_temp = parcel_temp + step_size * RELAX * (gas_heat - parcel_temp)
    new_vel = parcel_vel + step_size * DRAG * (gas_values[0:3] - parcel_vel)
    new_offsets = offsets + step_size * new_vel
    heat_source = -LATENT * lost_mass - HEAT_CAP * new_mass * (new_temp - parcel_temp)
    new_attrs = (
        jnp.concatenate([new_mass[None], new_temp[None], new_vel, new_offsets], axis=0)
        * alive_mask[None]
    )
    sources = jnp.stack([heat_source * alive_mask, lost_mass * alive_mask])
    return (new_attrs, sources)


def pressure_pad(values):
    padded = extended(values, (("axial", 0), ("azim", 1)), 1)
    return radial_pad(clear_ends(padded, 1, 0), 1, "constant")


def operate(values):
    padded = pressure_pad(values)
    beside = shifted(padded, 1, 0, 1) + shifted(padded, 1, 0, -1)
    beside = beside + shifted(padded, 1, 1, 1) + shifted(padded, 1, 1, -1)
    beside = beside + shifted(padded, 1, 2, 1) + shifted(padded, 1, 2, -1)
    return (6.0 + SHIFT_PRESSURE) * values - beside


def butterfly_partners():
    rounds = []
    for axis in ("azim", "axial"):
        step = 1
        while step < lax.axis_size(axis):
            rounds.append((axis, step))
            step *= 2
    return rounds


def coefficient_cg(gram, size, shift, half_width):
    def apply_a(c):
        out = [shift * c[j] for j in range(size)]
        for j in range(size - 1):
            if j == 0:
                out[1] = out[1] + half_width * c[0]
            else:
                out[j + 1] = out[j + 1] + 0.5 * half_width * c[j]
                out[j - 1] = out[j - 1] + 0.5 * half_width * c[j]
        return out

    def inner(a, b):
        acc = None
        for i in range(size):
            for j in range(size):
                if isinstance(a[i], float) and a[i] == 0.0:
                    continue
                if isinstance(b[j], float) and b[j] == 0.0:
                    continue
                term = a[i] * gram[i][j] * b[j]
                acc = term if acc is None else acc + term
        return acc

    solution_c = [0.0] * size
    residual = [1.0] + [0.0] * (size - 1)
    search = list(residual)
    norm_now = inner(residual, residual)
    for iteration in range(ITERS):
        image = apply_a(search)
        alpha = norm_now / inner(search, image)
        solution_c = [solution_c[j] + alpha * search[j] for j in range(size)]
        residual = [residual[j] - alpha * image[j] for j in range(size)]
        if iteration == ITERS - 1:
            break
        norm_next = inner(residual, residual)
        search = [residual[j] + norm_next / norm_now * search[j] for j in range(size)]
        norm_now = norm_next
    return solution_c


def reduce_kernel(rounds, shift, half_width, vel_ref, *refs):
    size = ITERS + 1
    basis_refs = refs[:size]
    o_ref, send_buf, recv_buf, send_sems, recv_sems = refs[size:]
    here = {"axial": lax.axis_index("axial"), "azim": lax.axis_index("azim")}

    def partner(axis, step):
        index = here[axis]
        other = index + step - 2 * step * ((index // step) % 2)
        coords = dict(here)
        coords[axis] = other
        return (coords["axial"], coords["azim"])

    barrier = pltpu.get_barrier_semaphore()
    for axis, step in rounds:
        pl.semaphore_signal(
            barrier, inc=1, device_id=partner(axis, step), device_id_type=pl.DeviceIdType.MESH
        )
    pl.semaphore_wait(barrier, len(rounds))
    row = lax.broadcasted_iota(jnp.int32, o_ref.shape, 0)
    lane = lax.broadcasted_iota(jnp.int32, o_ref.shape, 1)
    is_max = (row == 0) & (lane == 0)

    def total(x):
        return jnp.sum(jnp.sum(x, axis=0, keepdims=True), axis=1, keepdims=True)

    basis = [ref[...] for ref in basis_refs]
    pairs = [(i, j) for i in range(size) for j in range(i, size)]
    entries = [jnp.max(jnp.max(jnp.abs(vel_ref[...]), axis=0, keepdims=True), axis=1, keepdims=True)]
    entries += [total(basis[i] * basis[j]) for i, j in pairs]
    acc = jnp.zeros(o_ref.shape, jnp.float32)
    for n, entry in enumerate(entries):
        acc = jnp.where((row == 0) & (lane == n), entry, acc)
    for r, (axis, step) in enumerate(rounds):
        send_buf[r] = acc
        copy = pltpu.make_async_remote_copy(
            src_ref=send_buf.at[r],
            dst_ref=recv_buf.at[r],
            send_sem=send_sems.at[r],
            recv_sem=recv_sems.at[r],
            device_id=partner(axis, step),
            device_id_type=pl.DeviceIdType.MESH,
        )
        copy.start()
        copy.wait()
        other = recv_buf[r]
        acc = jnp.where(is_max, jnp.maximum(acc, other), acc + other)
    first = acc[0:1, :]
    first_lane = lax.broadcasted_iota(jnp.int32, first.shape, 1)

    def entry_at(n):
        return jnp.sum(jnp.where(first_lane == n, first, 0.0), axis=1, keepdims=True)

    gram = [[None] * size for _ in range(size)]
    for n, (i, j) in enumerate(pairs):
        gram[i][j] = entry_at(n + 1)
        gram[j][i] = gram[i][j]
    coefficients = coefficient_cg(gram, size, shift, half_width)
    out = jnp.where(lane == ITERS, entry_at(0), 0.0)
    for j in range(ITERS):
        out = jnp.where((lane == j), coefficients[j], out)
    o_ref[...] = out


def pressure_coefficients(velocity, basis, shift, half_width):
    rounds = butterfly_partners()
    flat = [v.reshape(-1, v.shape[-1]) for v in basis]
    out = pl.pallas_call(
        lambda *refs: reduce_kernel(rounds, shift, half_width, *refs),
        out_shape=jax.ShapeDtypeStruct((8, 128), jnp.float32),
        in_specs=[pl.BlockSpec(memory_space=pltpu.VMEM)] * (1 + len(flat)),
        out_specs=pl.BlockSpec(memory_space=pltpu.VMEM),
        scratch_shapes=[
            pltpu.VMEM((len(rounds), 8, 128), jnp.float32),
            pltpu.VMEM((len(rounds), 8, 128), jnp.float32),
            pltpu.SemaphoreType.DMA((len(rounds),)),
            pltpu.SemaphoreType.DMA((len(rounds),)),
        ],
        compiler_params=pltpu.CompilerParams(collective_id=0, has_side_effects=True),
    )(velocity.reshape(-1, velocity.shape[-1]), *flat)
    return [out[0, j] for j in range(ITERS)], out[0, ITERS]


def neighbour_sum(padded):
    beside = shifted(padded, 1, 0, 1) + shifted(padded, 1, 0, -1)
    beside = beside + shifted(padded, 1, 1, 1) + shifted(padded, 1, 1, -1)
    return beside + shifted(padded, 1, 2, 1) + shifted(padded, 1, 2, -1)


def axial_valid(values, rim):
    extent = values.shape[0]
    inner_x = extent - 2 * rim
    first = lax.axis_index("axial") * inner_x - rim
    position = first + lax.broadcasted_iota(jnp.int32, (extent, 1, 1), 0)
    inside = (position >= 0) & (position < inner_x * lax.axis_size("axial"))
    return jnp.where(inside, values, jnp.float32(0.0))


def crop(values, by):
    if by == 0:
        return values
    return values[by:-by, by:-by]


def neighbour_sum_wide(values):
    padded = jnp.pad(values, [(0, 0), (0, 0), (1, 1)])
    nx, ny, nz = padded.shape

    def at(dx, dy, dz):
        return padded[1 + dx : nx - 1 + dx, 1 + dy : ny - 1 + dy, 1 + dz : nz - 1 + dz]

    beside = at(1, 0, 0) + at(-1, 0, 0)
    beside = beside + at(0, 1, 0) + at(0, -1, 0)
    return beside + at(0, 0, 1) + at(0, 0, -1)


def solve_pressure(wide_velocity, velocity):
    half_width = 6.0
    u = wide_velocity
    divergence = 0.5 * (u[0, 2:, 1:-1, 1:-1] - u[0, :-2, 1:-1, 1:-1])
    divergence = divergence + 0.5 * (u[1, 1:-1, 2:, 1:-1] - u[1, 1:-1, :-2, 1:-1])
    divergence = divergence + 0.5 * (u[2, 1:-1, 1:-1, 2:] - u[2, 1:-1, 1:-1, :-2])
    basis = [axial_valid(divergence, ITERS)]
    for j in range(ITERS):
        scaled = neighbour_sum_wide(basis[j]) * (-1.0 / half_width)
        if j == 0:
            fresh = scaled
        else:
            fresh = 2.0 * scaled - crop(basis[j - 1], 2)
        basis.append(axial_valid(fresh, ITERS - 1 - j))
    interior = [crop(basis[j], ITERS - j) for j in range(ITERS + 1)]
    coefficients, fastest = pressure_coefficients(
        velocity, interior, 6.0 + SHIFT_PRESSURE, half_width
    )
    padded_basis = [radial_pad(crop(basis[j], ITERS - j - 1), 1, "constant") for j in range(ITERS)]
    padded_pressure = coefficients[0] * padded_basis[0]
    for j in range(1, ITERS):
        padded_pressure = padded_pressure + coefficients[j] * padded_basis[j]
    return padded_pressure, fastest


def along_axial(buffer, step_by):
    return shifted_2(buffer, "axial", step_by)


def along_azim(buffer, step_by):
    return shifted_3(buffer, "azim", step_by)


def on_device(state, diff_coef, parcel_state, parcel_cell, parcel_dest, live_count):
    velocity = state[1:4]
    whole_pad = extended(state, (("axial", 1), ("azim", 2)), 2)
    whole_pad = radial_pad(clear_ends(whole_pad, 2, 1), 2, "edge")
    moving = whole_pad[1:]
    density_pad = whole_pad[0]
    density_rim = 2
    vel_pad = moving[0:3]
    wide_velocity = extended(velocity, (("axial", 1), ("azim", 2)), ITERS + 1)
    wide_velocity = radial_pad(clear_ends(wide_velocity, ITERS + 1, 1), 1, "edge")
    padded_pressure, fastest = solve_pressure(wide_velocity, velocity)
    step_size = CFL / (fastest + 1e-06)
    transported = transport(
        moving[3:], vel_pad, density_pad, density_rim, diff_coef[:, None, None, None], step_size
    )
    npar_local = parcel_cell.shape[0]
    block_rows = 512
    cells_x, cells_y, cells_z = (state.shape[1], state.shape[2], state.shape[3])
    plane_count = cells_x * cells_y
    gas_table = jnp.transpose(state[1:6].reshape(5, plane_count, cells_z), (1, 0, 2)).reshape(
        plane_count, 5 * cells_z
    )
    live_now = live_count[0]

    def one_block(block_index, carried_pair):
        deposit, updated = carried_pair
        first_slot = block_index * block_rows
        cell_ids = lax.dynamic_slice_in_dim(parcel_cell, first_slot, block_rows)
        attrs = lax.dynamic_slice_in_dim(parcel_state, first_slot, block_rows, 1)
        alive_mask = (first_slot + jnp.arange(block_rows) < live_now).astype(jnp.float32)
        plane_ids = cell_ids // cells_z
        radial_ids = cell_ids % cells_z
        plane_hot = (plane_ids[:, None] == jnp.arange(plane_count)[None, :]).astype(jnp.float32)
        radial_hot = (radial_ids[:, None] == jnp.arange(cells_z)[None, :]).astype(jnp.float32)
        gas_rows = jnp.dot(plane_hot, gas_table, precision=HIGHEST).reshape(block_rows, 5, cells_z)
        gas_values = jnp.sum(gas_rows * radial_hot[:, None, :], axis=2).T
        new_attrs, sources = evaporate(attrs, gas_values, alive_mask, step_size)
        spread = (sources.T[:, :, None] * radial_hot[:, None, :]).reshape(block_rows, 2 * cells_z)
        deposit = deposit + lax.dot_general(
            plane_hot, spread, (((0,), (0,)), ((), ())), precision=HIGHEST
        )
        updated = lax.dynamic_update_slice_in_dim(updated, new_attrs, first_slot, 1)
        return (deposit, updated)

    initial = (jnp.zeros((plane_count, 2 * cells_z), jnp.float32), jnp.zeros_like(parcel_state))
    block_count = npar_local // block_rows
    deposit, updated = lax.fori_loop(0, block_count, one_block, initial)
    deposit = jnp.transpose(deposit.reshape(cells_x, cells_y, 2, cells_z), (2, 0, 1, 3))
    scalars_new = jnp.concatenate(
        [transported[:2] + deposit / state[0][None], transported[2:]], axis=0
    )
    slot_alive = jnp.arange(npar_local) < live_now
    stacked = jnp.stack([(parcel_dest == d + 1) & slot_alive for d in range(4)]).astype(jnp.int32)
    ranks = jnp.cumsum(stacked, axis=1) - 1
    mover = jnp.sum(stacked, axis=0) > 0
    target = jnp.where(mover, jnp.sum(stacked * (jnp.arange(4)[:, None] * CAP + ranks), axis=0), -1)
    select = (target[:, None] == jnp.arange(4 * CAP)[None, :]).astype(jnp.float32)
    buffers = jnp.transpose(
        jnp.dot(updated, select, precision=HIGHEST).reshape(updated.shape[0], 4, CAP), (1, 0, 2)
    )
    arrived = jnp.stack(
        [
            along_axial(buffers[0], -1),
            along_axial(buffers[1], 1),
            along_azim(buffers[2], -1),
            along_azim(buffers[3], 1),
        ]
    )
    kept_parcels = jnp.where((parcel_dest == 0)[None], updated, jnp.float32(0.0))
    velocity_new = jnp.stack(
        [
            velocity[d]
            - 0.5 * (shifted(padded_pressure, 1, d, 1) - shifted(padded_pressure, 1, d, -1))
            for d in range(3)
        ]
    )
    return (scalars_new, velocity_new, kept_parcels, arrived)


def solution(mesh):
    in_specs = (
        P(None, "axial", "azim", None),
        P(),
        P(None, ("axial", "azim")),
        P(("axial", "azim")),
        P(("axial", "azim")),
        P(("axial", "azim")),
    )
    out_specs = (
        P(None, "axial", "azim", None),
        P(None, "axial", "azim", None),
        P(None, ("axial", "azim")),
        P(None, None, ("axial", "azim")),
    )
    return jax.shard_map(
        on_device, mesh=mesh, in_specs=in_specs, out_specs=out_specs, check_vma=False
    )
```

```python
import jax
import jax.numpy as jnp
from jax import lax
from jax.sharding import PartitionSpec as P
from jax.experimental import pallas as pl
from jax.experimental.pallas import tpu as pltpu

CAP = 64
ITERS = 4


CFL = 0.4
SHIFT_PRESSURE = 0.25
EVAP = 8.0
RELAX = 4.0
DRAG = 6.0
LATENT = 0.5
HEAT_CAP = 0.8
HIGHEST = lax.Precision.HIGHEST


def extended(block, sides, width):
    for axis, dim in sides:
        count = lax.axis_size(axis)
        forward = [(i, i + 1) for i in range(count - 1)]
        forward.append((count - 1, 0))
        backward = [(target, source) for source, target in forward]
        low = lax.ppermute(
            lax.slice_in_dim(block, block.shape[dim] - width, None, axis=dim), axis, forward
        )
        high = lax.ppermute(lax.slice_in_dim(block, 0, width, axis=dim), axis, backward)
        block = jnp.concatenate([low, block, high], axis=dim)
    return block


def shifted_2(shard, axis, by):
    length = lax.axis_size(axis)
    pairs = [(i, i + by) for i in range(length) if 0 <= i + by < length]
    return lax.ppermute(shard, axis, pairs)


def shifted_3(shard, axis, by):
    length = lax.axis_size(axis)
    return lax.ppermute(shard, axis, [(i, (i + by) % length) for i in range(length)])


def shifted(padded, rim_width, direction, step_by):
    selector = []
    total_dims = padded.ndim
    for dim_index in range(total_dims):
        extent = padded.shape[dim_index]
        if dim_index == total_dims - 3 + direction:
            selector.append(slice(rim_width + step_by, extent - rim_width + step_by))
        elif dim_index >= total_dims - 3:
            selector.append(slice(rim_width, extent - rim_width))
        else:
            selector.append(slice(None))
    return padded[tuple(selector)]


def clear_ends(padded, rim_width, axial_dim):
    extent = padded.shape[axial_dim]
    at_first = lax.axis_index("axial") == 0
    at_last = lax.axis_index("axial") == lax.axis_size("axial") - 1
    shape_list = [1] * padded.ndim
    shape_list[axial_dim] = extent
    position = lax.broadcasted_iota(jnp.int32, tuple(shape_list), axial_dim)
    dropped = at_first & (position < rim_width) | at_last & (position >= extent - rim_width)
    return jnp.where(dropped, jnp.float32(0.0), padded)


def radial_pad(values, rim_width, radial_mode):
    return jnp.pad(
        values, [(0, 0)] * (values.ndim - 1) + [(rim_width, rim_width)], mode=radial_mode
    )


def transport(scalar_pad, vel_pad, density_pad, density_rim, diffusion, step_size):
    center = shifted(scalar_pad, 2, 0, 0)
    density = shifted(density_pad, density_rim, 0, 0)
    change = jnp.zeros_like(center)
    for direction in range(3):
        carried = vel_pad[direction] * scalar_pad
        advect = (
            -shifted(carried, 2, direction, 2)
            + 8.0 * shifted(carried, 2, direction, 1)
            - 8.0 * shifted(carried, 2, direction, -1)
            + shifted(carried, 2, direction, -2)
        ) / 12.0
        upper_flux = (
            0.5
            * diffusion
            * (density + shifted(density_pad, density_rim, direction, 1))
            * (shifted(scalar_pad, 2, direction, 1) - center)
        )
        lower_flux = (
            0.5
            * diffusion
            * (density + shifted(density_pad, density_rim, direction, -1))
            * (center - shifted(scalar_pad, 2, direction, -1))
        )
        change = change - advect + upper_flux - lower_flux
    return center + step_size * change


def evaporate(attrs, gas_values, alive_mask, step_size):
    parcel_mass = attrs[0]
    parcel_temp = attrs[1]
    parcel_vel = attrs[2:5]
    offsets = attrs[5:8]
    gas_heat = gas_values[3]
    gas_fuel = gas_values[4]
    evap_rate = EVAP * jax.nn.softplus(gas_heat - parcel_temp) * (1.0 - gas_fuel)
    new_mass = parcel_mass * jnp.exp(-step_size * evap_rate)
    lost_mass = parcel_mass - new_mass
    new_temp = parcel_temp + step_size * RELAX * (gas_heat - parcel_temp)
    new_vel = parcel_vel + step_size * DRAG * (gas_values[0:3] - parcel_vel)
    new_offsets = offsets + step_size * new_vel
    heat_source = -LATENT * lost_mass - HEAT_CAP * new_mass * (new_temp - parcel_temp)
    new_attrs = (
        jnp.concatenate([new_mass[None], new_temp[None], new_vel, new_offsets], axis=0)
        * alive_mask[None]
    )
    sources = jnp.stack([heat_source * alive_mask, lost_mass * alive_mask])
    return (new_attrs, sources)


def pressure_pad(values):
    padded = extended(values, (("axial", 0), ("azim", 1)), 1)
    return radial_pad(clear_ends(padded, 1, 0), 1, "constant")


def operate(values):
    padded = pressure_pad(values)
    beside = shifted(padded, 1, 0, 1) + shifted(padded, 1, 0, -1)
    beside = beside + shifted(padded, 1, 1, 1) + shifted(padded, 1, 1, -1)
    beside = beside + shifted(padded, 1, 2, 1) + shifted(padded, 1, 2, -1)
    return (6.0 + SHIFT_PRESSURE) * values - beside


def reduce_groups():
    axial = lax.axis_size("axial")
    along_x = 4 if axial % 4 == 0 else 1
    groups = [("azim", 1, lax.axis_size("azim")), ("axial", 1, along_x), ("axial", along_x, axial // along_x)]
    return [group for group in groups if group[2] > 1]


def coefficient_cg(gram, size, shift, half_width):
    def apply_a(c):
        out = [shift * c[j] for j in range(size)]
        for j in range(size - 1):
            if j == 0:
                out[1] = out[1] + half_width * c[0]
            else:
                out[j + 1] = out[j + 1] + 0.5 * half_width * c[j]
                out[j - 1] = out[j - 1] + 0.5 * half_width * c[j]
        return out

    def inner(a, b):
        acc = None
        for i in range(size):
            for j in range(size):
                if isinstance(a[i], float) and a[i] == 0.0:
                    continue
                if isinstance(b[j], float) and b[j] == 0.0:
                    continue
                term = a[i] * gram[i][j] * b[j]
                acc = term if acc is None else acc + term
        return acc

    solution_c = [0.0] * size
    residual = [1.0] + [0.0] * (size - 1)
    search = list(residual)
    norm_now = inner(residual, residual)
    for iteration in range(ITERS):
        image = apply_a(search)
        alpha = norm_now / inner(search, image)
        solution_c = [solution_c[j] + alpha * search[j] for j in range(size)]
        residual = [residual[j] - alpha * image[j] for j in range(size)]
        if iteration == ITERS - 1:
            break
        norm_next = inner(residual, residual)
        search = [residual[j] + norm_next / norm_now * search[j] for j in range(size)]
        norm_now = norm_next
    return solution_c


def reduce_kernel(groups, shift, half_width, vel_ref, *refs):
    size = ITERS + 1
    basis_refs = refs[:size]
    o_ref, slots, send_sems, recv_sems = refs[size:]
    here = {"axial": lax.axis_index("axial"), "azim": lax.axis_index("azim")}

    def member(axis, stride, count, m):
        index = here[axis]
        base = index - ((index // stride) % count) * stride
        coords = dict(here)
        coords[axis] = base + m * stride
        return (coords["axial"], coords["azim"])

    def position(axis, stride, count):
        return (here[axis] // stride) % count

    barrier = pltpu.get_barrier_semaphore()
    greeted = 0
    for axis, stride, count in groups:
        mine = position(axis, stride, count)
        for m in range(1, count):
            pl.semaphore_signal(
                barrier,
                inc=1,
                device_id=member(axis, stride, count, (mine + m) % count),
                device_id_type=pl.DeviceIdType.MESH,
            )
            greeted += 1
    pl.semaphore_wait(barrier, greeted)
    row = lax.broadcasted_iota(jnp.int32, o_ref.shape, 0)
    lane = lax.broadcasted_iota(jnp.int32, o_ref.shape, 1)
    is_max = (row == 0) & (lane == 0)

    def total(x):
        return jnp.sum(jnp.sum(x, axis=0, keepdims=True), axis=1, keepdims=True)

    basis = [ref[...] for ref in basis_refs]
    pairs = [(i, j) for i in range(size) for j in range(i, size)]
    entries = [jnp.max(jnp.max(jnp.abs(vel_ref[...]), axis=0, keepdims=True), axis=1, keepdims=True)]
    entries += [total(basis[i] * basis[j]) for i, j in pairs]
    acc = jnp.zeros(o_ref.shape, jnp.float32)
    for n, entry in enumerate(entries):
        acc = jnp.where((row == 0) & (lane == n), entry, acc)
    offset = 0
    for axis, stride, count in groups:
        mine = position(axis, stride, count)
        slots[offset + mine] = acc
        copies = []
        for m in range(1, count):
            target = (mine + m) % count
            copy = pltpu.make_async_remote_copy(
                src_ref=slots.at[offset + mine],
                dst_ref=slots.at[offset + mine],
                send_sem=send_sems.at[offset + target],
                recv_sem=recv_sems.at[offset + mine],
                device_id=member(axis, stride, count, target),
                device_id_type=pl.DeviceIdType.MESH,
            )
            copy.start()
            copies.append(copy)
        for copy in copies:
            copy.wait_send()
        for m in range(count):
            incoming = pltpu.make_async_remote_copy(
                src_ref=slots.at[offset + m],
                dst_ref=slots.at[offset + m],
                send_sem=send_sems.at[offset + m],
                recv_sem=recv_sems.at[offset + m],
                device_id=member(axis, stride, count, m),
                device_id_type=pl.DeviceIdType.MESH,
            )

            @pl.when(m != mine)
            def _():
                incoming.wait_recv()

        combined = slots[offset]
        for m in range(1, count):
            other = slots[offset + m]
            combined = jnp.where(is_max, jnp.maximum(combined, other), combined + other)
        acc = combined
        offset += count
    first = acc[0:1, :]
    first_lane = lax.broadcasted_iota(jnp.int32, first.shape, 1)

    def entry_at(n):
        return jnp.sum(jnp.where(first_lane == n, first, 0.0), axis=1, keepdims=True)

    gram = [[None] * size for _ in range(size)]
    for n, (i, j) in enumerate(pairs):
        gram[i][j] = entry_at(n + 1)
        gram[j][i] = gram[i][j]
    coefficients = coefficient_cg(gram, size, shift, half_width)
    out = jnp.where(lane == ITERS, entry_at(0), 0.0)
    for j in range(ITERS):
        out = jnp.where((lane == j), coefficients[j], out)
    o_ref[...] = out


def pressure_coefficients(velocity, basis, shift, half_width):
    groups = reduce_groups()
    slot_count = sum(count for _, _, count in groups)
    flat = [v.reshape(-1, v.shape[-1]) for v in basis]
    out = pl.pallas_call(
        lambda *refs: reduce_kernel(groups, shift, half_width, *refs),
        out_shape=jax.ShapeDtypeStruct((8, 128), jnp.float32),
        in_specs=[pl.BlockSpec(memory_space=pltpu.VMEM)] * (1 + len(flat)),
        out_specs=pl.BlockSpec(memory_space=pltpu.VMEM),
        scratch_shapes=[
            pltpu.VMEM((slot_count, 8, 128), jnp.float32),
            pltpu.SemaphoreType.DMA((slot_count,)),
            pltpu.SemaphoreType.DMA((slot_count,)),
        ],
        compiler_params=pltpu.CompilerParams(collective_id=0, has_side_effects=True),
    )(velocity.reshape(-1, velocity.shape[-1]), *flat)
    return [out[0, j] for j in range(ITERS)], out[0, ITERS]


def neighbour_sum(padded):
    beside = shifted(padded, 1, 0, 1) + shifted(padded, 1, 0, -1)
    beside = beside + shifted(padded, 1, 1, 1) + shifted(padded, 1, 1, -1)
    return beside + shifted(padded, 1, 2, 1) + shifted(padded, 1, 2, -1)


def axial_valid(values, rim):
    extent = values.shape[0]
    inner_x = extent - 2 * rim
    first = lax.axis_index("axial") * inner_x - rim
    position = first + lax.broadcasted_iota(jnp.int32, (extent, 1, 1), 0)
    inside = (position >= 0) & (position < inner_x * lax.axis_size("axial"))
    return jnp.where(inside, values, jnp.float32(0.0))


def crop(values, by):
    if by == 0:
        return values
    return values[by:-by, by:-by]


def neighbour_sum_wide(values):
    padded = jnp.pad(values, [(0, 0), (0, 0), (1, 1)])
    nx, ny, nz = padded.shape

    def at(dx, dy, dz):
        return padded[1 + dx : nx - 1 + dx, 1 + dy : ny - 1 + dy, 1 + dz : nz - 1 + dz]

    beside = at(1, 0, 0) + at(-1, 0, 0)
    beside = beside + at(0, 1, 0) + at(0, -1, 0)
    return beside + at(0, 0, 1) + at(0, 0, -1)


def solve_pressure(wide_velocity, velocity):
    half_width = 6.0
    u = wide_velocity
    divergence = 0.5 * (u[0, 2:, 1:-1, 1:-1] - u[0, :-2, 1:-1, 1:-1])
    divergence = divergence + 0.5 * (u[1, 1:-1, 2:, 1:-1] - u[1, 1:-1, :-2, 1:-1])
    divergence = divergence + 0.5 * (u[2, 1:-1, 1:-1, 2:] - u[2, 1:-1, 1:-1, :-2])
    basis = [axial_valid(divergence, ITERS)]
    for j in range(ITERS):
        scaled = neighbour_sum_wide(basis[j]) * (-1.0 / half_width)
        if j == 0:
            fresh = scaled
        else:
            fresh = 2.0 * scaled - crop(basis[j - 1], 2)
        basis.append(axial_valid(fresh, ITERS - 1 - j))
    interior = [crop(basis[j], ITERS - j) for j in range(ITERS + 1)]
    coefficients, fastest = pressure_coefficients(
        velocity, interior, 6.0 + SHIFT_PRESSURE, half_width
    )
    padded_basis = [radial_pad(crop(basis[j], ITERS - j - 1), 1, "constant") for j in range(ITERS)]
    padded_pressure = coefficients[0] * padded_basis[0]
    for j in range(1, ITERS):
        padded_pressure = padded_pressure + coefficients[j] * padded_basis[j]
    return padded_pressure, fastest


def along_axial(buffer, step_by):
    return shifted_2(buffer, "axial", step_by)


def along_azim(buffer, step_by):
    return shifted_3(buffer, "azim", step_by)


def on_device(state, diff_coef, parcel_state, parcel_cell, parcel_dest, live_count):
    velocity = state[1:4]
    whole_pad = extended(state, (("axial", 1), ("azim", 2)), 2)
    whole_pad = radial_pad(clear_ends(whole_pad, 2, 1), 2, "edge")
    moving = whole_pad[1:]
    density_pad = whole_pad[0]
    density_rim = 2
    vel_pad = moving[0:3]
    wide_velocity = extended(velocity, (("axial", 1), ("azim", 2)), ITERS + 1)
    wide_velocity = radial_pad(clear_ends(wide_velocity, ITERS + 1, 1), 1, "edge")
    padded_pressure, fastest = solve_pressure(wide_velocity, velocity)
    step_size = CFL / (fastest + 1e-06)
    transported = transport(
        moving[3:], vel_pad, density_pad, density_rim, diff_coef[:, None, None, None], step_size
    )
    npar_local = parcel_cell.shape[0]
    block_rows = 512
    cells_x, cells_y, cells_z = (state.shape[1], state.shape[2], state.shape[3])
    plane_count = cells_x * cells_y
    gas_table = jnp.transpose(state[1:6].reshape(5, plane_count, cells_z), (1, 0, 2)).reshape(
        plane_count, 5 * cells_z
    )
    live_now = live_count[0]

    def one_block(block_index, carried_pair):
        deposit, updated = carried_pair
        first_slot = block_index * block_rows
        cell_ids = lax.dynamic_slice_in_dim(parcel_cell, first_slot, block_rows)
        attrs = lax.dynamic_slice_in_dim(parcel_state, first_slot, block_rows, 1)
        alive_mask = (first_slot + jnp.arange(block_rows) < live_now).astype(jnp.float32)
        plane_ids = cell_ids // cells_z
        radial_ids = cell_ids % cells_z
        plane_hot = (plane_ids[:, None] == jnp.arange(plane_count)[None, :]).astype(jnp.float32)
        radial_hot = (radial_ids[:, None] == jnp.arange(cells_z)[None, :]).astype(jnp.float32)
        gas_rows = jnp.dot(plane_hot, gas_table, precision=HIGHEST).reshape(block_rows, 5, cells_z)
        gas_values = jnp.sum(gas_rows * radial_hot[:, None, :], axis=2).T
        new_attrs, sources = evaporate(attrs, gas_values, alive_mask, step_size)
        spread = (sources.T[:, :, None] * radial_hot[:, None, :]).reshape(block_rows, 2 * cells_z)
        deposit = deposit + lax.dot_general(
            plane_hot, spread, (((0,), (0,)), ((), ())), precision=HIGHEST
        )
        updated = lax.dynamic_update_slice_in_dim(updated, new_attrs, first_slot, 1)
        return (deposit, updated)

    initial = (jnp.zeros((plane_count, 2 * cells_z), jnp.float32), jnp.zeros_like(parcel_state))
    block_count = npar_local // block_rows
    deposit, updated = lax.fori_loop(0, block_count, one_block, initial)
    deposit = jnp.transpose(deposit.reshape(cells_x, cells_y, 2, cells_z), (2, 0, 1, 3))
    scalars_new = jnp.concatenate(
        [transported[:2] + deposit / state[0][None], transported[2:]], axis=0
    )
    slot_alive = jnp.arange(npar_local) < live_now
    stacked = jnp.stack([(parcel_dest == d + 1) & slot_alive for d in range(4)]).astype(jnp.int32)
    ranks = jnp.cumsum(stacked, axis=1) - 1
    mover = jnp.sum(stacked, axis=0) > 0
    target = jnp.where(mover, jnp.sum(stacked * (jnp.arange(4)[:, None] * CAP + ranks), axis=0), -1)
    select = (target[:, None] == jnp.arange(4 * CAP)[None, :]).astype(jnp.float32)
    buffers = jnp.transpose(
        jnp.dot(updated, select, precision=HIGHEST).reshape(updated.shape[0], 4, CAP), (1, 0, 2)
    )
    arrived = jnp.stack(
        [
            along_axial(buffers[0], -1),
            along_axial(buffers[1], 1),
            along_azim(buffers[2], -1),
            along_azim(buffers[3], 1),
        ]
    )
    kept_parcels = jnp.where((parcel_dest == 0)[None], updated, jnp.float32(0.0))
    velocity_new = jnp.stack(
        [
            velocity[d]
            - 0.5 * (shifted(padded_pressure, 1, d, 1) - shifted(padded_pressure, 1, d, -1))
            for d in range(3)
        ]
    )
    return (scalars_new, velocity_new, kept_parcels, arrived)


def solution(mesh):
    in_specs = (
        P(None, "axial", "azim", None),
        P(),
        P(None, ("axial", "azim")),
        P(("axial", "azim")),
        P(("axial", "azim")),
        P(("axial", "azim")),
    )
    out_specs = (
        P(None, "axial", "azim", None),
        P(None, "axial", "azim", None),
        P(None, ("axial", "azim")),
        P(None, None, ("axial", "azim")),
    )
    return jax.shard_map(
        on_device, mesh=mesh, in_specs=in_specs, out_specs=out_specs, check_vma=False
    )
```

```python
import jax
import jax.numpy as jnp
from jax import lax
from jax.sharding import PartitionSpec as P
from jax.experimental import pallas as pl
from jax.experimental.pallas import tpu as pltpu

CAP = 64
ITERS = 4


CFL = 0.4
SHIFT_PRESSURE = 0.25
EVAP = 8.0
RELAX = 4.0
DRAG = 6.0
LATENT = 0.5
HEAT_CAP = 0.8
HIGHEST = lax.Precision.HIGHEST


def extended(block, sides, width):
    for axis, dim in sides:
        count = lax.axis_size(axis)
        forward = [(i, i + 1) for i in range(count - 1)]
        forward.append((count - 1, 0))
        backward = [(target, source) for source, target in forward]
        low = lax.ppermute(
            lax.slice_in_dim(block, block.shape[dim] - width, None, axis=dim), axis, forward
        )
        high = lax.ppermute(lax.slice_in_dim(block, 0, width, axis=dim), axis, backward)
        block = jnp.concatenate([low, block, high], axis=dim)
    return block


def shifted_2(shard, axis, by):
    length = lax.axis_size(axis)
    pairs = [(i, i + by) for i in range(length) if 0 <= i + by < length]
    return lax.ppermute(shard, axis, pairs)


def shifted_3(shard, axis, by):
    length = lax.axis_size(axis)
    return lax.ppermute(shard, axis, [(i, (i + by) % length) for i in range(length)])


def shifted(padded, rim_width, direction, step_by):
    selector = []
    total_dims = padded.ndim
    for dim_index in range(total_dims):
        extent = padded.shape[dim_index]
        if dim_index == total_dims - 3 + direction:
            selector.append(slice(rim_width + step_by, extent - rim_width + step_by))
        elif dim_index >= total_dims - 3:
            selector.append(slice(rim_width, extent - rim_width))
        else:
            selector.append(slice(None))
    return padded[tuple(selector)]


def clear_ends(padded, rim_width, axial_dim):
    extent = padded.shape[axial_dim]
    at_first = lax.axis_index("axial") == 0
    at_last = lax.axis_index("axial") == lax.axis_size("axial") - 1
    shape_list = [1] * padded.ndim
    shape_list[axial_dim] = extent
    position = lax.broadcasted_iota(jnp.int32, tuple(shape_list), axial_dim)
    dropped = at_first & (position < rim_width) | at_last & (position >= extent - rim_width)
    return jnp.where(dropped, jnp.float32(0.0), padded)


def radial_pad(values, rim_width, radial_mode):
    return jnp.pad(
        values, [(0, 0)] * (values.ndim - 1) + [(rim_width, rim_width)], mode=radial_mode
    )


def transport(scalar_pad, vel_pad, density_pad, density_rim, diffusion, step_size):
    center = shifted(scalar_pad, 2, 0, 0)
    density = shifted(density_pad, density_rim, 0, 0)
    change = jnp.zeros_like(center)
    for direction in range(3):
        carried = vel_pad[direction] * scalar_pad
        advect = (
            -shifted(carried, 2, direction, 2)
            + 8.0 * shifted(carried, 2, direction, 1)
            - 8.0 * shifted(carried, 2, direction, -1)
            + shifted(carried, 2, direction, -2)
        ) / 12.0
        upper_flux = (
            0.5
            * diffusion
            * (density + shifted(density_pad, density_rim, direction, 1))
            * (shifted(scalar_pad, 2, direction, 1) - center)
        )
        lower_flux = (
            0.5
            * diffusion
            * (density + shifted(density_pad, density_rim, direction, -1))
            * (center - shifted(scalar_pad, 2, direction, -1))
        )
        change = change - advect + upper_flux - lower_flux
    return center + step_size * change


def evaporate(attrs, gas_values, alive_mask, step_size):
    parcel_mass = attrs[0]
    parcel_temp = attrs[1]
    parcel_vel = attrs[2:5]
    offsets = attrs[5:8]
    gas_heat = gas_values[3]
    gas_fuel = gas_values[4]
    evap_rate = EVAP * jax.nn.softplus(gas_heat - parcel_temp) * (1.0 - gas_fuel)
    new_mass = parcel_mass * jnp.exp(-step_size * evap_rate)
    lost_mass = parcel_mass - new_mass
    new_temp = parcel_temp + step_size * RELAX * (gas_heat - parcel_temp)
    new_vel = parcel_vel + step_size * DRAG * (gas_values[0:3] - parcel_vel)
    new_offsets = offsets + step_size * new_vel
    heat_source = -LATENT * lost_mass - HEAT_CAP * new_mass * (new_temp - parcel_temp)
    new_attrs = (
        jnp.concatenate([new_mass[None], new_temp[None], new_vel, new_offsets], axis=0)
        * alive_mask[None]
    )
    sources = jnp.stack([heat_source * alive_mask, lost_mass * alive_mask])
    return (new_attrs, sources)


def pressure_pad(values):
    padded = extended(values, (("axial", 0), ("azim", 1)), 1)
    return radial_pad(clear_ends(padded, 1, 0), 1, "constant")


def operate(values):
    padded = pressure_pad(values)
    beside = shifted(padded, 1, 0, 1) + shifted(padded, 1, 0, -1)
    beside = beside + shifted(padded, 1, 1, 1) + shifted(padded, 1, 1, -1)
    beside = beside + shifted(padded, 1, 2, 1) + shifted(padded, 1, 2, -1)
    return (6.0 + SHIFT_PRESSURE) * values - beside


def reduce_groups():
    axial = lax.axis_size("axial")
    along_x = 4 if axial % 4 == 0 else 1
    groups = [("azim", 1, lax.axis_size("azim")), ("axial", 1, along_x), ("axial", along_x, axial // along_x)]
    return [group for group in groups if group[2] > 1]


def coefficient_cg(gram, size, shift, half_width):
    def apply_a(c):
        out = [shift * c[j] for j in range(size)]
        for j in range(size - 1):
            if j == 0:
                out[1] = out[1] + half_width * c[0]
            else:
                out[j + 1] = out[j + 1] + 0.5 * half_width * c[j]
                out[j - 1] = out[j - 1] + 0.5 * half_width * c[j]
        return out

    def inner(a, b):
        acc = None
        for i in range(size):
            for j in range(size):
                if isinstance(a[i], float) and a[i] == 0.0:
                    continue
                if isinstance(b[j], float) and b[j] == 0.0:
                    continue
                term = a[i] * gram[i][j] * b[j]
                acc = term if acc is None else acc + term
        return acc

    solution_c = [0.0] * size
    residual = [1.0] + [0.0] * (size - 1)
    search = list(residual)
    norm_now = inner(residual, residual)
    for iteration in range(ITERS):
        image = apply_a(search)
        alpha = norm_now / inner(search, image)
        solution_c = [solution_c[j] + alpha * search[j] for j in range(size)]
        residual = [residual[j] - alpha * image[j] for j in range(size)]
        if iteration == ITERS - 1:
            break
        norm_next = inner(residual, residual)
        search = [residual[j] + norm_next / norm_now * search[j] for j in range(size)]
        norm_now = norm_next
    return solution_c


def reduce_kernel(groups, shift, half_width, vel_ref, *refs):
    size = ITERS + 1
    basis_refs = refs[:size]
    o_ref, slots, send_sems, recv_sems = refs[size:]
    here = {"axial": lax.axis_index("axial"), "azim": lax.axis_index("azim")}

    def member(axis, stride, count, m):
        index = here[axis]
        base = index - ((index // stride) % count) * stride
        coords = dict(here)
        coords[axis] = base + m * stride
        return (coords["axial"], coords["azim"])

    def position(axis, stride, count):
        return (here[axis] // stride) % count

    barrier = pltpu.get_barrier_semaphore()
    greeted = 0
    for axis, stride, count in groups:
        mine = position(axis, stride, count)
        for m in range(1, count):
            pl.semaphore_signal(
                barrier,
                inc=1,
                device_id=member(axis, stride, count, (mine + m) % count),
                device_id_type=pl.DeviceIdType.MESH,
            )
            greeted += 1
    pl.semaphore_wait(barrier, greeted)
    row = lax.broadcasted_iota(jnp.int32, o_ref.shape, 0)
    lane = lax.broadcasted_iota(jnp.int32, o_ref.shape, 1)
    is_max = (row == 0) & (lane == 0)

    def total(x):
        return jnp.sum(jnp.sum(x, axis=0, keepdims=True), axis=1, keepdims=True)

    basis = [ref[...] for ref in basis_refs]
    pairs = [(i, j) for i in range(size) for j in range(i, size)]
    entries = [jnp.max(jnp.max(jnp.abs(vel_ref[...]), axis=0, keepdims=True), axis=1, keepdims=True)]
    entries += [total(basis[i] * basis[j]) for i, j in pairs]
    acc = jnp.zeros(o_ref.shape, jnp.float32)
    for n, entry in enumerate(entries):
        acc = jnp.where((row == 0) & (lane == n), entry, acc)
    offset = 0
    for axis, stride, count in groups:
        mine = position(axis, stride, count)
        slots[offset + mine] = acc
        copies = []
        for m in range(1, count):
            target = (mine + m) % count
            copy = pltpu.make_async_remote_copy(
                src_ref=slots.at[offset + mine],
                dst_ref=slots.at[offset + mine],
                send_sem=send_sems.at[offset + target],
                recv_sem=recv_sems.at[offset + mine],
                device_id=member(axis, stride, count, target),
                device_id_type=pl.DeviceIdType.MESH,
            )
            copy.start()
            copies.append(copy)
        for copy in copies:
            copy.wait_send()
        for m in range(count):
            incoming = pltpu.make_async_remote_copy(
                src_ref=slots.at[offset + m],
                dst_ref=slots.at[offset + m],
                send_sem=send_sems.at[offset + m],
                recv_sem=recv_sems.at[offset + m],
                device_id=member(axis, stride, count, m),
                device_id_type=pl.DeviceIdType.MESH,
            )

            @pl.when(m != mine)
            def _():
                incoming.wait_recv()

        combined = slots[offset]
        for m in range(1, count):
            other = slots[offset + m]
            combined = jnp.where(is_max, jnp.maximum(combined, other), combined + other)
        acc = combined
        offset += count
    first = acc[0:1, :]
    first_lane = lax.broadcasted_iota(jnp.int32, first.shape, 1)

    def entry_at(n):
        return jnp.sum(jnp.where(first_lane == n, first, 0.0), axis=1, keepdims=True)

    gram = [[None] * size for _ in range(size)]
    for n, (i, j) in enumerate(pairs):
        gram[i][j] = entry_at(n + 1)
        gram[j][i] = gram[i][j]
    coefficients = coefficient_cg(gram, size, shift, half_width)
    out = jnp.where(lane == ITERS, entry_at(0), 0.0)
    for j in range(ITERS):
        out = jnp.where((lane == j), coefficients[j], out)
    o_ref[...] = out


def pressure_coefficients(velocity, basis, shift, half_width):
    groups = reduce_groups()
    slot_count = sum(count for _, _, count in groups)
    flat = [v.reshape(-1, v.shape[-1]) for v in basis]
    out = pl.pallas_call(
        lambda *refs: reduce_kernel(groups, shift, half_width, *refs),
        out_shape=jax.ShapeDtypeStruct((8, 128), jnp.float32),
        in_specs=[pl.BlockSpec(memory_space=pltpu.VMEM)] * (1 + len(flat)),
        out_specs=pl.BlockSpec(memory_space=pltpu.VMEM),
        scratch_shapes=[
            pltpu.VMEM((slot_count, 8, 128), jnp.float32),
            pltpu.SemaphoreType.DMA((slot_count,)),
            pltpu.SemaphoreType.DMA((slot_count,)),
        ],
        compiler_params=pltpu.CompilerParams(collective_id=0, has_side_effects=True),
    )(velocity.reshape(-1, velocity.shape[-1]), *flat)
    return [out[0, j] for j in range(ITERS)], out[0, ITERS]


def neighbour_sum(padded):
    beside = shifted(padded, 1, 0, 1) + shifted(padded, 1, 0, -1)
    beside = beside + shifted(padded, 1, 1, 1) + shifted(padded, 1, 1, -1)
    return beside + shifted(padded, 1, 2, 1) + shifted(padded, 1, 2, -1)


def axial_valid(values, rim):
    extent = values.shape[0]
    inner_x = extent - 2 * rim
    first = lax.axis_index("axial") * inner_x - rim
    position = first + lax.broadcasted_iota(jnp.int32, (extent, 1, 1), 0)
    inside = (position >= 0) & (position < inner_x * lax.axis_size("axial"))
    return jnp.where(inside, values, jnp.float32(0.0))


def crop(values, by):
    if by == 0:
        return values
    return values[by:-by, by:-by]


def neighbour_sum_wide(values):
    padded = jnp.pad(values, [(0, 0), (0, 0), (1, 1)])
    nx, ny, nz = padded.shape

    def at(dx, dy, dz):
        return padded[1 + dx : nx - 1 + dx, 1 + dy : ny - 1 + dy, 1 + dz : nz - 1 + dz]

    beside = at(1, 0, 0) + at(-1, 0, 0)
    beside = beside + at(0, 1, 0) + at(0, -1, 0)
    return beside + at(0, 0, 1) + at(0, 0, -1)


def solve_pressure(wide_velocity, velocity):
    half_width = 6.0
    u = wide_velocity
    divergence = 0.5 * (u[0, 2:, 1:-1, 1:-1] - u[0, :-2, 1:-1, 1:-1])
    divergence = divergence + 0.5 * (u[1, 1:-1, 2:, 1:-1] - u[1, 1:-1, :-2, 1:-1])
    divergence = divergence + 0.5 * (u[2, 1:-1, 1:-1, 2:] - u[2, 1:-1, 1:-1, :-2])
    basis = [axial_valid(divergence, ITERS)]
    for j in range(ITERS):
        scaled = neighbour_sum_wide(basis[j]) * (-1.0 / half_width)
        if j == 0:
            fresh = scaled
        else:
            fresh = 2.0 * scaled - crop(basis[j - 1], 2)
        basis.append(axial_valid(fresh, ITERS - 1 - j))
    interior = [crop(basis[j], ITERS - j) for j in range(ITERS + 1)]
    coefficients, fastest = pressure_coefficients(
        velocity, interior, 6.0 + SHIFT_PRESSURE, half_width
    )
    padded_basis = [radial_pad(crop(basis[j], ITERS - j - 1), 1, "constant") for j in range(ITERS)]
    padded_pressure = coefficients[0] * padded_basis[0]
    for j in range(1, ITERS):
        padded_pressure = padded_pressure + coefficients[j] * padded_basis[j]
    return padded_pressure, fastest


def along_axial(buffer, step_by):
    return shifted_2(buffer, "axial", step_by)


def along_azim(buffer, step_by):
    return shifted_3(buffer, "azim", step_by)


def on_device(state, diff_coef, parcel_state, parcel_cell, parcel_dest, live_count):
    velocity = state[1:4]
    whole_pad = extended(state, (("axial", 1), ("azim", 2)), 2)
    whole_pad = radial_pad(clear_ends(whole_pad, 2, 1), 2, "edge")
    moving = whole_pad[1:]
    density_pad = whole_pad[0]
    density_rim = 2
    vel_pad = moving[0:3]
    wide_velocity = extended(velocity, (("axial", 1), ("azim", 2)), ITERS + 1)
    wide_velocity = radial_pad(clear_ends(wide_velocity, ITERS + 1, 1), 1, "edge")
    padded_pressure, fastest = solve_pressure(wide_velocity, velocity)
    step_size = CFL / (fastest + 1e-06)
    transported = transport(
        moving[3:], vel_pad, density_pad, density_rim, diff_coef[:, None, None, None], step_size
    )
    npar_local = parcel_cell.shape[0]
    cells_x, cells_y, cells_z = (state.shape[1], state.shape[2], state.shape[3])
    plane_count = cells_x * cells_y
    gas_table = jnp.transpose(state[1:6].reshape(5, plane_count, cells_z), (1, 0, 2)).reshape(
        plane_count, 5 * cells_z
    )
    live_now = live_count[0]
    alive_mask = (jnp.arange(npar_local) < live_now).astype(jnp.float32)
    plane_ids = parcel_cell // cells_z
    radial_ids = parcel_cell % cells_z
    plane_hot = (plane_ids[:, None] == jnp.arange(plane_count)[None, :]).astype(jnp.float32)
    radial_hot = (radial_ids[:, None] == jnp.arange(cells_z)[None, :]).astype(jnp.float32)
    gas_rows = jnp.dot(plane_hot, gas_table, precision=HIGHEST).reshape(npar_local, 5, cells_z)
    gas_values = jnp.sum(gas_rows * radial_hot[:, None, :], axis=2).T
    updated, sources = evaporate(parcel_state, gas_values, alive_mask, step_size)
    spread = (sources.T[:, :, None] * radial_hot[:, None, :]).reshape(npar_local, 2 * cells_z)
    deposit = lax.dot_general(plane_hot, spread, (((0,), (0,)), ((), ())), precision=HIGHEST)
    deposit = jnp.transpose(deposit.reshape(cells_x, cells_y, 2, cells_z), (2, 0, 1, 3))
    scalars_new = jnp.concatenate(
        [transported[:2] + deposit / state[0][None], transported[2:]], axis=0
    )
    slot_alive = jnp.arange(npar_local) < live_now
    stacked = jnp.stack([(parcel_dest == d + 1) & slot_alive for d in range(4)]).astype(jnp.int32)
    ranks = jnp.cumsum(stacked, axis=1) - 1
    mover = jnp.sum(stacked, axis=0) > 0
    target = jnp.where(mover, jnp.sum(stacked * (jnp.arange(4)[:, None] * CAP + ranks), axis=0), -1)
    select = (target[:, None] == jnp.arange(4 * CAP)[None, :]).astype(jnp.float32)
    buffers = jnp.transpose(
        jnp.dot(updated, select, precision=HIGHEST).reshape(updated.shape[0], 4, CAP), (1, 0, 2)
    )
    arrived = jnp.stack(
        [
            along_axial(buffers[0], -1),
            along_axial(buffers[1], 1),
            along_azim(buffers[2], -1),
            along_azim(buffers[3], 1),
        ]
    )
    kept_parcels = jnp.where((parcel_dest == 0)[None], updated, jnp.float32(0.0))
    velocity_new = jnp.stack(
        [
            velocity[d]
            - 0.5 * (shifted(padded_pressure, 1, d, 1) - shifted(padded_pressure, 1, d, -1))
            for d in range(3)
        ]
    )
    return (scalars_new, velocity_new, kept_parcels, arrived)


def solution(mesh):
    in_specs = (
        P(None, "axial", "azim", None),
        P(),
        P(None, ("axial", "azim")),
        P(("axial", "azim")),
        P(("axial", "azim")),
        P(("axial", "azim")),
    )
    out_specs = (
        P(None, "axial", "azim", None),
        P(None, "axial", "azim", None),
        P(None, ("axial", "azim")),
        P(None, None, ("axial", "azim")),
    )
    return jax.shard_map(
        on_device, mesh=mesh, in_specs=in_specs, out_specs=out_specs, check_vma=False
    )
```

```python
import jax
import jax.numpy as jnp
from jax import lax
from jax.sharding import PartitionSpec as P
from jax.experimental import pallas as pl
from jax.experimental.pallas import tpu as pltpu

CAP = 64
ITERS = 4


CFL = 0.4
SHIFT_PRESSURE = 0.25
EVAP = 8.0
RELAX = 4.0
DRAG = 6.0
LATENT = 0.5
HEAT_CAP = 0.8
HIGHEST = lax.Precision.HIGHEST


def extended(block, sides, width):
    for axis, dim in sides:
        count = lax.axis_size(axis)
        forward = [(i, i + 1) for i in range(count - 1)]
        forward.append((count - 1, 0))
        backward = [(target, source) for source, target in forward]
        low = lax.ppermute(
            lax.slice_in_dim(block, block.shape[dim] - width, None, axis=dim), axis, forward
        )
        high = lax.ppermute(lax.slice_in_dim(block, 0, width, axis=dim), axis, backward)
        block = jnp.concatenate([low, block, high], axis=dim)
    return block


def extended_pair(first, first_width, second, second_width):
    blocks = [first, second]
    widths = [first_width, second_width]
    for axis, dim in (("axial", 1), ("azim", 2)):
        count = lax.axis_size(axis)
        forward = [(i, (i + 1) % count) for i in range(count)]
        backward = [(target, source) for source, target in forward]
        lows = [
            lax.slice_in_dim(b, b.shape[dim] - w, None, axis=dim) for b, w in zip(blocks, widths)
        ]
        highs = [lax.slice_in_dim(b, 0, w, axis=dim) for b, w in zip(blocks, widths)]
        sizes = [piece.size for piece in lows]

        def pack(pieces):
            return jnp.concatenate([p.reshape(-1, p.shape[-1]) for p in pieces], axis=0)

        def unpack(packed, like):
            rows = [s // like[0].shape[-1] for s in sizes]
            return [
                packed[sum(rows[:k]) : sum(rows[: k + 1])].reshape(like[k].shape)
                for k in range(len(like))
            ]

        got_low = unpack(lax.ppermute(pack(lows), axis, forward), lows)
        got_high = unpack(lax.ppermute(pack(highs), axis, backward), highs)
        blocks = [
            jnp.concatenate([lo, b, hi], axis=dim) for lo, b, hi in zip(got_low, blocks, got_high)
        ]
    return blocks


def shifted_2(shard, axis, by):
    length = lax.axis_size(axis)
    pairs = [(i, i + by) for i in range(length) if 0 <= i + by < length]
    return lax.ppermute(shard, axis, pairs)


def shifted_3(shard, axis, by):
    length = lax.axis_size(axis)
    return lax.ppermute(shard, axis, [(i, (i + by) % length) for i in range(length)])


def shifted(padded, rim_width, direction, step_by):
    selector = []
    total_dims = padded.ndim
    for dim_index in range(total_dims):
        extent = padded.shape[dim_index]
        if dim_index == total_dims - 3 + direction:
            selector.append(slice(rim_width + step_by, extent - rim_width + step_by))
        elif dim_index >= total_dims - 3:
            selector.append(slice(rim_width, extent - rim_width))
        else:
            selector.append(slice(None))
    return padded[tuple(selector)]


def clear_ends(padded, rim_width, axial_dim):
    extent = padded.shape[axial_dim]
    at_first = lax.axis_index("axial") == 0
    at_last = lax.axis_index("axial") == lax.axis_size("axial") - 1
    shape_list = [1] * padded.ndim
    shape_list[axial_dim] = extent
    position = lax.broadcasted_iota(jnp.int32, tuple(shape_list), axial_dim)
    dropped = at_first & (position < rim_width) | at_last & (position >= extent - rim_width)
    return jnp.where(dropped, jnp.float32(0.0), padded)


def radial_pad(values, rim_width, radial_mode):
    return jnp.pad(
        values, [(0, 0)] * (values.ndim - 1) + [(rim_width, rim_width)], mode=radial_mode
    )


def transport(scalar_pad, vel_pad, density_pad, density_rim, diffusion, step_size):
    center = shifted(scalar_pad, 2, 0, 0)
    density = shifted(density_pad, density_rim, 0, 0)
    change = jnp.zeros_like(center)
    for direction in range(3):
        carried = vel_pad[direction] * scalar_pad
        advect = (
            -shifted(carried, 2, direction, 2)
            + 8.0 * shifted(carried, 2, direction, 1)
            - 8.0 * shifted(carried, 2, direction, -1)
            + shifted(carried, 2, direction, -2)
        ) / 12.0
        upper_flux = (
            0.5
            * diffusion
            * (density + shifted(density_pad, density_rim, direction, 1))
            * (shifted(scalar_pad, 2, direction, 1) - center)
        )
        lower_flux = (
            0.5
            * diffusion
            * (density + shifted(density_pad, density_rim, direction, -1))
            * (center - shifted(scalar_pad, 2, direction, -1))
        )
        change = change - advect + upper_flux - lower_flux
    return center + step_size * change


def evaporate(attrs, gas_values, alive_mask, step_size):
    parcel_mass = attrs[0]
    parcel_temp = attrs[1]
    parcel_vel = attrs[2:5]
    offsets = attrs[5:8]
    gas_heat = gas_values[3]
    gas_fuel = gas_values[4]
    evap_rate = EVAP * jax.nn.softplus(gas_heat - parcel_temp) * (1.0 - gas_fuel)
    new_mass = parcel_mass * jnp.exp(-step_size * evap_rate)
    lost_mass = parcel_mass - new_mass
    new_temp = parcel_temp + step_size * RELAX * (gas_heat - parcel_temp)
    new_vel = parcel_vel + step_size * DRAG * (gas_values[0:3] - parcel_vel)
    new_offsets = offsets + step_size * new_vel
    heat_source = -LATENT * lost_mass - HEAT_CAP * new_mass * (new_temp - parcel_temp)
    new_attrs = (
        jnp.concatenate([new_mass[None], new_temp[None], new_vel, new_offsets], axis=0)
        * alive_mask[None]
    )
    sources = jnp.stack([heat_source * alive_mask, lost_mass * alive_mask])
    return (new_attrs, sources)


def pressure_pad(values):
    padded = extended(values, (("axial", 0), ("azim", 1)), 1)
    return radial_pad(clear_ends(padded, 1, 0), 1, "constant")


def operate(values):
    padded = pressure_pad(values)
    beside = shifted(padded, 1, 0, 1) + shifted(padded, 1, 0, -1)
    beside = beside + shifted(padded, 1, 1, 1) + shifted(padded, 1, 1, -1)
    beside = beside + shifted(padded, 1, 2, 1) + shifted(padded, 1, 2, -1)
    return (6.0 + SHIFT_PRESSURE) * values - beside


def reduce_groups():
    axial = lax.axis_size("axial")
    along_x = 4 if axial % 4 == 0 else 1
    groups = [("azim", 1, lax.axis_size("azim")), ("axial", 1, along_x), ("axial", along_x, axial // along_x)]
    return [group for group in groups if group[2] > 1]


def coefficient_cg(gram, size, shift, half_width):
    def apply_a(c):
        out = [shift * c[j] for j in range(size)]
        for j in range(size - 1):
            if j == 0:
                out[1] = out[1] + half_width * c[0]
            else:
                out[j + 1] = out[j + 1] + 0.5 * half_width * c[j]
                out[j - 1] = out[j - 1] + 0.5 * half_width * c[j]
        return out

    def inner(a, b):
        acc = None
        for i in range(size):
            for j in range(size):
                if isinstance(a[i], float) and a[i] == 0.0:
                    continue
                if isinstance(b[j], float) and b[j] == 0.0:
                    continue
                term = a[i] * gram[i][j] * b[j]
                acc = term if acc is None else acc + term
        return acc

    solution_c = [0.0] * size
    residual = [1.0] + [0.0] * (size - 1)
    search = list(residual)
    norm_now = inner(residual, residual)
    for iteration in range(ITERS):
        image = apply_a(search)
        alpha = norm_now / inner(search, image)
        solution_c = [solution_c[j] + alpha * search[j] for j in range(size)]
        residual = [residual[j] - alpha * image[j] for j in range(size)]
        if iteration == ITERS - 1:
            break
        norm_next = inner(residual, residual)
        search = [residual[j] + norm_next / norm_now * search[j] for j in range(size)]
        norm_now = norm_next
    return solution_c


def reduce_kernel(groups, shift, half_width, vel_ref, *refs):
    size = ITERS + 1
    basis_refs = refs[:size]
    o_ref, slots, send_sems, recv_sems = refs[size:]
    here = {"axial": lax.axis_index("axial"), "azim": lax.axis_index("azim")}

    def member(axis, stride, count, m):
        index = here[axis]
        base = index - ((index // stride) % count) * stride
        coords = dict(here)
        coords[axis] = base + m * stride
        return (coords["axial"], coords["azim"])

    def position(axis, stride, count):
        return (here[axis] // stride) % count

    barrier = pltpu.get_barrier_semaphore()
    greeted = 0
    for axis, stride, count in groups:
        mine = position(axis, stride, count)
        for m in range(1, count):
            pl.semaphore_signal(
                barrier,
                inc=1,
                device_id=member(axis, stride, count, (mine + m) % count),
                device_id_type=pl.DeviceIdType.MESH,
            )
            greeted += 1
    pl.semaphore_wait(barrier, greeted)
    row = lax.broadcasted_iota(jnp.int32, o_ref.shape, 0)
    lane = lax.broadcasted_iota(jnp.int32, o_ref.shape, 1)
    is_max = (row == 0) & (lane == 0)

    def total(x):
        return jnp.sum(jnp.sum(x, axis=0, keepdims=True), axis=1, keepdims=True)

    basis = [ref[...] for ref in basis_refs]
    pairs = [(i, j) for i in range(size) for j in range(i, size)]
    entries = [jnp.max(jnp.max(jnp.abs(vel_ref[...]), axis=0, keepdims=True), axis=1, keepdims=True)]
    entries += [total(basis[i] * basis[j]) for i, j in pairs]
    acc = jnp.zeros(o_ref.shape, jnp.float32)
    for n, entry in enumerate(entries):
        acc = jnp.where((row == 0) & (lane == n), entry, acc)
    offset = 0
    for axis, stride, count in groups:
        mine = position(axis, stride, count)
        slots[offset + mine] = acc
        copies = []
        for m in range(1, count):
            target = (mine + m) % count
            copy = pltpu.make_async_remote_copy(
                src_ref=slots.at[offset + mine],
                dst_ref=slots.at[offset + mine],
                send_sem=send_sems.at[offset + target],
                recv_sem=recv_sems.at[offset + mine],
                device_id=member(axis, stride, count, target),
                device_id_type=pl.DeviceIdType.MESH,
            )
            copy.start()
            copies.append(copy)
        for copy in copies:
            copy.wait_send()
        for m in range(count):
            incoming = pltpu.make_async_remote_copy(
                src_ref=slots.at[offset + m],
                dst_ref=slots.at[offset + m],
                send_sem=send_sems.at[offset + m],
                recv_sem=recv_sems.at[offset + m],
                device_id=member(axis, stride, count, m),
                device_id_type=pl.DeviceIdType.MESH,
            )

            @pl.when(m != mine)
            def _():
                incoming.wait_recv()

        combined = slots[offset]
        for m in range(1, count):
            other = slots[offset + m]
            combined = jnp.where(is_max, jnp.maximum(combined, other), combined + other)
        acc = combined
        offset += count
    first = acc[0:1, :]
    first_lane = lax.broadcasted_iota(jnp.int32, first.shape, 1)

    def entry_at(n):
        return jnp.sum(jnp.where(first_lane == n, first, 0.0), axis=1, keepdims=True)

    gram = [[None] * size for _ in range(size)]
    for n, (i, j) in enumerate(pairs):
        gram[i][j] = entry_at(n + 1)
        gram[j][i] = gram[i][j]
    coefficients = coefficient_cg(gram, size, shift, half_width)
    out = jnp.where(lane == ITERS, entry_at(0), 0.0)
    for j in range(ITERS):
        out = jnp.where((lane == j), coefficients[j], out)
    o_ref[...] = out


def pressure_coefficients(velocity, basis, shift, half_width):
    groups = reduce_groups()
    slot_count = sum(count for _, _, count in groups)
    flat = [v.reshape(-1, v.shape[-1]) for v in basis]
    out = pl.pallas_call(
        lambda *refs: reduce_kernel(groups, shift, half_width, *refs),
        out_shape=jax.ShapeDtypeStruct((8, 128), jnp.float32),
        in_specs=[pl.BlockSpec(memory_space=pltpu.VMEM)] * (1 + len(flat)),
        out_specs=pl.BlockSpec(memory_space=pltpu.VMEM),
        scratch_shapes=[
            pltpu.VMEM((slot_count, 8, 128), jnp.float32),
            pltpu.SemaphoreType.DMA((slot_count,)),
            pltpu.SemaphoreType.DMA((slot_count,)),
        ],
        compiler_params=pltpu.CompilerParams(collective_id=0, has_side_effects=True),
    )(velocity.reshape(-1, velocity.shape[-1]), *flat)
    return [out[0, j] for j in range(ITERS)], out[0, ITERS]


def neighbour_sum(padded):
    beside = shifted(padded, 1, 0, 1) + shifted(padded, 1, 0, -1)
    beside = beside + shifted(padded, 1, 1, 1) + shifted(padded, 1, 1, -1)
    return beside + shifted(padded, 1, 2, 1) + shifted(padded, 1, 2, -1)


def axial_valid(values, rim):
    extent = values.shape[0]
    inner_x = extent - 2 * rim
    first = lax.axis_index("axial") * inner_x - rim
    position = first + lax.broadcasted_iota(jnp.int32, (extent, 1, 1), 0)
    inside = (position >= 0) & (position < inner_x * lax.axis_size("axial"))
    return jnp.where(inside, values, jnp.float32(0.0))


def crop(values, by):
    if by == 0:
        return values
    return values[by:-by, by:-by]


def neighbour_sum_wide(values):
    padded = jnp.pad(values, [(0, 0), (0, 0), (1, 1)])
    nx, ny, nz = padded.shape

    def at(dx, dy, dz):
        return padded[1 + dx : nx - 1 + dx, 1 + dy : ny - 1 + dy, 1 + dz : nz - 1 + dz]

    beside = at(1, 0, 0) + at(-1, 0, 0)
    beside = beside + at(0, 1, 0) + at(0, -1, 0)
    return beside + at(0, 0, 1) + at(0, 0, -1)


def solve_pressure(wide_velocity, velocity):
    half_width = 6.0
    u = wide_velocity
    divergence = 0.5 * (u[0, 2:, 1:-1, 1:-1] - u[0, :-2, 1:-1, 1:-1])
    divergence = divergence + 0.5 * (u[1, 1:-1, 2:, 1:-1] - u[1, 1:-1, :-2, 1:-1])
    divergence = divergence + 0.5 * (u[2, 1:-1, 1:-1, 2:] - u[2, 1:-1, 1:-1, :-2])
    basis = [axial_valid(divergence, ITERS)]
    for j in range(ITERS):
        scaled = neighbour_sum_wide(basis[j]) * (-1.0 / half_width)
        if j == 0:
            fresh = scaled
        else:
            fresh = 2.0 * scaled - crop(basis[j - 1], 2)
        basis.append(axial_valid(fresh, ITERS - 1 - j))
    interior = [crop(basis[j], ITERS - j) for j in range(ITERS + 1)]
    coefficients, fastest = pressure_coefficients(
        velocity, interior, 6.0 + SHIFT_PRESSURE, half_width
    )
    padded_basis = [radial_pad(crop(basis[j], ITERS - j - 1), 1, "constant") for j in range(ITERS)]
    padded_pressure = coefficients[0] * padded_basis[0]
    for j in range(1, ITERS):
        padded_pressure = padded_pressure + coefficients[j] * padded_basis[j]
    return padded_pressure, fastest


def along_axial(buffer, step_by):
    return shifted_2(buffer, "axial", step_by)


def along_azim(buffer, step_by):
    return shifted_3(buffer, "azim", step_by)


def on_device(state, diff_coef, parcel_state, parcel_cell, parcel_dest, live_count):
    velocity = state[1:4]
    whole_pad, wide_velocity = extended_pair(state, 2, velocity, ITERS + 1)
    whole_pad = radial_pad(clear_ends(whole_pad, 2, 1), 2, "edge")
    moving = whole_pad[1:]
    density_pad = whole_pad[0]
    density_rim = 2
    vel_pad = moving[0:3]
    wide_velocity = radial_pad(clear_ends(wide_velocity, ITERS + 1, 1), 1, "edge")
    padded_pressure, fastest = solve_pressure(wide_velocity, velocity)
    step_size = CFL / (fastest + 1e-06)
    transported = transport(
        moving[3:], vel_pad, density_pad, density_rim, diff_coef[:, None, None, None], step_size
    )
    npar_local = parcel_cell.shape[0]
    cells_x, cells_y, cells_z = (state.shape[1], state.shape[2], state.shape[3])
    plane_count = cells_x * cells_y
    gas_table = jnp.transpose(state[1:6].reshape(5, plane_count, cells_z), (1, 0, 2)).reshape(
        plane_count, 5 * cells_z
    )
    live_now = live_count[0]
    alive_mask = (jnp.arange(npar_local) < live_now).astype(jnp.float32)
    plane_ids = parcel_cell // cells_z
    radial_ids = parcel_cell % cells_z
    plane_hot = (plane_ids[:, None] == jnp.arange(plane_count)[None, :]).astype(jnp.float32)
    radial_hot = (radial_ids[:, None] == jnp.arange(cells_z)[None, :]).astype(jnp.float32)
    gas_rows = jnp.dot(plane_hot, gas_table, precision=HIGHEST).reshape(npar_local, 5, cells_z)
    gas_values = jnp.sum(gas_rows * radial_hot[:, None, :], axis=2).T
    updated, sources = evaporate(parcel_state, gas_values, alive_mask, step_size)
    spread = (sources.T[:, :, None] * radial_hot[:, None, :]).reshape(npar_local, 2 * cells_z)
    deposit = lax.dot_general(plane_hot, spread, (((0,), (0,)), ((), ())), precision=HIGHEST)
    deposit = jnp.transpose(deposit.reshape(cells_x, cells_y, 2, cells_z), (2, 0, 1, 3))
    scalars_new = jnp.concatenate(
        [transported[:2] + deposit / state[0][None], transported[2:]], axis=0
    )
    slot_alive = jnp.arange(npar_local) < live_now
    stacked = jnp.stack([(parcel_dest == d + 1) & slot_alive for d in range(4)]).astype(jnp.int32)
    ranks = jnp.cumsum(stacked, axis=1) - 1
    mover = jnp.sum(stacked, axis=0) > 0
    target = jnp.where(mover, jnp.sum(stacked * (jnp.arange(4)[:, None] * CAP + ranks), axis=0), -1)
    select = (target[:, None] == jnp.arange(4 * CAP)[None, :]).astype(jnp.float32)
    buffers = jnp.transpose(
        jnp.dot(updated, select, precision=HIGHEST).reshape(updated.shape[0], 4, CAP), (1, 0, 2)
    )
    arrived = jnp.stack(
        [
            along_axial(buffers[0], -1),
            along_axial(buffers[1], 1),
            along_azim(buffers[2], -1),
            along_azim(buffers[3], 1),
        ]
    )
    kept_parcels = jnp.where((parcel_dest == 0)[None], updated, jnp.float32(0.0))
    velocity_new = jnp.stack(
        [
            velocity[d]
            - 0.5 * (shifted(padded_pressure, 1, d, 1) - shifted(padded_pressure, 1, d, -1))
            for d in range(3)
        ]
    )
    return (scalars_new, velocity_new, kept_parcels, arrived)


def solution(mesh):
    in_specs = (
        P(None, "axial", "azim", None),
        P(),
        P(None, ("axial", "azim")),
        P(("axial", "azim")),
        P(("axial", "azim")),
        P(("axial", "azim")),
    )
    out_specs = (
        P(None, "axial", "azim", None),
        P(None, "axial", "azim", None),
        P(None, ("axial", "azim")),
        P(None, None, ("axial", "azim")),
    )
    return jax.shard_map(
        on_device, mesh=mesh, in_specs=in_specs, out_specs=out_specs, check_vma=False
    )
```

```python
import jax
import jax.numpy as jnp
from jax import lax
from jax.sharding import PartitionSpec as P
from jax.experimental import pallas as pl
from jax.experimental.pallas import tpu as pltpu

CAP = 64
ITERS = 4


CFL = 0.4
SHIFT_PRESSURE = 0.25
EVAP = 8.0
RELAX = 4.0
DRAG = 6.0
LATENT = 0.5
HEAT_CAP = 0.8
HIGHEST = lax.Precision.HIGHEST


def extended(block, sides, width):
    for axis, dim in sides:
        count = lax.axis_size(axis)
        forward = [(i, i + 1) for i in range(count - 1)]
        forward.append((count - 1, 0))
        backward = [(target, source) for source, target in forward]
        low = lax.ppermute(
            lax.slice_in_dim(block, block.shape[dim] - width, None, axis=dim), axis, forward
        )
        high = lax.ppermute(lax.slice_in_dim(block, 0, width, axis=dim), axis, backward)
        block = jnp.concatenate([low, block, high], axis=dim)
    return block


def exchange_kernel(offsets, *refs):
    count = len(offsets)
    sources = refs[:count]
    outs = refs[count : 2 * count]
    landing = refs[2 * count : 3 * count]
    send_sems, recv_sems = refs[3 * count :]
    axial = lax.axis_index("axial")
    azim = lax.axis_index("azim")

    def device(step_axial, step_azim):
        return (
            (axial + step_axial + lax.axis_size("axial")) % lax.axis_size("axial"),
            (azim + step_azim + lax.axis_size("azim")) % lax.axis_size("azim"),
        )

    neighbours = sorted(set(offsets))
    barrier = pltpu.get_barrier_semaphore()
    for step in neighbours:
        pl.semaphore_signal(
            barrier, inc=1, device_id=device(*step), device_id_type=pl.DeviceIdType.MESH
        )
    pl.semaphore_wait(barrier, len(neighbours))
    copies = []
    for k, step in enumerate(offsets):
        copy = pltpu.make_async_remote_copy(
            src_ref=sources[k],
            dst_ref=landing[k],
            send_sem=send_sems.at[k],
            recv_sem=recv_sems.at[k],
            device_id=device(*step),
            device_id_type=pl.DeviceIdType.MESH,
        )
        copy.start()
        copies.append(copy)
    for k, copy in enumerate(copies):
        copy.wait()
        outs[k][...] = landing[k][...]


def neighbour_exchange(items):
    offsets = [step for _, step in items]
    flat = [a.reshape(-1, a.shape[-1]) for a, _ in items]
    count = len(flat)
    outs = pl.pallas_call(
        lambda *refs: exchange_kernel(offsets, *refs),
        out_shape=[jax.ShapeDtypeStruct(f.shape, f.dtype) for f in flat],
        in_specs=[pl.BlockSpec(memory_space=pltpu.VMEM)] * count,
        out_specs=[pl.BlockSpec(memory_space=pltpu.VMEM)] * count,
        scratch_shapes=[pltpu.VMEM(f.shape, f.dtype) for f in flat]
        + [pltpu.SemaphoreType.DMA((count,)), pltpu.SemaphoreType.DMA((count,))],
        compiler_params=pltpu.CompilerParams(collective_id=1, has_side_effects=True),
    )(*flat)
    return [o.reshape(a.shape) for o, (a, _) in zip(outs, items)]


def rim_slab(block, width, step_axial, step_azim):
    def pick(values, dim, step):
        if step > 0:
            return lax.slice_in_dim(values, values.shape[dim] - width, None, axis=dim)
        if step < 0:
            return lax.slice_in_dim(values, 0, width, axis=dim)
        return values

    return pick(pick(block, 1, step_axial), 2, step_azim)


NEIGHBOURS = [(sa, sz) for sa in (-1, 0, 1) for sz in (-1, 0, 1) if (sa, sz) != (0, 0)]


def assemble(block, received):
    bands = []
    for pz in (-1, 0, 1):
        row = [block if (pa, pz) == (0, 0) else received[(pa, pz)] for pa in (-1, 0, 1)]
        bands.append(jnp.concatenate(row, axis=1))
    return jnp.concatenate(bands, axis=2)


def shifted_2(shard, axis, by):
    length = lax.axis_size(axis)
    pairs = [(i, i + by) for i in range(length) if 0 <= i + by < length]
    return lax.ppermute(shard, axis, pairs)


def shifted_3(shard, axis, by):
    length = lax.axis_size(axis)
    return lax.ppermute(shard, axis, [(i, (i + by) % length) for i in range(length)])


def shifted(padded, rim_width, direction, step_by):
    selector = []
    total_dims = padded.ndim
    for dim_index in range(total_dims):
        extent = padded.shape[dim_index]
        if dim_index == total_dims - 3 + direction:
            selector.append(slice(rim_width + step_by, extent - rim_width + step_by))
        elif dim_index >= total_dims - 3:
            selector.append(slice(rim_width, extent - rim_width))
        else:
            selector.append(slice(None))
    return padded[tuple(selector)]


def clear_ends(padded, rim_width, axial_dim):
    extent = padded.shape[axial_dim]
    at_first = lax.axis_index("axial") == 0
    at_last = lax.axis_index("axial") == lax.axis_size("axial") - 1
    shape_list = [1] * padded.ndim
    shape_list[axial_dim] = extent
    position = lax.broadcasted_iota(jnp.int32, tuple(shape_list), axial_dim)
    dropped = at_first & (position < rim_width) | at_last & (position >= extent - rim_width)
    return jnp.where(dropped, jnp.float32(0.0), padded)


def radial_pad(values, rim_width, radial_mode):
    return jnp.pad(
        values, [(0, 0)] * (values.ndim - 1) + [(rim_width, rim_width)], mode=radial_mode
    )


def transport(scalar_pad, vel_pad, density_pad, density_rim, diffusion, step_size):
    center = shifted(scalar_pad, 2, 0, 0)
    density = shifted(density_pad, density_rim, 0, 0)
    change = jnp.zeros_like(center)
    for direction in range(3):
        carried = vel_pad[direction] * scalar_pad
        advect = (
            -shifted(carried, 2, direction, 2)
            + 8.0 * shifted(carried, 2, direction, 1)
            - 8.0 * shifted(carried, 2, direction, -1)
            + shifted(carried, 2, direction, -2)
        ) / 12.0
        upper_flux = (
            0.5
            * diffusion
            * (density + shifted(density_pad, density_rim, direction, 1))
            * (shifted(scalar_pad, 2, direction, 1) - center)
        )
        lower_flux = (
            0.5
            * diffusion
            * (density + shifted(density_pad, density_rim, direction, -1))
            * (center - shifted(scalar_pad, 2, direction, -1))
        )
        change = change - advect + upper_flux - lower_flux
    return center + step_size * change


def evaporate(attrs, gas_values, alive_mask, step_size):
    parcel_mass = attrs[0]
    parcel_temp = attrs[1]
    parcel_vel = attrs[2:5]
    offsets = attrs[5:8]
    gas_heat = gas_values[3]
    gas_fuel = gas_values[4]
    evap_rate = EVAP * jax.nn.softplus(gas_heat - parcel_temp) * (1.0 - gas_fuel)
    new_mass = parcel_mass * jnp.exp(-step_size * evap_rate)
    lost_mass = parcel_mass - new_mass
    new_temp = parcel_temp + step_size * RELAX * (gas_heat - parcel_temp)
    new_vel = parcel_vel + step_size * DRAG * (gas_values[0:3] - parcel_vel)
    new_offsets = offsets + step_size * new_vel
    heat_source = -LATENT * lost_mass - HEAT_CAP * new_mass * (new_temp - parcel_temp)
    new_attrs = (
        jnp.concatenate([new_mass[None], new_temp[None], new_vel, new_offsets], axis=0)
        * alive_mask[None]
    )
    sources = jnp.stack([heat_source * alive_mask, lost_mass * alive_mask])
    return (new_attrs, sources)


def pressure_pad(values):
    padded = extended(values, (("axial", 0), ("azim", 1)), 1)
    return radial_pad(clear_ends(padded, 1, 0), 1, "constant")


def operate(values):
    padded = pressure_pad(values)
    beside = shifted(padded, 1, 0, 1) + shifted(padded, 1, 0, -1)
    beside = beside + shifted(padded, 1, 1, 1) + shifted(padded, 1, 1, -1)
    beside = beside + shifted(padded, 1, 2, 1) + shifted(padded, 1, 2, -1)
    return (6.0 + SHIFT_PRESSURE) * values - beside


def reduce_groups():
    axial = lax.axis_size("axial")
    along_x = 4 if axial % 4 == 0 else 1
    groups = [("azim", 1, lax.axis_size("azim")), ("axial", 1, along_x), ("axial", along_x, axial // along_x)]
    return [group for group in groups if group[2] > 1]


def coefficient_cg(gram, size, shift, half_width):
    def apply_a(c):
        out = [shift * c[j] for j in range(size)]
        for j in range(size - 1):
            if j == 0:
                out[1] = out[1] + half_width * c[0]
            else:
                out[j + 1] = out[j + 1] + 0.5 * half_width * c[j]
                out[j - 1] = out[j - 1] + 0.5 * half_width * c[j]
        return out

    def inner(a, b):
        acc = None
        for i in range(size):
            for j in range(size):
                if isinstance(a[i], float) and a[i] == 0.0:
                    continue
                if isinstance(b[j], float) and b[j] == 0.0:
                    continue
                term = a[i] * gram[i][j] * b[j]
                acc = term if acc is None else acc + term
        return acc

    solution_c = [0.0] * size
    residual = [1.0] + [0.0] * (size - 1)
    search = list(residual)
    norm_now = inner(residual, residual)
    for iteration in range(ITERS):
        image = apply_a(search)
        alpha = norm_now / inner(search, image)
        solution_c = [solution_c[j] + alpha * search[j] for j in range(size)]
        residual = [residual[j] - alpha * image[j] for j in range(size)]
        if iteration == ITERS - 1:
            break
        norm_next = inner(residual, residual)
        search = [residual[j] + norm_next / norm_now * search[j] for j in range(size)]
        norm_now = norm_next
    return solution_c


def reduce_kernel(groups, shift, half_width, vel_ref, *refs):
    size = ITERS + 1
    basis_refs = refs[:size]
    o_ref, slots, send_sems, recv_sems = refs[size:]
    here = {"axial": lax.axis_index("axial"), "azim": lax.axis_index("azim")}

    def member(axis, stride, count, m):
        index = here[axis]
        base = index - ((index // stride) % count) * stride
        coords = dict(here)
        coords[axis] = base + m * stride
        return (coords["axial"], coords["azim"])

    def position(axis, stride, count):
        return (here[axis] // stride) % count

    barrier = pltpu.get_barrier_semaphore()
    greeted = 0
    for axis, stride, count in groups:
        mine = position(axis, stride, count)
        for m in range(1, count):
            pl.semaphore_signal(
                barrier,
                inc=1,
                device_id=member(axis, stride, count, (mine + m) % count),
                device_id_type=pl.DeviceIdType.MESH,
            )
            greeted += 1
    pl.semaphore_wait(barrier, greeted)
    row = lax.broadcasted_iota(jnp.int32, o_ref.shape, 0)
    lane = lax.broadcasted_iota(jnp.int32, o_ref.shape, 1)
    is_max = (row == 0) & (lane == 0)

    def total(x):
        return jnp.sum(jnp.sum(x, axis=0, keepdims=True), axis=1, keepdims=True)

    basis = [ref[...] for ref in basis_refs]
    pairs = [(i, j) for i in range(size) for j in range(i, size)]
    entries = [jnp.max(jnp.max(jnp.abs(vel_ref[...]), axis=0, keepdims=True), axis=1, keepdims=True)]
    entries += [total(basis[i] * basis[j]) for i, j in pairs]
    acc = jnp.zeros(o_ref.shape, jnp.float32)
    for n, entry in enumerate(entries):
        acc = jnp.where((row == 0) & (lane == n), entry, acc)
    offset = 0
    for axis, stride, count in groups:
        mine = position(axis, stride, count)
        slots[offset + mine] = acc
        copies = []
        for m in range(1, count):
            target = (mine + m) % count
            copy = pltpu.make_async_remote_copy(
                src_ref=slots.at[offset + mine],
                dst_ref=slots.at[offset + mine],
                send_sem=send_sems.at[offset + target],
                recv_sem=recv_sems.at[offset + mine],
                device_id=member(axis, stride, count, target),
                device_id_type=pl.DeviceIdType.MESH,
            )
            copy.start()
            copies.append(copy)
        for copy in copies:
            copy.wait_send()
        for m in range(count):
            incoming = pltpu.make_async_remote_copy(
                src_ref=slots.at[offset + m],
                dst_ref=slots.at[offset + m],
                send_sem=send_sems.at[offset + m],
                recv_sem=recv_sems.at[offset + m],
                device_id=member(axis, stride, count, m),
                device_id_type=pl.DeviceIdType.MESH,
            )

            @pl.when(m != mine)
            def _():
                incoming.wait_recv()

        combined = slots[offset]
        for m in range(1, count):
            other = slots[offset + m]
            combined = jnp.where(is_max, jnp.maximum(combined, other), combined + other)
        acc = combined
        offset += count
    first = acc[0:1, :]
    first_lane = lax.broadcasted_iota(jnp.int32, first.shape, 1)

    def entry_at(n):
        return jnp.sum(jnp.where(first_lane == n, first, 0.0), axis=1, keepdims=True)

    gram = [[None] * size for _ in range(size)]
    for n, (i, j) in enumerate(pairs):
        gram[i][j] = entry_at(n + 1)
        gram[j][i] = gram[i][j]
    coefficients = coefficient_cg(gram, size, shift, half_width)
    out = jnp.where(lane == ITERS, entry_at(0), 0.0)
    for j in range(ITERS):
        out = jnp.where((lane == j), coefficients[j], out)
    o_ref[...] = out


def pressure_coefficients(velocity, basis, shift, half_width):
    groups = reduce_groups()
    slot_count = sum(count for _, _, count in groups)
    flat = [v.reshape(-1, v.shape[-1]) for v in basis]
    out = pl.pallas_call(
        lambda *refs: reduce_kernel(groups, shift, half_width, *refs),
        out_shape=jax.ShapeDtypeStruct((8, 128), jnp.float32),
        in_specs=[pl.BlockSpec(memory_space=pltpu.VMEM)] * (1 + len(flat)),
        out_specs=pl.BlockSpec(memory_space=pltpu.VMEM),
        scratch_shapes=[
            pltpu.VMEM((slot_count, 8, 128), jnp.float32),
            pltpu.SemaphoreType.DMA((slot_count,)),
            pltpu.SemaphoreType.DMA((slot_count,)),
        ],
        compiler_params=pltpu.CompilerParams(collective_id=0, has_side_effects=True),
    )(velocity.reshape(-1, velocity.shape[-1]), *flat)
    return [out[0, j] for j in range(ITERS)], out[0, ITERS]


def neighbour_sum(padded):
    beside = shifted(padded, 1, 0, 1) + shifted(padded, 1, 0, -1)
    beside = beside + shifted(padded, 1, 1, 1) + shifted(padded, 1, 1, -1)
    return beside + shifted(padded, 1, 2, 1) + shifted(padded, 1, 2, -1)


def axial_valid(values, rim):
    extent = values.shape[0]
    inner_x = extent - 2 * rim
    first = lax.axis_index("axial") * inner_x - rim
    position = first + lax.broadcasted_iota(jnp.int32, (extent, 1, 1), 0)
    inside = (position >= 0) & (position < inner_x * lax.axis_size("axial"))
    return jnp.where(inside, values, jnp.float32(0.0))


def crop(values, by):
    if by == 0:
        return values
    return values[by:-by, by:-by]


def neighbour_sum_wide(values):
    padded = jnp.pad(values, [(0, 0), (0, 0), (1, 1)])
    nx, ny, nz = padded.shape

    def at(dx, dy, dz):
        return padded[1 + dx : nx - 1 + dx, 1 + dy : ny - 1 + dy, 1 + dz : nz - 1 + dz]

    beside = at(1, 0, 0) + at(-1, 0, 0)
    beside = beside + at(0, 1, 0) + at(0, -1, 0)
    return beside + at(0, 0, 1) + at(0, 0, -1)


def solve_pressure(wide_velocity, velocity):
    half_width = 6.0
    u = wide_velocity
    divergence = 0.5 * (u[0, 2:, 1:-1, 1:-1] - u[0, :-2, 1:-1, 1:-1])
    divergence = divergence + 0.5 * (u[1, 1:-1, 2:, 1:-1] - u[1, 1:-1, :-2, 1:-1])
    divergence = divergence + 0.5 * (u[2, 1:-1, 1:-1, 2:] - u[2, 1:-1, 1:-1, :-2])
    basis = [axial_valid(divergence, ITERS)]
    for j in range(ITERS):
        scaled = neighbour_sum_wide(basis[j]) * (-1.0 / half_width)
        if j == 0:
            fresh = scaled
        else:
            fresh = 2.0 * scaled - crop(basis[j - 1], 2)
        basis.append(axial_valid(fresh, ITERS - 1 - j))
    interior = [crop(basis[j], ITERS - j) for j in range(ITERS + 1)]
    coefficients, fastest = pressure_coefficients(
        velocity, interior, 6.0 + SHIFT_PRESSURE, half_width
    )
    padded_basis = [radial_pad(crop(basis[j], ITERS - j - 1), 1, "constant") for j in range(ITERS)]
    padded_pressure = coefficients[0] * padded_basis[0]
    for j in range(1, ITERS):
        padded_pressure = padded_pressure + coefficients[j] * padded_basis[j]
    return padded_pressure, fastest


def along_axial(buffer, step_by):
    return shifted_2(buffer, "axial", step_by)


def along_azim(buffer, step_by):
    return shifted_3(buffer, "azim", step_by)


def on_device(state, diff_coef, parcel_state, parcel_cell, parcel_dest, live_count):
    velocity = state[1:4]
    npar_local = parcel_cell.shape[0]
    cells_x, cells_y, cells_z = (state.shape[1], state.shape[2], state.shape[3])
    plane_count = cells_x * cells_y
    gas_table = jnp.transpose(state[1:6].reshape(5, plane_count, cells_z), (1, 0, 2)).reshape(
        plane_count, 5 * cells_z
    )
    live_now = live_count[0]
    slot_alive = jnp.arange(npar_local) < live_now
    alive_mask = slot_alive.astype(jnp.float32)
    plane_ids = parcel_cell // cells_z
    radial_ids = parcel_cell % cells_z
    plane_hot = (plane_ids[:, None] == jnp.arange(plane_count)[None, :]).astype(jnp.float32)
    radial_hot = (radial_ids[:, None] == jnp.arange(cells_z)[None, :]).astype(jnp.float32)
    gas_rows = jnp.dot(plane_hot, gas_table, precision=HIGHEST).reshape(npar_local, 5, cells_z)
    gas_values = jnp.sum(gas_rows * radial_hot[:, None, :], axis=2).T
    stacked = jnp.stack([(parcel_dest == d + 1) & slot_alive for d in range(4)]).astype(jnp.int32)
    ranks = jnp.cumsum(stacked, axis=1) - 1
    mover = jnp.sum(stacked, axis=0) > 0
    target = jnp.where(mover, jnp.sum(stacked * (jnp.arange(4)[:, None] * CAP + ranks), axis=0), -1)
    select = (target[:, None] == jnp.arange(4 * CAP)[None, :]).astype(jnp.float32)
    raw = jnp.concatenate([parcel_state, gas_values, alive_mask[None]], axis=0)
    leaving = jnp.transpose(
        jnp.dot(raw, select, precision=HIGHEST).reshape(raw.shape[0], 4, CAP), (1, 0, 2)
    )
    parcel_steps = [(-1, 0), (1, 0), (0, -1), (0, 1)]
    items = [(rim_slab(state, 2, sa, sz), (sa, sz)) for sa, sz in NEIGHBOURS]
    items += [(rim_slab(velocity, ITERS + 1, sa, sz), (sa, sz)) for sa, sz in NEIGHBOURS]
    items += [(leaving[d], parcel_steps[d]) for d in range(4)]
    got = neighbour_exchange(items)
    count = len(NEIGHBOURS)
    state_rims = {(-sa, -sz): got[k] for k, (sa, sz) in enumerate(NEIGHBOURS)}
    velocity_rims = {(-sa, -sz): got[count + k] for k, (sa, sz) in enumerate(NEIGHBOURS)}
    landed = got[2 * count :]
    whole_pad = assemble(state, state_rims)
    whole_pad = radial_pad(clear_ends(whole_pad, 2, 1), 2, "edge")
    moving = whole_pad[1:]
    density_pad = whole_pad[0]
    density_rim = 2
    vel_pad = moving[0:3]
    wide_velocity = assemble(velocity, velocity_rims)
    wide_velocity = radial_pad(clear_ends(wide_velocity, ITERS + 1, 1), 1, "edge")
    padded_pressure, fastest = solve_pressure(wide_velocity, velocity)
    step_size = CFL / (fastest + 1e-06)
    transported = transport(
        moving[3:], vel_pad, density_pad, density_rim, diff_coef[:, None, None, None], step_size
    )
    updated, sources = evaporate(parcel_state, gas_values, alive_mask, step_size)
    spread = (sources.T[:, :, None] * radial_hot[:, None, :]).reshape(npar_local, 2 * cells_z)
    deposit = lax.dot_general(plane_hot, spread, (((0,), (0,)), ((), ())), precision=HIGHEST)
    deposit = jnp.transpose(deposit.reshape(cells_x, cells_y, 2, cells_z), (2, 0, 1, 3))
    scalars_new = jnp.concatenate(
        [transported[:2] + deposit / state[0][None], transported[2:]], axis=0
    )
    at_first = lax.axis_index("axial") == 0
    at_last = lax.axis_index("axial") == lax.axis_size("axial") - 1
    arriving = []
    for d in range(4):
        payload = landed[d]
        if d == 0:
            payload = jnp.where(at_last, jnp.float32(0.0), payload)
        if d == 1:
            payload = jnp.where(at_first, jnp.float32(0.0), payload)
        moved, _ = evaporate(payload[:8], payload[8:13], payload[13], step_size)
        arriving.append(moved)
    arrived = jnp.stack(arriving)
    kept_parcels = jnp.where((parcel_dest == 0)[None], updated, jnp.float32(0.0))
    velocity_new = jnp.stack(
        [
            velocity[d]
            - 0.5 * (shifted(padded_pressure, 1, d, 1) - shifted(padded_pressure, 1, d, -1))
            for d in range(3)
        ]
    )
    return (scalars_new, velocity_new, kept_parcels, arrived)


def solution(mesh):
    in_specs = (
        P(None, "axial", "azim", None),
        P(),
        P(None, ("axial", "azim")),
        P(("axial", "azim")),
        P(("axial", "azim")),
        P(("axial", "azim")),
    )
    out_specs = (
        P(None, "axial", "azim", None),
        P(None, "axial", "azim", None),
        P(None, ("axial", "azim")),
        P(None, None, ("axial", "azim")),
    )
    return jax.shard_map(
        on_device, mesh=mesh, in_specs=in_specs, out_specs=out_specs, check_vma=False
    )
```

```python
import jax
import jax.numpy as jnp
from jax import lax
from jax.sharding import PartitionSpec as P
from jax.experimental import pallas as pl
from jax.experimental.pallas import tpu as pltpu

CAP = 64
ITERS = 4


CFL = 0.4
SHIFT_PRESSURE = 0.25
EVAP = 8.0
RELAX = 4.0
DRAG = 6.0
LATENT = 0.5
HEAT_CAP = 0.8
HIGHEST = lax.Precision.HIGHEST


def extended(block, sides, width):
    for axis, dim in sides:
        count = lax.axis_size(axis)
        forward = [(i, i + 1) for i in range(count - 1)]
        forward.append((count - 1, 0))
        backward = [(target, source) for source, target in forward]
        low = lax.ppermute(
            lax.slice_in_dim(block, block.shape[dim] - width, None, axis=dim), axis, forward
        )
        high = lax.ppermute(lax.slice_in_dim(block, 0, width, axis=dim), axis, backward)
        block = jnp.concatenate([low, block, high], axis=dim)
    return block


def exchange_kernel(offsets, *refs):
    count = len(offsets)
    sources = refs[:count]
    outs = refs[count : 2 * count]
    landing = refs[2 * count : 3 * count]
    send_sems, recv_sems = refs[3 * count :]
    axial = lax.axis_index("axial")
    azim = lax.axis_index("azim")

    def device(step_axial, step_azim):
        return (
            (axial + step_axial + lax.axis_size("axial")) % lax.axis_size("axial"),
            (azim + step_azim + lax.axis_size("azim")) % lax.axis_size("azim"),
        )

    neighbours = sorted(set(offsets))
    barrier = pltpu.get_barrier_semaphore()
    for step in neighbours:
        pl.semaphore_signal(
            barrier, inc=1, device_id=device(*step), device_id_type=pl.DeviceIdType.MESH
        )
    pl.semaphore_wait(barrier, len(neighbours))
    copies = []
    for k, step in enumerate(offsets):
        copy = pltpu.make_async_remote_copy(
            src_ref=sources[k],
            dst_ref=landing[k],
            send_sem=send_sems.at[k],
            recv_sem=recv_sems.at[k],
            device_id=device(*step),
            device_id_type=pl.DeviceIdType.MESH,
        )
        copy.start()
        copies.append(copy)
    for k, copy in enumerate(copies):
        copy.wait()
        outs[k][...] = landing[k][...]


def neighbour_exchange(items):
    offsets = [step for _, step in items]
    flat = [a.reshape(-1, a.shape[-1]) for a, _ in items]
    count = len(flat)
    outs = pl.pallas_call(
        lambda *refs: exchange_kernel(offsets, *refs),
        out_shape=[jax.ShapeDtypeStruct(f.shape, f.dtype) for f in flat],
        in_specs=[pl.BlockSpec(memory_space=pltpu.VMEM)] * count,
        out_specs=[pl.BlockSpec(memory_space=pltpu.VMEM)] * count,
        scratch_shapes=[pltpu.VMEM(f.shape, f.dtype) for f in flat]
        + [pltpu.SemaphoreType.DMA((count,)), pltpu.SemaphoreType.DMA((count,))],
        compiler_params=pltpu.CompilerParams(collective_id=1, has_side_effects=True),
    )(*flat)
    return [o.reshape(a.shape) for o, (a, _) in zip(outs, items)]


def rim_slab(block, width, step_axial, step_azim):
    def pick(values, dim, step):
        if step > 0:
            return lax.slice_in_dim(values, values.shape[dim] - width, None, axis=dim)
        if step < 0:
            return lax.slice_in_dim(values, 0, width, axis=dim)
        return values

    return pick(pick(block, 1, step_axial), 2, step_azim)


NEIGHBOURS = [(sa, sz) for sa in (-1, 0, 1) for sz in (-1, 0, 1) if (sa, sz) != (0, 0)]


def assemble(block, received):
    bands = []
    for pz in (-1, 0, 1):
        row = [block if (pa, pz) == (0, 0) else received[(pa, pz)] for pa in (-1, 0, 1)]
        bands.append(jnp.concatenate(row, axis=1))
    return jnp.concatenate(bands, axis=2)


def shifted_2(shard, axis, by):
    length = lax.axis_size(axis)
    pairs = [(i, i + by) for i in range(length) if 0 <= i + by < length]
    return lax.ppermute(shard, axis, pairs)


def shifted_3(shard, axis, by):
    length = lax.axis_size(axis)
    return lax.ppermute(shard, axis, [(i, (i + by) % length) for i in range(length)])


def shifted(padded, rim_width, direction, step_by):
    selector = []
    total_dims = padded.ndim
    for dim_index in range(total_dims):
        extent = padded.shape[dim_index]
        if dim_index == total_dims - 3 + direction:
            selector.append(slice(rim_width + step_by, extent - rim_width + step_by))
        elif dim_index >= total_dims - 3:
            selector.append(slice(rim_width, extent - rim_width))
        else:
            selector.append(slice(None))
    return padded[tuple(selector)]


def clear_ends(padded, rim_width, axial_dim):
    extent = padded.shape[axial_dim]
    at_first = lax.axis_index("axial") == 0
    at_last = lax.axis_index("axial") == lax.axis_size("axial") - 1
    shape_list = [1] * padded.ndim
    shape_list[axial_dim] = extent
    position = lax.broadcasted_iota(jnp.int32, tuple(shape_list), axial_dim)
    dropped = at_first & (position < rim_width) | at_last & (position >= extent - rim_width)
    return jnp.where(dropped, jnp.float32(0.0), padded)


def radial_pad(values, rim_width, radial_mode):
    return jnp.pad(
        values, [(0, 0)] * (values.ndim - 1) + [(rim_width, rim_width)], mode=radial_mode
    )


def transport(scalar_pad, vel_pad, density_pad, density_rim, diffusion, step_size):
    center = shifted(scalar_pad, 2, 0, 0)
    density = shifted(density_pad, density_rim, 0, 0)
    change = jnp.zeros_like(center)
    for direction in range(3):
        carried = vel_pad[direction] * scalar_pad
        advect = (
            -shifted(carried, 2, direction, 2)
            + 8.0 * shifted(carried, 2, direction, 1)
            - 8.0 * shifted(carried, 2, direction, -1)
            + shifted(carried, 2, direction, -2)
        ) / 12.0
        upper_flux = (
            0.5
            * diffusion
            * (density + shifted(density_pad, density_rim, direction, 1))
            * (shifted(scalar_pad, 2, direction, 1) - center)
        )
        lower_flux = (
            0.5
            * diffusion
            * (density + shifted(density_pad, density_rim, direction, -1))
            * (center - shifted(scalar_pad, 2, direction, -1))
        )
        change = change - advect + upper_flux - lower_flux
    return center + step_size * change


def evaporate(attrs, gas_values, alive_mask, step_size):
    parcel_mass = attrs[0]
    parcel_temp = attrs[1]
    parcel_vel = attrs[2:5]
    offsets = attrs[5:8]
    gas_heat = gas_values[3]
    gas_fuel = gas_values[4]
    evap_rate = EVAP * jax.nn.softplus(gas_heat - parcel_temp) * (1.0 - gas_fuel)
    new_mass = parcel_mass * jnp.exp(-step_size * evap_rate)
    lost_mass = parcel_mass - new_mass
    new_temp = parcel_temp + step_size * RELAX * (gas_heat - parcel_temp)
    new_vel = parcel_vel + step_size * DRAG * (gas_values[0:3] - parcel_vel)
    new_offsets = offsets + step_size * new_vel
    heat_source = -LATENT * lost_mass - HEAT_CAP * new_mass * (new_temp - parcel_temp)
    new_attrs = (
        jnp.concatenate([new_mass[None], new_temp[None], new_vel, new_offsets], axis=0)
        * alive_mask[None]
    )
    sources = jnp.stack([heat_source * alive_mask, lost_mass * alive_mask])
    return (new_attrs, sources)


def pressure_pad(values):
    padded = extended(values, (("axial", 0), ("azim", 1)), 1)
    return radial_pad(clear_ends(padded, 1, 0), 1, "constant")


def operate(values):
    padded = pressure_pad(values)
    beside = shifted(padded, 1, 0, 1) + shifted(padded, 1, 0, -1)
    beside = beside + shifted(padded, 1, 1, 1) + shifted(padded, 1, 1, -1)
    beside = beside + shifted(padded, 1, 2, 1) + shifted(padded, 1, 2, -1)
    return (6.0 + SHIFT_PRESSURE) * values - beside


def reduce_groups():
    axial = lax.axis_size("axial")
    along_x = 4 if axial % 4 == 0 else 1
    groups = [("azim", 1, lax.axis_size("azim")), ("axial", 1, along_x), ("axial", along_x, axial // along_x)]
    return [group for group in groups if group[2] > 1]


def coefficient_cg(gram, size, shift, half_width):
    def apply_a(c):
        out = [shift * c[j] for j in range(size)]
        for j in range(size - 1):
            if j == 0:
                out[1] = out[1] + half_width * c[0]
            else:
                out[j + 1] = out[j + 1] + 0.5 * half_width * c[j]
                out[j - 1] = out[j - 1] + 0.5 * half_width * c[j]
        return out

    def inner(a, b):
        acc = None
        for i in range(size):
            for j in range(size):
                if isinstance(a[i], float) and a[i] == 0.0:
                    continue
                if isinstance(b[j], float) and b[j] == 0.0:
                    continue
                term = a[i] * gram[i][j] * b[j]
                acc = term if acc is None else acc + term
        return acc

    solution_c = [0.0] * size
    residual = [1.0] + [0.0] * (size - 1)
    search = list(residual)
    norm_now = inner(residual, residual)
    for iteration in range(ITERS):
        image = apply_a(search)
        alpha = norm_now / inner(search, image)
        solution_c = [solution_c[j] + alpha * search[j] for j in range(size)]
        residual = [residual[j] - alpha * image[j] for j in range(size)]
        if iteration == ITERS - 1:
            break
        norm_next = inner(residual, residual)
        search = [residual[j] + norm_next / norm_now * search[j] for j in range(size)]
        norm_now = norm_next
    return solution_c


def reduce_kernel(groups, halo_steps, shift, half_width, vel_ref, *refs):
    size = ITERS + 1
    halos = len(halo_steps)
    basis_refs = refs[:size]
    halo_sources = refs[size : size + halos]
    o_ref = refs[size + halos]
    halo_outs = refs[size + halos + 1 : size + 2 * halos + 1]
    slots, send_sems, recv_sems = refs[size + 2 * halos + 1 : size + 2 * halos + 4]
    halo_landing = refs[size + 2 * halos + 4 : size + 3 * halos + 4]
    halo_send, halo_recv = refs[size + 3 * halos + 4 :]
    here = {"axial": lax.axis_index("axial"), "azim": lax.axis_index("azim")}

    def neighbour(step_axial, step_azim):
        return (
            (here["axial"] + step_axial + lax.axis_size("axial")) % lax.axis_size("axial"),
            (here["azim"] + step_azim + lax.axis_size("azim")) % lax.axis_size("azim"),
        )

    def member(axis, stride, count, m):
        index = here[axis]
        base = index - ((index // stride) % count) * stride
        coords = dict(here)
        coords[axis] = base + m * stride
        return (coords["axial"], coords["azim"])

    def position(axis, stride, count):
        return (here[axis] // stride) % count

    barrier = pltpu.get_barrier_semaphore()
    greeted = 0
    for axis, stride, count in groups:
        mine = position(axis, stride, count)
        for m in range(1, count):
            pl.semaphore_signal(
                barrier,
                inc=1,
                device_id=member(axis, stride, count, (mine + m) % count),
                device_id_type=pl.DeviceIdType.MESH,
            )
            greeted += 1
    for step in sorted(set(halo_steps)):
        pl.semaphore_signal(
            barrier, inc=1, device_id=neighbour(*step), device_id_type=pl.DeviceIdType.MESH
        )
        greeted += 1
    pl.semaphore_wait(barrier, greeted)
    halo_copies = []
    for k, step in enumerate(halo_steps):
        copy = pltpu.make_async_remote_copy(
            src_ref=halo_sources[k],
            dst_ref=halo_landing[k],
            send_sem=halo_send.at[k],
            recv_sem=halo_recv.at[k],
            device_id=neighbour(*step),
            device_id_type=pl.DeviceIdType.MESH,
        )
        copy.start()
        halo_copies.append(copy)
    row = lax.broadcasted_iota(jnp.int32, o_ref.shape, 0)
    lane = lax.broadcasted_iota(jnp.int32, o_ref.shape, 1)
    is_max = (row == 0) & (lane == 0)

    def total(x):
        return jnp.sum(jnp.sum(x, axis=0, keepdims=True), axis=1, keepdims=True)

    basis = [ref[...] for ref in basis_refs]
    pairs = [(i, j) for i in range(size) for j in range(i, size)]
    entries = [jnp.max(jnp.max(jnp.abs(vel_ref[...]), axis=0, keepdims=True), axis=1, keepdims=True)]
    entries += [total(basis[i] * basis[j]) for i, j in pairs]
    acc = jnp.zeros(o_ref.shape, jnp.float32)
    for n, entry in enumerate(entries):
        acc = jnp.where((row == 0) & (lane == n), entry, acc)
    offset = 0
    for axis, stride, count in groups:
        mine = position(axis, stride, count)
        slots[offset + mine] = acc
        copies = []
        for m in range(1, count):
            target = (mine + m) % count
            copy = pltpu.make_async_remote_copy(
                src_ref=slots.at[offset + mine],
                dst_ref=slots.at[offset + mine],
                send_sem=send_sems.at[offset + target],
                recv_sem=recv_sems.at[offset + mine],
                device_id=member(axis, stride, count, target),
                device_id_type=pl.DeviceIdType.MESH,
            )
            copy.start()
            copies.append(copy)
        for copy in copies:
            copy.wait_send()
        for m in range(count):
            incoming = pltpu.make_async_remote_copy(
                src_ref=slots.at[offset + m],
                dst_ref=slots.at[offset + m],
                send_sem=send_sems.at[offset + m],
                recv_sem=recv_sems.at[offset + m],
                device_id=member(axis, stride, count, m),
                device_id_type=pl.DeviceIdType.MESH,
            )

            @pl.when(m != mine)
            def _():
                incoming.wait_recv()

        combined = slots[offset]
        for m in range(1, count):
            other = slots[offset + m]
            combined = jnp.where(is_max, jnp.maximum(combined, other), combined + other)
        acc = combined
        offset += count
    first = acc[0:1, :]
    first_lane = lax.broadcasted_iota(jnp.int32, first.shape, 1)

    def entry_at(n):
        return jnp.sum(jnp.where(first_lane == n, first, 0.0), axis=1, keepdims=True)

    gram = [[None] * size for _ in range(size)]
    for n, (i, j) in enumerate(pairs):
        gram[i][j] = entry_at(n + 1)
        gram[j][i] = gram[i][j]
    coefficients = coefficient_cg(gram, size, shift, half_width)
    out = jnp.where(lane == ITERS, entry_at(0), 0.0)
    for j in range(ITERS):
        out = jnp.where((lane == j), coefficients[j], out)
    o_ref[...] = out
    for k, copy in enumerate(halo_copies):
        copy.wait()
        halo_outs[k][...] = halo_landing[k][...]


def pressure_coefficients(velocity, basis, shift, half_width, halo_items):
    groups = reduce_groups()
    slot_count = sum(count for _, _, count in groups)
    flat = [v.reshape(-1, v.shape[-1]) for v in basis]
    halo_steps = [step for _, step in halo_items]
    halo_flat = [a.reshape(-1, a.shape[-1]) for a, _ in halo_items]
    halos = len(halo_flat)
    outs = pl.pallas_call(
        lambda *refs: reduce_kernel(groups, halo_steps, shift, half_width, *refs),
        out_shape=[jax.ShapeDtypeStruct((8, 128), jnp.float32)]
        + [jax.ShapeDtypeStruct(f.shape, f.dtype) for f in halo_flat],
        in_specs=[pl.BlockSpec(memory_space=pltpu.VMEM)] * (1 + len(flat) + halos),
        out_specs=[pl.BlockSpec(memory_space=pltpu.VMEM)] * (1 + halos),
        scratch_shapes=[
            pltpu.VMEM((slot_count, 8, 128), jnp.float32),
            pltpu.SemaphoreType.DMA((slot_count,)),
            pltpu.SemaphoreType.DMA((slot_count,)),
        ]
        + [pltpu.VMEM(f.shape, f.dtype) for f in halo_flat]
        + [pltpu.SemaphoreType.DMA((halos,)), pltpu.SemaphoreType.DMA((halos,))],
        compiler_params=pltpu.CompilerParams(collective_id=0, has_side_effects=True),
    )(velocity.reshape(-1, velocity.shape[-1]), *flat, *halo_flat)
    out = outs[0]
    received = [o.reshape(a.shape) for o, (a, _) in zip(outs[1:], halo_items)]
    return [out[0, j] for j in range(ITERS)], out[0, ITERS], received


def neighbour_sum(padded):
    beside = shifted(padded, 1, 0, 1) + shifted(padded, 1, 0, -1)
    beside = beside + shifted(padded, 1, 1, 1) + shifted(padded, 1, 1, -1)
    return beside + shifted(padded, 1, 2, 1) + shifted(padded, 1, 2, -1)


def axial_valid(values, rim):
    extent = values.shape[0]
    inner_x = extent - 2 * rim
    first = lax.axis_index("axial") * inner_x - rim
    position = first + lax.broadcasted_iota(jnp.int32, (extent, 1, 1), 0)
    inside = (position >= 0) & (position < inner_x * lax.axis_size("axial"))
    return jnp.where(inside, values, jnp.float32(0.0))


def crop(values, by):
    if by == 0:
        return values
    return values[by:-by, by:-by]


def neighbour_sum_wide(values):
    padded = jnp.pad(values, [(0, 0), (0, 0), (1, 1)])
    nx, ny, nz = padded.shape

    def at(dx, dy, dz):
        return padded[1 + dx : nx - 1 + dx, 1 + dy : ny - 1 + dy, 1 + dz : nz - 1 + dz]

    beside = at(1, 0, 0) + at(-1, 0, 0)
    beside = beside + at(0, 1, 0) + at(0, -1, 0)
    return beside + at(0, 0, 1) + at(0, 0, -1)


def solve_pressure(wide_velocity, velocity, halo_items):
    half_width = 6.0
    u = wide_velocity
    divergence = 0.5 * (u[0, 2:, 1:-1, 1:-1] - u[0, :-2, 1:-1, 1:-1])
    divergence = divergence + 0.5 * (u[1, 1:-1, 2:, 1:-1] - u[1, 1:-1, :-2, 1:-1])
    divergence = divergence + 0.5 * (u[2, 1:-1, 1:-1, 2:] - u[2, 1:-1, 1:-1, :-2])
    basis = [axial_valid(divergence, ITERS)]
    for j in range(ITERS):
        scaled = neighbour_sum_wide(basis[j]) * (-1.0 / half_width)
        if j == 0:
            fresh = scaled
        else:
            fresh = 2.0 * scaled - crop(basis[j - 1], 2)
        basis.append(axial_valid(fresh, ITERS - 1 - j))
    interior = [crop(basis[j], ITERS - j) for j in range(ITERS + 1)]
    coefficients, fastest, received = pressure_coefficients(
        velocity, interior, 6.0 + SHIFT_PRESSURE, half_width, halo_items
    )
    padded_basis = [radial_pad(crop(basis[j], ITERS - j - 1), 1, "constant") for j in range(ITERS)]
    padded_pressure = coefficients[0] * padded_basis[0]
    for j in range(1, ITERS):
        padded_pressure = padded_pressure + coefficients[j] * padded_basis[j]
    return padded_pressure, fastest, received


def along_axial(buffer, step_by):
    return shifted_2(buffer, "axial", step_by)


def along_azim(buffer, step_by):
    return shifted_3(buffer, "azim", step_by)


def on_device(state, diff_coef, parcel_state, parcel_cell, parcel_dest, live_count):
    velocity = state[1:4]
    npar_local = parcel_cell.shape[0]
    cells_x, cells_y, cells_z = (state.shape[1], state.shape[2], state.shape[3])
    plane_count = cells_x * cells_y
    gas_table = jnp.transpose(state[1:6].reshape(5, plane_count, cells_z), (1, 0, 2)).reshape(
        plane_count, 5 * cells_z
    )
    live_now = live_count[0]
    slot_alive = jnp.arange(npar_local) < live_now
    alive_mask = slot_alive.astype(jnp.float32)
    plane_ids = parcel_cell // cells_z
    radial_ids = parcel_cell % cells_z
    plane_hot = (plane_ids[:, None] == jnp.arange(plane_count)[None, :]).astype(jnp.float32)
    radial_hot = (radial_ids[:, None] == jnp.arange(cells_z)[None, :]).astype(jnp.float32)
    gas_rows = jnp.dot(plane_hot, gas_table, precision=HIGHEST).reshape(npar_local, 5, cells_z)
    gas_values = jnp.sum(gas_rows * radial_hot[:, None, :], axis=2).T
    stacked = jnp.stack([(parcel_dest == d + 1) & slot_alive for d in range(4)]).astype(jnp.int32)
    ranks = jnp.cumsum(stacked, axis=1) - 1
    mover = jnp.sum(stacked, axis=0) > 0
    target = jnp.where(mover, jnp.sum(stacked * (jnp.arange(4)[:, None] * CAP + ranks), axis=0), -1)
    select = (target[:, None] == jnp.arange(4 * CAP)[None, :]).astype(jnp.float32)
    raw = jnp.concatenate([parcel_state, gas_values, alive_mask[None]], axis=0)
    leaving = jnp.transpose(
        jnp.dot(raw, select, precision=HIGHEST).reshape(raw.shape[0], 4, CAP), (1, 0, 2)
    )
    parcel_steps = [(-1, 0), (1, 0), (0, -1), (0, 1)]
    rim = ITERS + 1
    items = [(rim_slab(velocity, rim, sa, sz), (sa, sz)) for sa, sz in NEIGHBOURS]
    items += [(leaving[d], parcel_steps[d]) for d in range(4)]
    got = neighbour_exchange(items)
    count = len(NEIGHBOURS)
    velocity_rims = {(-sa, -sz): got[k] for k, (sa, sz) in enumerate(NEIGHBOURS)}
    landed = got[count:]
    others = jnp.concatenate([state[0:1], state[4:]], axis=0)
    halo_items = [(rim_slab(others, 2, sa, sz), (sa, sz)) for sa, sz in NEIGHBOURS]
    wide_raw = assemble(velocity, velocity_rims)
    wide_velocity = radial_pad(clear_ends(wide_raw, rim, 1), 1, "edge")
    padded_pressure, fastest, received = solve_pressure(wide_velocity, velocity, halo_items)
    others_rims = {(-sa, -sz): received[k] for k, (sa, sz) in enumerate(NEIGHBOURS)}
    others_pad = assemble(others, others_rims)
    cut = rim - 2
    velocity_pad2 = wide_raw[:, cut:-cut, cut:-cut]
    whole_pad = jnp.concatenate([others_pad[0:1], velocity_pad2, others_pad[1:]], axis=0)
    whole_pad = radial_pad(clear_ends(whole_pad, 2, 1), 2, "edge")
    moving = whole_pad[1:]
    density_pad = whole_pad[0]
    density_rim = 2
    vel_pad = moving[0:3]
    step_size = CFL / (fastest + 1e-06)
    transported = transport(
        moving[3:], vel_pad, density_pad, density_rim, diff_coef[:, None, None, None], step_size
    )
    updated, sources = evaporate(parcel_state, gas_values, alive_mask, step_size)
    spread = (sources.T[:, :, None] * radial_hot[:, None, :]).reshape(npar_local, 2 * cells_z)
    deposit = lax.dot_general(plane_hot, spread, (((0,), (0,)), ((), ())), precision=HIGHEST)
    deposit = jnp.transpose(deposit.reshape(cells_x, cells_y, 2, cells_z), (2, 0, 1, 3))
    scalars_new = jnp.concatenate(
        [transported[:2] + deposit / state[0][None], transported[2:]], axis=0
    )
    at_first = lax.axis_index("axial") == 0
    at_last = lax.axis_index("axial") == lax.axis_size("axial") - 1
    arriving = []
    for d in range(4):
        payload = landed[d]
        if d == 0:
            payload = jnp.where(at_last, jnp.float32(0.0), payload)
        if d == 1:
            payload = jnp.where(at_first, jnp.float32(0.0), payload)
        moved, _ = evaporate(payload[:8], payload[8:13], payload[13], step_size)
        arriving.append(moved)
    arrived = jnp.stack(arriving)
    kept_parcels = jnp.where((parcel_dest == 0)[None], updated, jnp.float32(0.0))
    velocity_new = jnp.stack(
        [
            velocity[d]
            - 0.5 * (shifted(padded_pressure, 1, d, 1) - shifted(padded_pressure, 1, d, -1))
            for d in range(3)
        ]
    )
    return (scalars_new, velocity_new, kept_parcels, arrived)


def solution(mesh):
    in_specs = (
        P(None, "axial", "azim", None),
        P(),
        P(None, ("axial", "azim")),
        P(("axial", "azim")),
        P(("axial", "azim")),
        P(("axial", "azim")),
    )
    out_specs = (
        P(None, "axial", "azim", None),
        P(None, "axial", "azim", None),
        P(None, ("axial", "azim")),
        P(None, None, ("axial", "azim")),
    )
    return jax.shard_map(
        on_device, mesh=mesh, in_specs=in_specs, out_specs=out_specs, check_vma=False
    )
```

```python
import jax
import jax.numpy as jnp
from jax import lax
from jax.sharding import PartitionSpec as P
from jax.experimental import pallas as pl
from jax.experimental.pallas import tpu as pltpu

CAP = 64
ITERS = 4


CFL = 0.4
SHIFT_PRESSURE = 0.25
EVAP = 8.0
RELAX = 4.0
DRAG = 6.0
LATENT = 0.5
HEAT_CAP = 0.8
HIGHEST = lax.Precision.HIGHEST


def extended(block, sides, width):
    for axis, dim in sides:
        count = lax.axis_size(axis)
        forward = [(i, i + 1) for i in range(count - 1)]
        forward.append((count - 1, 0))
        backward = [(target, source) for source, target in forward]
        low = lax.ppermute(
            lax.slice_in_dim(block, block.shape[dim] - width, None, axis=dim), axis, forward
        )
        high = lax.ppermute(lax.slice_in_dim(block, 0, width, axis=dim), axis, backward)
        block = jnp.concatenate([low, block, high], axis=dim)
    return block


def exchange_kernel(offsets, *refs):
    count = len(offsets)
    sources = refs[:count]
    outs = refs[count : 2 * count]
    landing = refs[2 * count : 3 * count]
    send_sems, recv_sems = refs[3 * count :]
    axial = lax.axis_index("axial")
    azim = lax.axis_index("azim")

    def device(step_axial, step_azim):
        return (
            (axial + step_axial + lax.axis_size("axial")) % lax.axis_size("axial"),
            (azim + step_azim + lax.axis_size("azim")) % lax.axis_size("azim"),
        )

    neighbours = sorted(set(offsets))
    barrier = pltpu.get_barrier_semaphore()
    for step in neighbours:
        pl.semaphore_signal(
            barrier, inc=1, device_id=device(*step), device_id_type=pl.DeviceIdType.MESH
        )
    pl.semaphore_wait(barrier, len(neighbours))
    copies = []
    for k, step in enumerate(offsets):
        copy = pltpu.make_async_remote_copy(
            src_ref=sources[k],
            dst_ref=landing[k],
            send_sem=send_sems.at[k],
            recv_sem=recv_sems.at[k],
            device_id=device(*step),
            device_id_type=pl.DeviceIdType.MESH,
        )
        copy.start()
        copies.append(copy)
    for k, copy in enumerate(copies):
        copy.wait()
        outs[k][...] = landing[k][...]


def neighbour_exchange(items):
    offsets = [step for _, step in items]
    flat = [a for a, _ in items]
    count = len(flat)
    outs = pl.pallas_call(
        lambda *refs: exchange_kernel(offsets, *refs),
        out_shape=[jax.ShapeDtypeStruct(f.shape, f.dtype) for f in flat],
        in_specs=[pl.BlockSpec(memory_space=pltpu.VMEM)] * count,
        out_specs=[pl.BlockSpec(memory_space=pltpu.VMEM)] * count,
        scratch_shapes=[pltpu.VMEM(f.shape, f.dtype) for f in flat]
        + [pltpu.SemaphoreType.DMA((count,)), pltpu.SemaphoreType.DMA((count,))],
        compiler_params=pltpu.CompilerParams(collective_id=1, has_side_effects=True),
    )(*flat)
    return list(outs)


def rim_slab(block, width, step_axial, step_azim):
    def pick(values, dim, step):
        if step > 0:
            return lax.slice_in_dim(values, values.shape[dim] - width, None, axis=dim)
        if step < 0:
            return lax.slice_in_dim(values, 0, width, axis=dim)
        return values

    return pick(pick(block, 1, step_axial), 2, step_azim)


NEIGHBOURS = [(sa, sz) for sa in (-1, 0, 1) for sz in (-1, 0, 1) if (sa, sz) != (0, 0)]


def assemble(block, received):
    bands = []
    for pz in (-1, 0, 1):
        row = [block if (pa, pz) == (0, 0) else received[(pa, pz)] for pa in (-1, 0, 1)]
        bands.append(jnp.concatenate(row, axis=1))
    return jnp.concatenate(bands, axis=2)


def shifted_2(shard, axis, by):
    length = lax.axis_size(axis)
    pairs = [(i, i + by) for i in range(length) if 0 <= i + by < length]
    return lax.ppermute(shard, axis, pairs)


def shifted_3(shard, axis, by):
    length = lax.axis_size(axis)
    return lax.ppermute(shard, axis, [(i, (i + by) % length) for i in range(length)])


def shifted(padded, rim_width, direction, step_by):
    selector = []
    total_dims = padded.ndim
    for dim_index in range(total_dims):
        extent = padded.shape[dim_index]
        if dim_index == total_dims - 3 + direction:
            selector.append(slice(rim_width + step_by, extent - rim_width + step_by))
        elif dim_index >= total_dims - 3:
            selector.append(slice(rim_width, extent - rim_width))
        else:
            selector.append(slice(None))
    return padded[tuple(selector)]


def clear_ends(padded, rim_width, axial_dim):
    extent = padded.shape[axial_dim]
    at_first = lax.axis_index("axial") == 0
    at_last = lax.axis_index("axial") == lax.axis_size("axial") - 1
    shape_list = [1] * padded.ndim
    shape_list[axial_dim] = extent
    position = lax.broadcasted_iota(jnp.int32, tuple(shape_list), axial_dim)
    dropped = at_first & (position < rim_width) | at_last & (position >= extent - rim_width)
    return jnp.where(dropped, jnp.float32(0.0), padded)


def radial_pad(values, rim_width, radial_mode):
    return jnp.pad(
        values, [(0, 0)] * (values.ndim - 1) + [(rim_width, rim_width)], mode=radial_mode
    )


def transport(scalar_pad, vel_pad, density_pad, density_rim, diffusion, step_size):
    center = shifted(scalar_pad, 2, 0, 0)
    density = shifted(density_pad, density_rim, 0, 0)
    change = jnp.zeros_like(center)
    for direction in range(3):
        carried = vel_pad[direction] * scalar_pad
        advect = (
            -shifted(carried, 2, direction, 2)
            + 8.0 * shifted(carried, 2, direction, 1)
            - 8.0 * shifted(carried, 2, direction, -1)
            + shifted(carried, 2, direction, -2)
        ) / 12.0
        upper_flux = (
            0.5
            * diffusion
            * (density + shifted(density_pad, density_rim, direction, 1))
            * (shifted(scalar_pad, 2, direction, 1) - center)
        )
        lower_flux = (
            0.5
            * diffusion
            * (density + shifted(density_pad, density_rim, direction, -1))
            * (center - shifted(scalar_pad, 2, direction, -1))
        )
        change = change - advect + upper_flux - lower_flux
    return center + step_size * change


def evaporate(attrs, gas_values, alive_mask, step_size):
    parcel_mass = attrs[0]
    parcel_temp = attrs[1]
    parcel_vel = attrs[2:5]
    offsets = attrs[5:8]
    gas_heat = gas_values[3]
    gas_fuel = gas_values[4]
    evap_rate = EVAP * jax.nn.softplus(gas_heat - parcel_temp) * (1.0 - gas_fuel)
    new_mass = parcel_mass * jnp.exp(-step_size * evap_rate)
    lost_mass = parcel_mass - new_mass
    new_temp = parcel_temp + step_size * RELAX * (gas_heat - parcel_temp)
    new_vel = parcel_vel + step_size * DRAG * (gas_values[0:3] - parcel_vel)
    new_offsets = offsets + step_size * new_vel
    heat_source = -LATENT * lost_mass - HEAT_CAP * new_mass * (new_temp - parcel_temp)
    new_attrs = (
        jnp.concatenate([new_mass[None], new_temp[None], new_vel, new_offsets], axis=0)
        * alive_mask[None]
    )
    sources = jnp.stack([heat_source * alive_mask, lost_mass * alive_mask])
    return (new_attrs, sources)


def pressure_pad(values):
    padded = extended(values, (("axial", 0), ("azim", 1)), 1)
    return radial_pad(clear_ends(padded, 1, 0), 1, "constant")


def operate(values):
    padded = pressure_pad(values)
    beside = shifted(padded, 1, 0, 1) + shifted(padded, 1, 0, -1)
    beside = beside + shifted(padded, 1, 1, 1) + shifted(padded, 1, 1, -1)
    beside = beside + shifted(padded, 1, 2, 1) + shifted(padded, 1, 2, -1)
    return (6.0 + SHIFT_PRESSURE) * values - beside


def reduce_groups():
    axial = lax.axis_size("axial")
    along_x = 4 if axial % 4 == 0 else 1
    groups = [("azim", 1, lax.axis_size("azim")), ("axial", 1, along_x), ("axial", along_x, axial // along_x)]
    return [group for group in groups if group[2] > 1]


def coefficient_cg(gram, size, shift, half_width):
    def apply_a(c):
        out = [shift * c[j] for j in range(size)]
        for j in range(size - 1):
            if j == 0:
                out[1] = out[1] + half_width * c[0]
            else:
                out[j + 1] = out[j + 1] + 0.5 * half_width * c[j]
                out[j - 1] = out[j - 1] + 0.5 * half_width * c[j]
        return out

    def inner(a, b):
        acc = None
        for i in range(size):
            for j in range(size):
                if isinstance(a[i], float) and a[i] == 0.0:
                    continue
                if isinstance(b[j], float) and b[j] == 0.0:
                    continue
                term = a[i] * gram[i][j] * b[j]
                acc = term if acc is None else acc + term
        return acc

    solution_c = [0.0] * size
    residual = [1.0] + [0.0] * (size - 1)
    search = list(residual)
    norm_now = inner(residual, residual)
    for iteration in range(ITERS):
        image = apply_a(search)
        alpha = norm_now / inner(search, image)
        solution_c = [solution_c[j] + alpha * search[j] for j in range(size)]
        residual = [residual[j] - alpha * image[j] for j in range(size)]
        if iteration == ITERS - 1:
            break
        norm_next = inner(residual, residual)
        search = [residual[j] + norm_next / norm_now * search[j] for j in range(size)]
        norm_now = norm_next
    return solution_c


def reduce_kernel(groups, shift, half_width, vel_ref, *refs):
    size = ITERS + 1
    basis_refs = refs[:size]
    o_ref, slots, send_sems, recv_sems = refs[size:]
    here = {"axial": lax.axis_index("axial"), "azim": lax.axis_index("azim")}

    def member(axis, stride, count, m):
        index = here[axis]
        base = index - ((index // stride) % count) * stride
        coords = dict(here)
        coords[axis] = base + m * stride
        return (coords["axial"], coords["azim"])

    def position(axis, stride, count):
        return (here[axis] // stride) % count

    barrier = pltpu.get_barrier_semaphore()
    greeted = 0
    for axis, stride, count in groups:
        mine = position(axis, stride, count)
        for m in range(1, count):
            pl.semaphore_signal(
                barrier,
                inc=1,
                device_id=member(axis, stride, count, (mine + m) % count),
                device_id_type=pl.DeviceIdType.MESH,
            )
            greeted += 1
    pl.semaphore_wait(barrier, greeted)
    row = lax.broadcasted_iota(jnp.int32, o_ref.shape, 0)
    lane = lax.broadcasted_iota(jnp.int32, o_ref.shape, 1)
    is_max = (row == 0) & (lane == 0)

    def total(x):
        return jnp.sum(jnp.sum(x, axis=0, keepdims=True), axis=1, keepdims=True)

    basis = [ref[...] for ref in basis_refs]
    pairs = [(i, j) for i in range(size) for j in range(i, size)]
    entries = [jnp.max(jnp.max(jnp.abs(vel_ref[...]), axis=0, keepdims=True), axis=1, keepdims=True)]
    entries += [total(basis[i] * basis[j]) for i, j in pairs]
    acc = jnp.zeros(o_ref.shape, jnp.float32)
    for n, entry in enumerate(entries):
        acc = jnp.where((row == 0) & (lane == n), entry, acc)
    offset = 0
    for axis, stride, count in groups:
        mine = position(axis, stride, count)
        slots[offset + mine] = acc
        copies = []
        for m in range(1, count):
            target = (mine + m) % count
            copy = pltpu.make_async_remote_copy(
                src_ref=slots.at[offset + mine],
                dst_ref=slots.at[offset + mine],
                send_sem=send_sems.at[offset + target],
                recv_sem=recv_sems.at[offset + mine],
                device_id=member(axis, stride, count, target),
                device_id_type=pl.DeviceIdType.MESH,
            )
            copy.start()
            copies.append(copy)
        for copy in copies:
            copy.wait_send()
        for m in range(count):
            incoming = pltpu.make_async_remote_copy(
                src_ref=slots.at[offset + m],
                dst_ref=slots.at[offset + m],
                send_sem=send_sems.at[offset + m],
                recv_sem=recv_sems.at[offset + m],
                device_id=member(axis, stride, count, m),
                device_id_type=pl.DeviceIdType.MESH,
            )

            @pl.when(m != mine)
            def _():
                incoming.wait_recv()

        combined = slots[offset]
        for m in range(1, count):
            other = slots[offset + m]
            combined = jnp.where(is_max, jnp.maximum(combined, other), combined + other)
        acc = combined
        offset += count
    first = acc[0:1, :]
    first_lane = lax.broadcasted_iota(jnp.int32, first.shape, 1)

    def entry_at(n):
        return jnp.sum(jnp.where(first_lane == n, first, 0.0), axis=1, keepdims=True)

    gram = [[None] * size for _ in range(size)]
    for n, (i, j) in enumerate(pairs):
        gram[i][j] = entry_at(n + 1)
        gram[j][i] = gram[i][j]
    coefficients = coefficient_cg(gram, size, shift, half_width)
    out = jnp.where(lane == ITERS, entry_at(0), 0.0)
    for j in range(ITERS):
        out = jnp.where((lane == j), coefficients[j], out)
    o_ref[...] = out


def pressure_coefficients(velocity, basis, shift, half_width):
    groups = reduce_groups()
    slot_count = sum(count for _, _, count in groups)
    flat = [v.reshape(-1, v.shape[-1]) for v in basis]
    out = pl.pallas_call(
        lambda *refs: reduce_kernel(groups, shift, half_width, *refs),
        out_shape=jax.ShapeDtypeStruct((8, 128), jnp.float32),
        in_specs=[pl.BlockSpec(memory_space=pltpu.VMEM)] * (1 + len(flat)),
        out_specs=pl.BlockSpec(memory_space=pltpu.VMEM),
        scratch_shapes=[
            pltpu.VMEM((slot_count, 8, 128), jnp.float32),
            pltpu.SemaphoreType.DMA((slot_count,)),
            pltpu.SemaphoreType.DMA((slot_count,)),
        ],
        compiler_params=pltpu.CompilerParams(collective_id=0, has_side_effects=True),
    )(velocity.reshape(-1, velocity.shape[-1]), *flat)
    return [out[0, j] for j in range(ITERS)], out[0, ITERS]


def neighbour_sum(padded):
    beside = shifted(padded, 1, 0, 1) + shifted(padded, 1, 0, -1)
    beside = beside + shifted(padded, 1, 1, 1) + shifted(padded, 1, 1, -1)
    return beside + shifted(padded, 1, 2, 1) + shifted(padded, 1, 2, -1)


def axial_valid(values, rim):
    extent = values.shape[0]
    inner_x = extent - 2 * rim
    first = lax.axis_index("axial") * inner_x - rim
    position = first + lax.broadcasted_iota(jnp.int32, (extent, 1, 1), 0)
    inside = (position >= 0) & (position < inner_x * lax.axis_size("axial"))
    return jnp.where(inside, values, jnp.float32(0.0))


def crop(values, by):
    if by == 0:
        return values
    return values[by:-by, by:-by]


def neighbour_sum_wide(values):
    padded = jnp.pad(values, [(0, 0), (0, 0), (1, 1)])
    nx, ny, nz = padded.shape

    def at(dx, dy, dz):
        return padded[1 + dx : nx - 1 + dx, 1 + dy : ny - 1 + dy, 1 + dz : nz - 1 + dz]

    beside = at(1, 0, 0) + at(-1, 0, 0)
    beside = beside + at(0, 1, 0) + at(0, -1, 0)
    return beside + at(0, 0, 1) + at(0, 0, -1)


def solve_pressure(wide_velocity, velocity):
    half_width = 6.0
    u = wide_velocity
    divergence = 0.5 * (u[0, 2:, 1:-1, 1:-1] - u[0, :-2, 1:-1, 1:-1])
    divergence = divergence + 0.5 * (u[1, 1:-1, 2:, 1:-1] - u[1, 1:-1, :-2, 1:-1])
    divergence = divergence + 0.5 * (u[2, 1:-1, 1:-1, 2:] - u[2, 1:-1, 1:-1, :-2])
    basis = [axial_valid(divergence, ITERS)]
    for j in range(ITERS):
        scaled = neighbour_sum_wide(basis[j]) * (-1.0 / half_width)
        if j == 0:
            fresh = scaled
        else:
            fresh = 2.0 * scaled - crop(basis[j - 1], 2)
        basis.append(axial_valid(fresh, ITERS - 1 - j))
    interior = [crop(basis[j], ITERS - j) for j in range(ITERS + 1)]
    coefficients, fastest = pressure_coefficients(
        velocity, interior, 6.0 + SHIFT_PRESSURE, half_width
    )
    padded_basis = [radial_pad(crop(basis[j], ITERS - j - 1), 1, "constant") for j in range(ITERS)]
    padded_pressure = coefficients[0] * padded_basis[0]
    for j in range(1, ITERS):
        padded_pressure = padded_pressure + coefficients[j] * padded_basis[j]
    return padded_pressure, fastest


def along_axial(buffer, step_by):
    return shifted_2(buffer, "axial", step_by)


def along_azim(buffer, step_by):
    return shifted_3(buffer, "azim", step_by)


def on_device(state, diff_coef, parcel_state, parcel_cell, parcel_dest, live_count):
    velocity = state[1:4]
    npar_local = parcel_cell.shape[0]
    cells_x, cells_y, cells_z = (state.shape[1], state.shape[2], state.shape[3])
    plane_count = cells_x * cells_y
    gas_table = jnp.transpose(state[1:6].reshape(5, plane_count, cells_z), (1, 0, 2)).reshape(
        plane_count, 5 * cells_z
    )
    live_now = live_count[0]
    slot_alive = jnp.arange(npar_local) < live_now
    alive_mask = slot_alive.astype(jnp.float32)
    plane_ids = parcel_cell // cells_z
    radial_ids = parcel_cell % cells_z
    plane_hot = (plane_ids[:, None] == jnp.arange(plane_count)[None, :]).astype(jnp.float32)
    radial_hot = (radial_ids[:, None] == jnp.arange(cells_z)[None, :]).astype(jnp.float32)
    gas_rows = jnp.dot(plane_hot, gas_table, precision=HIGHEST).reshape(npar_local, 5, cells_z)
    gas_values = jnp.sum(gas_rows * radial_hot[:, None, :], axis=2).T
    stacked = jnp.stack([(parcel_dest == d + 1) & slot_alive for d in range(4)]).astype(jnp.int32)
    ranks = jnp.cumsum(stacked, axis=1) - 1
    mover = jnp.sum(stacked, axis=0) > 0
    target = jnp.where(mover, jnp.sum(stacked * (jnp.arange(4)[:, None] * CAP + ranks), axis=0), -1)
    select = (target[:, None] == jnp.arange(4 * CAP)[None, :]).astype(jnp.float32)
    raw = jnp.concatenate([parcel_state, gas_values, alive_mask[None]], axis=0)
    leaving = jnp.transpose(
        jnp.dot(raw, select, precision=HIGHEST).reshape(raw.shape[0], 4, CAP), (1, 0, 2)
    )
    parcel_steps = [(-1, 0), (1, 0), (0, -1), (0, 1)]
    items = [(rim_slab(state, 2, sa, sz), (sa, sz)) for sa, sz in NEIGHBOURS]
    items += [(rim_slab(velocity, ITERS + 1, sa, sz), (sa, sz)) for sa, sz in NEIGHBOURS]
    items += [(leaving[d], parcel_steps[d]) for d in range(4)]
    got = neighbour_exchange(items)
    count = len(NEIGHBOURS)
    state_rims = {(-sa, -sz): got[k] for k, (sa, sz) in enumerate(NEIGHBOURS)}
    velocity_rims = {(-sa, -sz): got[count + k] for k, (sa, sz) in enumerate(NEIGHBOURS)}
    landed = got[2 * count :]
    whole_pad = assemble(state, state_rims)
    whole_pad = radial_pad(clear_ends(whole_pad, 2, 1), 2, "edge")
    moving = whole_pad[1:]
    density_pad = whole_pad[0]
    density_rim = 2
    vel_pad = moving[0:3]
    wide_velocity = assemble(velocity, velocity_rims)
    wide_velocity = radial_pad(clear_ends(wide_velocity, ITERS + 1, 1), 1, "edge")
    padded_pressure, fastest = solve_pressure(wide_velocity, velocity)
    step_size = CFL / (fastest + 1e-06)
    transported = transport(
        moving[3:], vel_pad, density_pad, density_rim, diff_coef[:, None, None, None], step_size
    )
    updated, sources = evaporate(parcel_state, gas_values, alive_mask, step_size)
    spread = (sources.T[:, :, None] * radial_hot[:, None, :]).reshape(npar_local, 2 * cells_z)
    deposit = lax.dot_general(plane_hot, spread, (((0,), (0,)), ((), ())), precision=HIGHEST)
    deposit = jnp.transpose(deposit.reshape(cells_x, cells_y, 2, cells_z), (2, 0, 1, 3))
    scalars_new = jnp.concatenate(
        [transported[:2] + deposit / state[0][None], transported[2:]], axis=0
    )
    at_first = lax.axis_index("axial") == 0
    at_last = lax.axis_index("axial") == lax.axis_size("axial") - 1
    arriving = []
    for d in range(4):
        payload = landed[d]
        if d == 0:
            payload = jnp.where(at_last, jnp.float32(0.0), payload)
        if d == 1:
            payload = jnp.where(at_first, jnp.float32(0.0), payload)
        moved, _ = evaporate(payload[:8], payload[8:13], payload[13], step_size)
        arriving.append(moved)
    arrived = jnp.stack(arriving)
    kept_parcels = jnp.where((parcel_dest == 0)[None], updated, jnp.float32(0.0))
    velocity_new = jnp.stack(
        [
            velocity[d]
            - 0.5 * (shifted(padded_pressure, 1, d, 1) - shifted(padded_pressure, 1, d, -1))
            for d in range(3)
        ]
    )
    return (scalars_new, velocity_new, kept_parcels, arrived)


def solution(mesh):
    in_specs = (
        P(None, "axial", "azim", None),
        P(),
        P(None, ("axial", "azim")),
        P(("axial", "azim")),
        P(("axial", "azim")),
        P(("axial", "azim")),
    )
    out_specs = (
        P(None, "axial", "azim", None),
        P(None, "axial", "azim", None),
        P(None, ("axial", "azim")),
        P(None, None, ("axial", "azim")),
    )
    return jax.shard_map(
        on_device, mesh=mesh, in_specs=in_specs, out_specs=out_specs, check_vma=False
    )
```

```python
import jax
import jax.numpy as jnp
from jax import lax
from jax.sharding import PartitionSpec as P
from jax.experimental import pallas as pl
from jax.experimental.pallas import tpu as pltpu

CAP = 64
ITERS = 4


CFL = 0.4
SHIFT_PRESSURE = 0.25
EVAP = 8.0
RELAX = 4.0
DRAG = 6.0
LATENT = 0.5
HEAT_CAP = 0.8
HIGHEST = lax.Precision.HIGHEST


def extended(block, sides, width):
    for axis, dim in sides:
        count = lax.axis_size(axis)
        forward = [(i, i + 1) for i in range(count - 1)]
        forward.append((count - 1, 0))
        backward = [(target, source) for source, target in forward]
        low = lax.ppermute(
            lax.slice_in_dim(block, block.shape[dim] - width, None, axis=dim), axis, forward
        )
        high = lax.ppermute(lax.slice_in_dim(block, 0, width, axis=dim), axis, backward)
        block = jnp.concatenate([low, block, high], axis=dim)
    return block


def exchange_kernel(offsets, *refs):
    count = len(offsets)
    sources = refs[:count]
    outs = refs[count : 2 * count]
    landing = refs[2 * count : 3 * count]
    send_sems, recv_sems = refs[3 * count :]
    axial = lax.axis_index("axial")
    azim = lax.axis_index("azim")

    def device(step_axial, step_azim):
        return (
            (axial + step_axial + lax.axis_size("axial")) % lax.axis_size("axial"),
            (azim + step_azim + lax.axis_size("azim")) % lax.axis_size("azim"),
        )

    neighbours = sorted(set(offsets))
    barrier = pltpu.get_barrier_semaphore()
    for step in neighbours:
        pl.semaphore_signal(
            barrier, inc=1, device_id=device(*step), device_id_type=pl.DeviceIdType.MESH
        )
    pl.semaphore_wait(barrier, len(neighbours))
    copies = []
    for k, step in enumerate(offsets):
        copy = pltpu.make_async_remote_copy(
            src_ref=sources[k],
            dst_ref=landing[k],
            send_sem=send_sems.at[k],
            recv_sem=recv_sems.at[k],
            device_id=device(*step),
            device_id_type=pl.DeviceIdType.MESH,
        )
        copy.start()
        copies.append(copy)
    for k, copy in enumerate(copies):
        copy.wait()
        outs[k][...] = landing[k][...]


def neighbour_exchange(items):
    offsets = [step for _, step in items]
    flat = [a for a, _ in items]
    count = len(flat)
    outs = pl.pallas_call(
        lambda *refs: exchange_kernel(offsets, *refs),
        out_shape=[jax.ShapeDtypeStruct(f.shape, f.dtype) for f in flat],
        in_specs=[pl.BlockSpec(memory_space=pltpu.VMEM)] * count,
        out_specs=[pl.BlockSpec(memory_space=pltpu.VMEM)] * count,
        scratch_shapes=[pltpu.VMEM(f.shape, f.dtype) for f in flat]
        + [pltpu.SemaphoreType.DMA((count,)), pltpu.SemaphoreType.DMA((count,))],
        compiler_params=pltpu.CompilerParams(collective_id=1, has_side_effects=True),
    )(*flat)
    return list(outs)


def rim_slab(block, width, step_axial, step_azim):
    def pick(values, dim, step):
        if step > 0:
            return lax.slice_in_dim(values, values.shape[dim] - width, None, axis=dim)
        if step < 0:
            return lax.slice_in_dim(values, 0, width, axis=dim)
        return values

    return pick(pick(block, 1, step_axial), 2, step_azim)


NEIGHBOURS = [(sa, sz) for sa in (-1, 0, 1) for sz in (-1, 0, 1) if (sa, sz) != (0, 0)]


def assemble(block, received):
    rim_a = received[(-1, 0)].shape[1]
    rim_z = received[(0, -1)].shape[2]
    bands = []
    for pz in (-1, 0, 1):
        row = []
        for pa in (-1, 0, 1):
            if (pa, pz) == (0, 0):
                row.append(block)
            elif (pa, pz) in received:
                row.append(received[(pa, pz)])
            else:
                row.append(jnp.zeros(block.shape[:1] + (rim_a, rim_z) + block.shape[3:], block.dtype))
        bands.append(jnp.concatenate(row, axis=1))
    return jnp.concatenate(bands, axis=2)


def shifted_2(shard, axis, by):
    length = lax.axis_size(axis)
    pairs = [(i, i + by) for i in range(length) if 0 <= i + by < length]
    return lax.ppermute(shard, axis, pairs)


def shifted_3(shard, axis, by):
    length = lax.axis_size(axis)
    return lax.ppermute(shard, axis, [(i, (i + by) % length) for i in range(length)])


def shifted(padded, rim_width, direction, step_by):
    selector = []
    total_dims = padded.ndim
    for dim_index in range(total_dims):
        extent = padded.shape[dim_index]
        if dim_index == total_dims - 3 + direction:
            selector.append(slice(rim_width + step_by, extent - rim_width + step_by))
        elif dim_index >= total_dims - 3:
            selector.append(slice(rim_width, extent - rim_width))
        else:
            selector.append(slice(None))
    return padded[tuple(selector)]


def clear_ends(padded, rim_width, axial_dim):
    extent = padded.shape[axial_dim]
    at_first = lax.axis_index("axial") == 0
    at_last = lax.axis_index("axial") == lax.axis_size("axial") - 1
    shape_list = [1] * padded.ndim
    shape_list[axial_dim] = extent
    position = lax.broadcasted_iota(jnp.int32, tuple(shape_list), axial_dim)
    dropped = at_first & (position < rim_width) | at_last & (position >= extent - rim_width)
    return jnp.where(dropped, jnp.float32(0.0), padded)


def radial_pad(values, rim_width, radial_mode):
    return jnp.pad(
        values, [(0, 0)] * (values.ndim - 1) + [(rim_width, rim_width)], mode=radial_mode
    )


def transport(scalar_pad, vel_pad, density_pad, density_rim, diffusion, step_size):
    center = shifted(scalar_pad, 2, 0, 0)
    density = shifted(density_pad, density_rim, 0, 0)
    change = jnp.zeros_like(center)
    for direction in range(3):
        carried = vel_pad[direction] * scalar_pad
        advect = (
            -shifted(carried, 2, direction, 2)
            + 8.0 * shifted(carried, 2, direction, 1)
            - 8.0 * shifted(carried, 2, direction, -1)
            + shifted(carried, 2, direction, -2)
        ) / 12.0
        upper_flux = (
            0.5
            * diffusion
            * (density + shifted(density_pad, density_rim, direction, 1))
            * (shifted(scalar_pad, 2, direction, 1) - center)
        )
        lower_flux = (
            0.5
            * diffusion
            * (density + shifted(density_pad, density_rim, direction, -1))
            * (center - shifted(scalar_pad, 2, direction, -1))
        )
        change = change - advect + upper_flux - lower_flux
    return center + step_size * change


def evaporate(attrs, gas_values, alive_mask, step_size):
    parcel_mass = attrs[0]
    parcel_temp = attrs[1]
    parcel_vel = attrs[2:5]
    offsets = attrs[5:8]
    gas_heat = gas_values[3]
    gas_fuel = gas_values[4]
    evap_rate = EVAP * jax.nn.softplus(gas_heat - parcel_temp) * (1.0 - gas_fuel)
    new_mass = parcel_mass * jnp.exp(-step_size * evap_rate)
    lost_mass = parcel_mass - new_mass
    new_temp = parcel_temp + step_size * RELAX * (gas_heat - parcel_temp)
    new_vel = parcel_vel + step_size * DRAG * (gas_values[0:3] - parcel_vel)
    new_offsets = offsets + step_size * new_vel
    heat_source = -LATENT * lost_mass - HEAT_CAP * new_mass * (new_temp - parcel_temp)
    new_attrs = (
        jnp.concatenate([new_mass[None], new_temp[None], new_vel, new_offsets], axis=0)
        * alive_mask[None]
    )
    sources = jnp.stack([heat_source * alive_mask, lost_mass * alive_mask])
    return (new_attrs, sources)


def pressure_pad(values):
    padded = extended(values, (("axial", 0), ("azim", 1)), 1)
    return radial_pad(clear_ends(padded, 1, 0), 1, "constant")


def operate(values):
    padded = pressure_pad(values)
    beside = shifted(padded, 1, 0, 1) + shifted(padded, 1, 0, -1)
    beside = beside + shifted(padded, 1, 1, 1) + shifted(padded, 1, 1, -1)
    beside = beside + shifted(padded, 1, 2, 1) + shifted(padded, 1, 2, -1)
    return (6.0 + SHIFT_PRESSURE) * values - beside


def reduce_groups():
    axial = lax.axis_size("axial")
    along_x = 4 if axial % 4 == 0 else 1
    groups = [("azim", 1, lax.axis_size("azim")), ("axial", 1, along_x), ("axial", along_x, axial // along_x)]
    return [group for group in groups if group[2] > 1]


def coefficient_cg(gram, size, shift, half_width):
    def apply_a(c):
        out = [shift * c[j] for j in range(size)]
        for j in range(size - 1):
            if j == 0:
                out[1] = out[1] + half_width * c[0]
            else:
                out[j + 1] = out[j + 1] + 0.5 * half_width * c[j]
                out[j - 1] = out[j - 1] + 0.5 * half_width * c[j]
        return out

    def inner(a, b):
        acc = None
        for i in range(size):
            for j in range(size):
                if isinstance(a[i], float) and a[i] == 0.0:
                    continue
                if isinstance(b[j], float) and b[j] == 0.0:
                    continue
                term = a[i] * gram[i][j] * b[j]
                acc = term if acc is None else acc + term
        return acc

    solution_c = [0.0] * size
    residual = [1.0] + [0.0] * (size - 1)
    search = list(residual)
    norm_now = inner(residual, residual)
    for iteration in range(ITERS):
        image = apply_a(search)
        alpha = norm_now / inner(search, image)
        solution_c = [solution_c[j] + alpha * search[j] for j in range(size)]
        residual = [residual[j] - alpha * image[j] for j in range(size)]
        if iteration == ITERS - 1:
            break
        norm_next = inner(residual, residual)
        search = [residual[j] + norm_next / norm_now * search[j] for j in range(size)]
        norm_now = norm_next
    return solution_c


def reduce_kernel(groups, shift, half_width, vel_ref, *refs):
    size = ITERS + 1
    basis_refs = refs[:size]
    o_ref, slots, send_sems, recv_sems = refs[size:]
    here = {"axial": lax.axis_index("axial"), "azim": lax.axis_index("azim")}

    def member(axis, stride, count, m):
        index = here[axis]
        base = index - ((index // stride) % count) * stride
        coords = dict(here)
        coords[axis] = base + m * stride
        return (coords["axial"], coords["azim"])

    def position(axis, stride, count):
        return (here[axis] // stride) % count

    barrier = pltpu.get_barrier_semaphore()
    greeted = 0
    for axis, stride, count in groups:
        mine = position(axis, stride, count)
        for m in range(1, count):
            pl.semaphore_signal(
                barrier,
                inc=1,
                device_id=member(axis, stride, count, (mine + m) % count),
                device_id_type=pl.DeviceIdType.MESH,
            )
            greeted += 1
    pl.semaphore_wait(barrier, greeted)
    row = lax.broadcasted_iota(jnp.int32, o_ref.shape, 0)
    lane = lax.broadcasted_iota(jnp.int32, o_ref.shape, 1)
    is_max = (row == 0) & (lane == 0)

    def total(x):
        return jnp.sum(jnp.sum(x, axis=0, keepdims=True), axis=1, keepdims=True)

    basis = [ref[...] for ref in basis_refs]
    pairs = [(i, j) for i in range(size) for j in range(i, size)]
    entries = [jnp.max(jnp.max(jnp.abs(vel_ref[...]), axis=0, keepdims=True), axis=1, keepdims=True)]
    entries += [total(basis[i] * basis[j]) for i, j in pairs]
    acc = jnp.zeros(o_ref.shape, jnp.float32)
    for n, entry in enumerate(entries):
        acc = jnp.where((row == 0) & (lane == n), entry, acc)
    offset = 0
    for axis, stride, count in groups:
        mine = position(axis, stride, count)
        slots[offset + mine] = acc
        copies = []
        for m in range(1, count):
            target = (mine + m) % count
            copy = pltpu.make_async_remote_copy(
                src_ref=slots.at[offset + mine],
                dst_ref=slots.at[offset + mine],
                send_sem=send_sems.at[offset + target],
                recv_sem=recv_sems.at[offset + mine],
                device_id=member(axis, stride, count, target),
                device_id_type=pl.DeviceIdType.MESH,
            )
            copy.start()
            copies.append(copy)
        for copy in copies:
            copy.wait_send()
        for m in range(count):
            incoming = pltpu.make_async_remote_copy(
                src_ref=slots.at[offset + m],
                dst_ref=slots.at[offset + m],
                send_sem=send_sems.at[offset + m],
                recv_sem=recv_sems.at[offset + m],
                device_id=member(axis, stride, count, m),
                device_id_type=pl.DeviceIdType.MESH,
            )

            @pl.when(m != mine)
            def _():
                incoming.wait_recv()

        combined = slots[offset]
        for m in range(1, count):
            other = slots[offset + m]
            combined = jnp.where(is_max, jnp.maximum(combined, other), combined + other)
        acc = combined
        offset += count
    first = acc[0:1, :]
    first_lane = lax.broadcasted_iota(jnp.int32, first.shape, 1)

    def entry_at(n):
        return jnp.sum(jnp.where(first_lane == n, first, 0.0), axis=1, keepdims=True)

    gram = [[None] * size for _ in range(size)]
    for n, (i, j) in enumerate(pairs):
        gram[i][j] = entry_at(n + 1)
        gram[j][i] = gram[i][j]
    coefficients = coefficient_cg(gram, size, shift, half_width)
    out = jnp.where(lane == ITERS, entry_at(0), 0.0)
    for j in range(ITERS):
        out = jnp.where((lane == j), coefficients[j], out)
    o_ref[...] = out


def pressure_coefficients(velocity, basis, shift, half_width):
    groups = reduce_groups()
    slot_count = sum(count for _, _, count in groups)
    flat = [v.reshape(-1, v.shape[-1]) for v in basis]
    out = pl.pallas_call(
        lambda *refs: reduce_kernel(groups, shift, half_width, *refs),
        out_shape=jax.ShapeDtypeStruct((8, 128), jnp.float32),
        in_specs=[pl.BlockSpec(memory_space=pltpu.VMEM)] * (1 + len(flat)),
        out_specs=pl.BlockSpec(memory_space=pltpu.VMEM),
        scratch_shapes=[
            pltpu.VMEM((slot_count, 8, 128), jnp.float32),
            pltpu.SemaphoreType.DMA((slot_count,)),
            pltpu.SemaphoreType.DMA((slot_count,)),
        ],
        compiler_params=pltpu.CompilerParams(collective_id=0, has_side_effects=True),
    )(velocity.reshape(-1, velocity.shape[-1]), *flat)
    return [out[0, j] for j in range(ITERS)], out[0, ITERS]


def neighbour_sum(padded):
    beside = shifted(padded, 1, 0, 1) + shifted(padded, 1, 0, -1)
    beside = beside + shifted(padded, 1, 1, 1) + shifted(padded, 1, 1, -1)
    return beside + shifted(padded, 1, 2, 1) + shifted(padded, 1, 2, -1)


def axial_valid(values, rim):
    extent = values.shape[0]
    inner_x = extent - 2 * rim
    first = lax.axis_index("axial") * inner_x - rim
    position = first + lax.broadcasted_iota(jnp.int32, (extent, 1, 1), 0)
    inside = (position >= 0) & (position < inner_x * lax.axis_size("axial"))
    return jnp.where(inside, values, jnp.float32(0.0))


def crop(values, by):
    if by == 0:
        return values
    return values[by:-by, by:-by]


def neighbour_sum_wide(values):
    padded = jnp.pad(values, [(0, 0), (0, 0), (1, 1)])
    nx, ny, nz = padded.shape

    def at(dx, dy, dz):
        return padded[1 + dx : nx - 1 + dx, 1 + dy : ny - 1 + dy, 1 + dz : nz - 1 + dz]

    beside = at(1, 0, 0) + at(-1, 0, 0)
    beside = beside + at(0, 1, 0) + at(0, -1, 0)
    return beside + at(0, 0, 1) + at(0, 0, -1)


def solve_pressure(wide_velocity, velocity):
    half_width = 6.0
    u = wide_velocity
    divergence = 0.5 * (u[0, 2:, 1:-1, 1:-1] - u[0, :-2, 1:-1, 1:-1])
    divergence = divergence + 0.5 * (u[1, 1:-1, 2:, 1:-1] - u[1, 1:-1, :-2, 1:-1])
    divergence = divergence + 0.5 * (u[2, 1:-1, 1:-1, 2:] - u[2, 1:-1, 1:-1, :-2])
    basis = [axial_valid(divergence, ITERS)]
    for j in range(ITERS):
        scaled = neighbour_sum_wide(basis[j]) * (-1.0 / half_width)
        if j == 0:
            fresh = scaled
        else:
            fresh = 2.0 * scaled - crop(basis[j - 1], 2)
        basis.append(axial_valid(fresh, ITERS - 1 - j))
    interior = [crop(basis[j], ITERS - j) for j in range(ITERS + 1)]
    coefficients, fastest = pressure_coefficients(
        velocity, interior, 6.0 + SHIFT_PRESSURE, half_width
    )
    padded_basis = [radial_pad(crop(basis[j], ITERS - j - 1), 1, "constant") for j in range(ITERS)]
    padded_pressure = coefficients[0] * padded_basis[0]
    for j in range(1, ITERS):
        padded_pressure = padded_pressure + coefficients[j] * padded_basis[j]
    return padded_pressure, fastest


def along_axial(buffer, step_by):
    return shifted_2(buffer, "axial", step_by)


def along_azim(buffer, step_by):
    return shifted_3(buffer, "azim", step_by)


def on_device(state, diff_coef, parcel_state, parcel_cell, parcel_dest, live_count):
    velocity = state[1:4]
    npar_local = parcel_cell.shape[0]
    cells_x, cells_y, cells_z = (state.shape[1], state.shape[2], state.shape[3])
    plane_count = cells_x * cells_y
    gas_table = jnp.transpose(state[1:6].reshape(5, plane_count, cells_z), (1, 0, 2)).reshape(
        plane_count, 5 * cells_z
    )
    live_now = live_count[0]
    slot_alive = jnp.arange(npar_local) < live_now
    alive_mask = slot_alive.astype(jnp.float32)
    plane_ids = parcel_cell // cells_z
    radial_ids = parcel_cell % cells_z
    plane_hot = (plane_ids[:, None] == jnp.arange(plane_count)[None, :]).astype(jnp.float32)
    radial_hot = (radial_ids[:, None] == jnp.arange(cells_z)[None, :]).astype(jnp.float32)
    gas_rows = jnp.dot(plane_hot, gas_table, precision=HIGHEST).reshape(npar_local, 5, cells_z)
    gas_values = jnp.sum(gas_rows * radial_hot[:, None, :], axis=2).T
    stacked = jnp.stack([(parcel_dest == d + 1) & slot_alive for d in range(4)]).astype(jnp.int32)
    ranks = jnp.cumsum(stacked, axis=1) - 1
    mover = jnp.sum(stacked, axis=0) > 0
    target = jnp.where(mover, jnp.sum(stacked * (jnp.arange(4)[:, None] * CAP + ranks), axis=0), -1)
    select = (target[:, None] == jnp.arange(4 * CAP)[None, :]).astype(jnp.float32)
    raw = jnp.concatenate([parcel_state, gas_values, alive_mask[None]], axis=0)
    leaving = jnp.transpose(
        jnp.dot(raw, select, precision=HIGHEST).reshape(raw.shape[0], 4, CAP), (1, 0, 2)
    )
    parcel_steps = [(-1, 0), (1, 0), (0, -1), (0, 1)]
    faces = [(sa, sz) for sa, sz in NEIGHBOURS if sa == 0 or sz == 0]

    def outgoing(block, width, sa, sz):
        slab = rim_slab(block, width, sa, sz)
        return jnp.swapaxes(slab, 1, 2) if sa == 0 else slab

    def incoming(slab, sa):
        return jnp.swapaxes(slab, 1, 2) if sa == 0 else slab

    rim = ITERS + 1
    items = [(outgoing(state, 2, sa, sz), (sa, sz)) for sa, sz in faces]
    items += [(outgoing(velocity, rim, sa, sz), (sa, sz)) for sa, sz in NEIGHBOURS]
    items += [(leaving[d], parcel_steps[d]) for d in range(4)]
    got = neighbour_exchange(items)
    count = len(faces)
    state_rims = {(-sa, -sz): incoming(got[k], sa) for k, (sa, sz) in enumerate(faces)}
    velocity_rims = {
        (-sa, -sz): incoming(got[count + k], sa) for k, (sa, sz) in enumerate(NEIGHBOURS)
    }
    landed = got[count + len(NEIGHBOURS) :]
    whole_pad = assemble(state, state_rims)
    whole_pad = radial_pad(clear_ends(whole_pad, 2, 1), 2, "edge")
    moving = whole_pad[1:]
    density_pad = whole_pad[0]
    density_rim = 2
    vel_pad = moving[0:3]
    wide_velocity = assemble(velocity, velocity_rims)
    wide_velocity = radial_pad(clear_ends(wide_velocity, rim, 1), 1, "edge")
    padded_pressure, fastest = solve_pressure(wide_velocity, velocity)
    step_size = CFL / (fastest + 1e-06)
    transported = transport(
        moving[3:], vel_pad, density_pad, density_rim, diff_coef[:, None, None, None], step_size
    )
    updated, sources = evaporate(parcel_state, gas_values, alive_mask, step_size)
    spread = (sources.T[:, :, None] * radial_hot[:, None, :]).reshape(npar_local, 2 * cells_z)
    deposit = lax.dot_general(plane_hot, spread, (((0,), (0,)), ((), ())), precision=HIGHEST)
    deposit = jnp.transpose(deposit.reshape(cells_x, cells_y, 2, cells_z), (2, 0, 1, 3))
    scalars_new = jnp.concatenate(
        [transported[:2] + deposit / state[0][None], transported[2:]], axis=0
    )
    at_first = lax.axis_index("axial") == 0
    at_last = lax.axis_index("axial") == lax.axis_size("axial") - 1
    arriving = []
    for d in range(4):
        payload = landed[d]
        if d == 0:
            payload = jnp.where(at_last, jnp.float32(0.0), payload)
        if d == 1:
            payload = jnp.where(at_first, jnp.float32(0.0), payload)
        moved, _ = evaporate(payload[:8], payload[8:13], payload[13], step_size)
        arriving.append(moved)
    arrived = jnp.stack(arriving)
    kept_parcels = jnp.where((parcel_dest == 0)[None], updated, jnp.float32(0.0))
    velocity_new = jnp.stack(
        [
            velocity[d]
            - 0.5 * (shifted(padded_pressure, 1, d, 1) - shifted(padded_pressure, 1, d, -1))
            for d in range(3)
        ]
    )
    return (scalars_new, velocity_new, kept_parcels, arrived)


def solution(mesh):
    in_specs = (
        P(None, "axial", "azim", None),
        P(),
        P(None, ("axial", "azim")),
        P(("axial", "azim")),
        P(("axial", "azim")),
        P(("axial", "azim")),
    )
    out_specs = (
        P(None, "axial", "azim", None),
        P(None, "axial", "azim", None),
        P(None, ("axial", "azim")),
        P(None, None, ("axial", "azim")),
    )
    return jax.shard_map(
        on_device, mesh=mesh, in_specs=in_specs, out_specs=out_specs, check_vma=False
    )
```

```python
import jax
import jax.numpy as jnp
from jax import lax
from jax.sharding import PartitionSpec as P
from jax.experimental import pallas as pl
from jax.experimental.pallas import tpu as pltpu

CAP = 64
ITERS = 4


CFL = 0.4
SHIFT_PRESSURE = 0.25
EVAP = 8.0
RELAX = 4.0
DRAG = 6.0
LATENT = 0.5
HEAT_CAP = 0.8
HIGHEST = lax.Precision.HIGHEST


def extended(block, sides, width):
    for axis, dim in sides:
        count = lax.axis_size(axis)
        forward = [(i, i + 1) for i in range(count - 1)]
        forward.append((count - 1, 0))
        backward = [(target, source) for source, target in forward]
        low = lax.ppermute(
            lax.slice_in_dim(block, block.shape[dim] - width, None, axis=dim), axis, forward
        )
        high = lax.ppermute(lax.slice_in_dim(block, 0, width, axis=dim), axis, backward)
        block = jnp.concatenate([low, block, high], axis=dim)
    return block


def exchange_kernel(offsets, *refs):
    count = len(offsets)
    sources = refs[:count]
    outs = refs[count : 2 * count]
    landing = refs[2 * count : 3 * count]
    send_sems, recv_sems = refs[3 * count :]
    axial = lax.axis_index("axial")
    azim = lax.axis_index("azim")

    def device(step_axial, step_azim):
        return (
            (axial + step_axial + lax.axis_size("axial")) % lax.axis_size("axial"),
            (azim + step_azim + lax.axis_size("azim")) % lax.axis_size("azim"),
        )

    neighbours = sorted(set(offsets))
    barrier = pltpu.get_barrier_semaphore()
    for step in neighbours:
        pl.semaphore_signal(
            barrier, inc=1, device_id=device(*step), device_id_type=pl.DeviceIdType.MESH
        )
    pl.semaphore_wait(barrier, len(neighbours))
    copies = []
    for k, step in enumerate(offsets):
        copy = pltpu.make_async_remote_copy(
            src_ref=sources[k],
            dst_ref=landing[k],
            send_sem=send_sems.at[k],
            recv_sem=recv_sems.at[k],
            device_id=device(*step),
            device_id_type=pl.DeviceIdType.MESH,
        )
        copy.start()
        copies.append(copy)
    for k, copy in enumerate(copies):
        copy.wait()
        outs[k][...] = landing[k][...]


def neighbour_exchange(items):
    offsets = [step for _, step in items]
    flat = [a for a, _ in items]
    count = len(flat)
    outs = pl.pallas_call(
        lambda *refs: exchange_kernel(offsets, *refs),
        out_shape=[jax.ShapeDtypeStruct(f.shape, f.dtype) for f in flat],
        in_specs=[pl.BlockSpec(memory_space=pltpu.VMEM)] * count,
        out_specs=[pl.BlockSpec(memory_space=pltpu.VMEM)] * count,
        scratch_shapes=[pltpu.VMEM(f.shape, f.dtype) for f in flat]
        + [pltpu.SemaphoreType.DMA((count,)), pltpu.SemaphoreType.DMA((count,))],
        compiler_params=pltpu.CompilerParams(collective_id=1, has_side_effects=True),
    )(*flat)
    return list(outs)


def rim_slab(block, width, step_axial, step_azim):
    def pick(values, dim, step):
        if step > 0:
            return lax.slice_in_dim(values, values.shape[dim] - width, None, axis=dim)
        if step < 0:
            return lax.slice_in_dim(values, 0, width, axis=dim)
        return values

    return pick(pick(block, 1, step_axial), 2, step_azim)


NEIGHBOURS = [(sa, sz) for sa in (-1, 0, 1) for sz in (-1, 0, 1) if (sa, sz) != (0, 0)]


def assemble(block, received):
    rim_a = received[(-1, 0)].shape[1]
    rim_z = received[(0, -1)].shape[2]
    corner = block.shape[:1] + (rim_a, rim_z) + block.shape[3:]
    bands = []
    for pz in (-1, 0, 1):
        row = []
        for pa in (-1, 0, 1):
            if (pa, pz) == (0, 0):
                row.append(block)
            elif (pa, pz) in received:
                row.append(received[(pa, pz)])
            else:
                row.append(jnp.zeros(corner, block.dtype))
        bands.append(jnp.concatenate(row, axis=1))
    return jnp.concatenate(bands, axis=2)


def shifted_2(shard, axis, by):
    length = lax.axis_size(axis)
    pairs = [(i, i + by) for i in range(length) if 0 <= i + by < length]
    return lax.ppermute(shard, axis, pairs)


def shifted_3(shard, axis, by):
    length = lax.axis_size(axis)
    return lax.ppermute(shard, axis, [(i, (i + by) % length) for i in range(length)])


def shifted(padded, rim_width, direction, step_by):
    selector = []
    total_dims = padded.ndim
    for dim_index in range(total_dims):
        extent = padded.shape[dim_index]
        if dim_index == total_dims - 3 + direction:
            selector.append(slice(rim_width + step_by, extent - rim_width + step_by))
        elif dim_index >= total_dims - 3:
            selector.append(slice(rim_width, extent - rim_width))
        else:
            selector.append(slice(None))
    return padded[tuple(selector)]


def clear_ends(padded, rim_width, axial_dim):
    extent = padded.shape[axial_dim]
    at_first = lax.axis_index("axial") == 0
    at_last = lax.axis_index("axial") == lax.axis_size("axial") - 1
    shape_list = [1] * padded.ndim
    shape_list[axial_dim] = extent
    position = lax.broadcasted_iota(jnp.int32, tuple(shape_list), axial_dim)
    dropped = at_first & (position < rim_width) | at_last & (position >= extent - rim_width)
    return jnp.where(dropped, jnp.float32(0.0), padded)


def radial_pad(values, rim_width, radial_mode):
    return jnp.pad(
        values, [(0, 0)] * (values.ndim - 1) + [(rim_width, rim_width)], mode=radial_mode
    )


def transport(scalar_pad, vel_pad, density_pad, density_rim, diffusion, step_size):
    center = shifted(scalar_pad, 2, 0, 0)
    density = shifted(density_pad, density_rim, 0, 0)
    change = jnp.zeros_like(center)
    for direction in range(3):
        carried = vel_pad[direction] * scalar_pad
        advect = (
            -shifted(carried, 2, direction, 2)
            + 8.0 * shifted(carried, 2, direction, 1)
            - 8.0 * shifted(carried, 2, direction, -1)
            + shifted(carried, 2, direction, -2)
        ) / 12.0
        upper_flux = (
            0.5
            * diffusion
            * (density + shifted(density_pad, density_rim, direction, 1))
            * (shifted(scalar_pad, 2, direction, 1) - center)
        )
        lower_flux = (
            0.5
            * diffusion
            * (density + shifted(density_pad, density_rim, direction, -1))
            * (center - shifted(scalar_pad, 2, direction, -1))
        )
        change = change - advect + upper_flux - lower_flux
    return center + step_size * change


def evaporate(attrs, gas_values, alive_mask, step_size):
    parcel_mass = attrs[0]
    parcel_temp = attrs[1]
    parcel_vel = attrs[2:5]
    offsets = attrs[5:8]
    gas_heat = gas_values[3]
    gas_fuel = gas_values[4]
    evap_rate = EVAP * jax.nn.softplus(gas_heat - parcel_temp) * (1.0 - gas_fuel)
    new_mass = parcel_mass * jnp.exp(-step_size * evap_rate)
    lost_mass = parcel_mass - new_mass
    new_temp = parcel_temp + step_size * RELAX * (gas_heat - parcel_temp)
    new_vel = parcel_vel + step_size * DRAG * (gas_values[0:3] - parcel_vel)
    new_offsets = offsets + step_size * new_vel
    heat_source = -LATENT * lost_mass - HEAT_CAP * new_mass * (new_temp - parcel_temp)
    new_attrs = (
        jnp.concatenate([new_mass[None], new_temp[None], new_vel, new_offsets], axis=0)
        * alive_mask[None]
    )
    sources = jnp.stack([heat_source * alive_mask, lost_mass * alive_mask])
    return (new_attrs, sources)


def pressure_pad(values):
    padded = extended(values, (("axial", 0), ("azim", 1)), 1)
    return radial_pad(clear_ends(padded, 1, 0), 1, "constant")


def operate(values):
    padded = pressure_pad(values)
    beside = shifted(padded, 1, 0, 1) + shifted(padded, 1, 0, -1)
    beside = beside + shifted(padded, 1, 1, 1) + shifted(padded, 1, 1, -1)
    beside = beside + shifted(padded, 1, 2, 1) + shifted(padded, 1, 2, -1)
    return (6.0 + SHIFT_PRESSURE) * values - beside


def reduce_groups():
    axial = lax.axis_size("axial")
    along_x = 4 if axial % 4 == 0 else 1
    groups = [("azim", 1, lax.axis_size("azim")), ("axial", 1, along_x), ("axial", along_x, axial // along_x)]
    return [group for group in groups if group[2] > 1]


def coefficient_cg(gram, size, shift, half_width):
    def apply_a(c):
        out = [shift * c[j] for j in range(size)]
        for j in range(size - 1):
            if j == 0:
                out[1] = out[1] + half_width * c[0]
            else:
                out[j + 1] = out[j + 1] + 0.5 * half_width * c[j]
                out[j - 1] = out[j - 1] + 0.5 * half_width * c[j]
        return out

    def inner(a, b):
        acc = None
        for i in range(size):
            for j in range(size):
                if isinstance(a[i], float) and a[i] == 0.0:
                    continue
                if isinstance(b[j], float) and b[j] == 0.0:
                    continue
                term = a[i] * gram[i][j] * b[j]
                acc = term if acc is None else acc + term
        return acc

    solution_c = [0.0] * size
    residual = [1.0] + [0.0] * (size - 1)
    search = list(residual)
    norm_now = inner(residual, residual)
    for iteration in range(ITERS):
        image = apply_a(search)
        alpha = norm_now / inner(search, image)
        solution_c = [solution_c[j] + alpha * search[j] for j in range(size)]
        residual = [residual[j] - alpha * image[j] for j in range(size)]
        if iteration == ITERS - 1:
            break
        norm_next = inner(residual, residual)
        search = [residual[j] + norm_next / norm_now * search[j] for j in range(size)]
        norm_now = norm_next
    return solution_c


def reduce_kernel(groups, shift, half_width, vel_ref, *refs):
    size = ITERS + 1
    basis_refs = refs[:size]
    o_ref, slots, send_sems, recv_sems = refs[size:]
    here = {"axial": lax.axis_index("axial"), "azim": lax.axis_index("azim")}

    def member(axis, stride, count, m):
        index = here[axis]
        base = index - ((index // stride) % count) * stride
        coords = dict(here)
        coords[axis] = base + m * stride
        return (coords["axial"], coords["azim"])

    def position(axis, stride, count):
        return (here[axis] // stride) % count

    barrier = pltpu.get_barrier_semaphore()
    greeted = 0
    for axis, stride, count in groups:
        mine = position(axis, stride, count)
        for m in range(1, count):
            pl.semaphore_signal(
                barrier,
                inc=1,
                device_id=member(axis, stride, count, (mine + m) % count),
                device_id_type=pl.DeviceIdType.MESH,
            )
            greeted += 1
    pl.semaphore_wait(barrier, greeted)
    row = lax.broadcasted_iota(jnp.int32, o_ref.shape, 0)
    lane = lax.broadcasted_iota(jnp.int32, o_ref.shape, 1)
    is_max = (row == 0) & (lane == 0)

    def total(x):
        return jnp.sum(jnp.sum(x, axis=0, keepdims=True), axis=1, keepdims=True)

    basis = [ref[...] for ref in basis_refs]
    pairs = [(i, j) for i in range(size) for j in range(i, size)]
    entries = [jnp.max(jnp.max(jnp.abs(vel_ref[...]), axis=0, keepdims=True), axis=1, keepdims=True)]
    entries += [total(basis[i] * basis[j]) for i, j in pairs]
    acc = jnp.zeros(o_ref.shape, jnp.float32)
    for n, entry in enumerate(entries):
        acc = jnp.where((row == 0) & (lane == n), entry, acc)
    offset = 0
    for axis, stride, count in groups:
        mine = position(axis, stride, count)
        slots[offset + mine] = acc
        copies = []
        for m in range(1, count):
            target = (mine + m) % count
            copy = pltpu.make_async_remote_copy(
                src_ref=slots.at[offset + mine],
                dst_ref=slots.at[offset + mine],
                send_sem=send_sems.at[offset + target],
                recv_sem=recv_sems.at[offset + mine],
                device_id=member(axis, stride, count, target),
                device_id_type=pl.DeviceIdType.MESH,
            )
            copy.start()
            copies.append(copy)
        for copy in copies:
            copy.wait_send()
        for m in range(count):
            incoming = pltpu.make_async_remote_copy(
                src_ref=slots.at[offset + m],
                dst_ref=slots.at[offset + m],
                send_sem=send_sems.at[offset + m],
                recv_sem=recv_sems.at[offset + m],
                device_id=member(axis, stride, count, m),
                device_id_type=pl.DeviceIdType.MESH,
            )

            @pl.when(m != mine)
            def _():
                incoming.wait_recv()

        combined = slots[offset]
        for m in range(1, count):
            other = slots[offset + m]
            combined = jnp.where(is_max, jnp.maximum(combined, other), combined + other)
        acc = combined
        offset += count
    first = acc[0:1, :]
    first_lane = lax.broadcasted_iota(jnp.int32, first.shape, 1)

    def entry_at(n):
        return jnp.sum(jnp.where(first_lane == n, first, 0.0), axis=1, keepdims=True)

    gram = [[None] * size for _ in range(size)]
    for n, (i, j) in enumerate(pairs):
        gram[i][j] = entry_at(n + 1)
        gram[j][i] = gram[i][j]
    coefficients = coefficient_cg(gram, size, shift, half_width)
    out = jnp.where(lane == ITERS, entry_at(0), 0.0)
    for j in range(ITERS):
        out = jnp.where((lane == j), coefficients[j], out)
    o_ref[...] = out


def pressure_coefficients(velocity, basis, shift, half_width):
    groups = reduce_groups()
    slot_count = sum(count for _, _, count in groups)
    flat = [v.reshape(-1, v.shape[-1]) for v in basis]
    out = pl.pallas_call(
        lambda *refs: reduce_kernel(groups, shift, half_width, *refs),
        out_shape=jax.ShapeDtypeStruct((8, 128), jnp.float32),
        in_specs=[pl.BlockSpec(memory_space=pltpu.VMEM)] * (1 + len(flat)),
        out_specs=pl.BlockSpec(memory_space=pltpu.VMEM),
        scratch_shapes=[
            pltpu.VMEM((slot_count, 8, 128), jnp.float32),
            pltpu.SemaphoreType.DMA((slot_count,)),
            pltpu.SemaphoreType.DMA((slot_count,)),
        ],
        compiler_params=pltpu.CompilerParams(collective_id=0, has_side_effects=True),
    )(velocity.reshape(-1, velocity.shape[-1]), *flat)
    return [out[0, j] for j in range(ITERS)], out[0, ITERS]


def neighbour_sum(padded):
    beside = shifted(padded, 1, 0, 1) + shifted(padded, 1, 0, -1)
    beside = beside + shifted(padded, 1, 1, 1) + shifted(padded, 1, 1, -1)
    return beside + shifted(padded, 1, 2, 1) + shifted(padded, 1, 2, -1)


def axial_valid(values, rim):
    extent = values.shape[0]
    inner_x = extent - 2 * rim
    first = lax.axis_index("axial") * inner_x - rim
    position = first + lax.broadcasted_iota(jnp.int32, (extent, 1, 1), 0)
    inside = (position >= 0) & (position < inner_x * lax.axis_size("axial"))
    return jnp.where(inside, values, jnp.float32(0.0))


def crop(values, by):
    if by == 0:
        return values
    return values[by:-by, by:-by]


def neighbour_sum_wide(values):
    padded = jnp.pad(values, [(0, 0), (0, 0), (1, 1)])
    nx, ny, nz = padded.shape

    def at(dx, dy, dz):
        return padded[1 + dx : nx - 1 + dx, 1 + dy : ny - 1 + dy, 1 + dz : nz - 1 + dz]

    beside = at(1, 0, 0) + at(-1, 0, 0)
    beside = beside + at(0, 1, 0) + at(0, -1, 0)
    return beside + at(0, 0, 1) + at(0, 0, -1)


def solve_pressure(wide_velocity, velocity):
    half_width = 6.0
    u = wide_velocity
    divergence = 0.5 * (u[0, 2:, 1:-1, 1:-1] - u[0, :-2, 1:-1, 1:-1])
    divergence = divergence + 0.5 * (u[1, 1:-1, 2:, 1:-1] - u[1, 1:-1, :-2, 1:-1])
    divergence = divergence + 0.5 * (u[2, 1:-1, 1:-1, 2:] - u[2, 1:-1, 1:-1, :-2])
    basis = [axial_valid(divergence, ITERS)]
    for j in range(ITERS):
        scaled = neighbour_sum_wide(basis[j]) * (-1.0 / half_width)
        if j == 0:
            fresh = scaled
        else:
            fresh = 2.0 * scaled - crop(basis[j - 1], 2)
        basis.append(axial_valid(fresh, ITERS - 1 - j))
    interior = [crop(basis[j], ITERS - j) for j in range(ITERS + 1)]
    coefficients, fastest = pressure_coefficients(
        velocity, interior, 6.0 + SHIFT_PRESSURE, half_width
    )
    padded_basis = [radial_pad(crop(basis[j], ITERS - j - 1), 1, "constant") for j in range(ITERS)]
    padded_pressure = coefficients[0] * padded_basis[0]
    for j in range(1, ITERS):
        padded_pressure = padded_pressure + coefficients[j] * padded_basis[j]
    return padded_pressure, fastest


def along_axial(buffer, step_by):
    return shifted_2(buffer, "axial", step_by)


def along_azim(buffer, step_by):
    return shifted_3(buffer, "azim", step_by)


def on_device(state, diff_coef, parcel_state, parcel_cell, parcel_dest, live_count):
    velocity = state[1:4]
    npar_local = parcel_cell.shape[0]
    cells_x, cells_y, cells_z = (state.shape[1], state.shape[2], state.shape[3])
    plane_count = cells_x * cells_y
    gas_table = jnp.transpose(state[1:6].reshape(5, plane_count, cells_z), (1, 0, 2)).reshape(
        plane_count, 5 * cells_z
    )
    live_now = live_count[0]
    slot_alive = jnp.arange(npar_local) < live_now
    alive_mask = slot_alive.astype(jnp.float32)
    plane_ids = parcel_cell // cells_z
    radial_ids = parcel_cell % cells_z
    plane_hot = (plane_ids[:, None] == jnp.arange(plane_count)[None, :]).astype(jnp.float32)
    radial_hot = (radial_ids[:, None] == jnp.arange(cells_z)[None, :]).astype(jnp.float32)
    gas_rows = jnp.dot(plane_hot, gas_table, precision=HIGHEST).reshape(npar_local, 5, cells_z)
    gas_values = jnp.sum(gas_rows * radial_hot[:, None, :], axis=2).T
    stacked = jnp.stack([(parcel_dest == d + 1) & slot_alive for d in range(4)]).astype(jnp.int32)
    ranks = jnp.cumsum(stacked, axis=1) - 1
    mover = jnp.sum(stacked, axis=0) > 0
    target = jnp.where(mover, jnp.sum(stacked * (jnp.arange(4)[:, None] * CAP + ranks), axis=0), -1)
    select = (target[:, None] == jnp.arange(4 * CAP)[None, :]).astype(jnp.float32)
    raw = jnp.concatenate([parcel_state, gas_values, alive_mask[None]], axis=0)
    leaving = jnp.transpose(
        jnp.dot(raw, select, precision=HIGHEST).reshape(raw.shape[0], 4, CAP), (1, 0, 2)
    )
    parcel_steps = [(-1, 0), (1, 0), (0, -1), (0, 1)]
    faces = [(sa, sz) for sa, sz in NEIGHBOURS if sa == 0 or sz == 0]
    items = [(rim_slab(state, 2, sa, sz), (sa, sz)) for sa, sz in faces]
    items += [(rim_slab(velocity, ITERS + 1, sa, sz), (sa, sz)) for sa, sz in NEIGHBOURS]
    items += [(leaving[d], parcel_steps[d]) for d in range(4)]
    got = neighbour_exchange(items)
    count = len(faces)
    state_rims = {(-sa, -sz): got[k] for k, (sa, sz) in enumerate(faces)}
    velocity_rims = {
        (-sa, -sz): got[count + k] for k, (sa, sz) in enumerate(NEIGHBOURS)
    }
    landed = got[count + len(NEIGHBOURS) :]
    whole_pad = assemble(state, state_rims)
    whole_pad = radial_pad(clear_ends(whole_pad, 2, 1), 2, "edge")
    moving = whole_pad[1:]
    density_pad = whole_pad[0]
    density_rim = 2
    vel_pad = moving[0:3]
    wide_velocity = assemble(velocity, velocity_rims)
    wide_velocity = radial_pad(clear_ends(wide_velocity, ITERS + 1, 1), 1, "edge")
    padded_pressure, fastest = solve_pressure(wide_velocity, velocity)
    step_size = CFL / (fastest + 1e-06)
    transported = transport(
        moving[3:], vel_pad, density_pad, density_rim, diff_coef[:, None, None, None], step_size
    )
    updated, sources = evaporate(parcel_state, gas_values, alive_mask, step_size)
    spread = (sources.T[:, :, None] * radial_hot[:, None, :]).reshape(npar_local, 2 * cells_z)
    deposit = lax.dot_general(plane_hot, spread, (((0,), (0,)), ((), ())), precision=HIGHEST)
    deposit = jnp.transpose(deposit.reshape(cells_x, cells_y, 2, cells_z), (2, 0, 1, 3))
    scalars_new = jnp.concatenate(
        [transported[:2] + deposit / state[0][None], transported[2:]], axis=0
    )
    at_first = lax.axis_index("axial") == 0
    at_last = lax.axis_index("axial") == lax.axis_size("axial") - 1
    arriving = []
    for d in range(4):
        payload = landed[d]
        if d == 0:
            payload = jnp.where(at_last, jnp.float32(0.0), payload)
        if d == 1:
            payload = jnp.where(at_first, jnp.float32(0.0), payload)
        moved, _ = evaporate(payload[:8], payload[8:13], payload[13], step_size)
        arriving.append(moved)
    arrived = jnp.stack(arriving)
    kept_parcels = jnp.where((parcel_dest == 0)[None], updated, jnp.float32(0.0))
    velocity_new = jnp.stack(
        [
            velocity[d]
            - 0.5 * (shifted(padded_pressure, 1, d, 1) - shifted(padded_pressure, 1, d, -1))
            for d in range(3)
        ]
    )
    return (scalars_new, velocity_new, kept_parcels, arrived)


def solution(mesh):
    in_specs = (
        P(None, "axial", "azim", None),
        P(),
        P(None, ("axial", "azim")),
        P(("axial", "azim")),
        P(("axial", "azim")),
        P(("axial", "azim")),
    )
    out_specs = (
        P(None, "axial", "azim", None),
        P(None, "axial", "azim", None),
        P(None, ("axial", "azim")),
        P(None, None, ("axial", "azim")),
    )
    return jax.shard_map(
        on_device, mesh=mesh, in_specs=in_specs, out_specs=out_specs, check_vma=False
    )
```

```python
import jax
import jax.numpy as jnp
from jax import lax
from jax.sharding import PartitionSpec as P
from jax.experimental import pallas as pl
from jax.experimental.pallas import tpu as pltpu

CAP = 64
ITERS = 4


CFL = 0.4
SHIFT_PRESSURE = 0.25
EVAP = 8.0
RELAX = 4.0
DRAG = 6.0
LATENT = 0.5
HEAT_CAP = 0.8
HIGHEST = lax.Precision.HIGHEST


def extended(block, sides, width):
    for axis, dim in sides:
        count = lax.axis_size(axis)
        forward = [(i, i + 1) for i in range(count - 1)]
        forward.append((count - 1, 0))
        backward = [(target, source) for source, target in forward]
        low = lax.ppermute(
            lax.slice_in_dim(block, block.shape[dim] - width, None, axis=dim), axis, forward
        )
        high = lax.ppermute(lax.slice_in_dim(block, 0, width, axis=dim), axis, backward)
        block = jnp.concatenate([low, block, high], axis=dim)
    return block


def exchange_kernel(offsets, *refs):
    count = len(offsets)
    sources = refs[:count]
    outs = refs[count : 2 * count]
    send_sems, recv_sems = refs[2 * count :]
    axial = lax.axis_index("axial")
    azim = lax.axis_index("azim")

    def device(step_axial, step_azim):
        return (
            (axial + step_axial + lax.axis_size("axial")) % lax.axis_size("axial"),
            (azim + step_azim + lax.axis_size("azim")) % lax.axis_size("azim"),
        )

    neighbours = sorted(set(offsets))
    barrier = pltpu.get_barrier_semaphore()
    for step in neighbours:
        pl.semaphore_signal(
            barrier, inc=1, device_id=device(*step), device_id_type=pl.DeviceIdType.MESH
        )
    pl.semaphore_wait(barrier, len(neighbours))
    copies = []
    for k, step in enumerate(offsets):
        copy = pltpu.make_async_remote_copy(
            src_ref=sources[k],
            dst_ref=outs[k],
            send_sem=send_sems.at[k],
            recv_sem=recv_sems.at[k],
            device_id=device(*step),
            device_id_type=pl.DeviceIdType.MESH,
        )
        copy.start()
        copies.append(copy)
    for copy in copies:
        copy.wait()


def neighbour_exchange(items):
    offsets = [step for _, step in items]
    flat = [a for a, _ in items]
    count = len(flat)
    outs = pl.pallas_call(
        lambda *refs: exchange_kernel(offsets, *refs),
        out_shape=[jax.ShapeDtypeStruct(f.shape, f.dtype) for f in flat],
        in_specs=[pl.BlockSpec(memory_space=pl.ANY)] * count,
        out_specs=[pl.BlockSpec(memory_space=pl.ANY)] * count,
        scratch_shapes=[pltpu.SemaphoreType.DMA((count,)), pltpu.SemaphoreType.DMA((count,))],
        compiler_params=pltpu.CompilerParams(collective_id=1, has_side_effects=True),
    )(*flat)
    return list(outs)


def rim_slab(block, width, step_axial, step_azim):
    def pick(values, dim, step):
        if step > 0:
            return lax.slice_in_dim(values, values.shape[dim] - width, None, axis=dim)
        if step < 0:
            return lax.slice_in_dim(values, 0, width, axis=dim)
        return values

    return pick(pick(block, 1, step_axial), 2, step_azim)


NEIGHBOURS = [(sa, sz) for sa in (-1, 0, 1) for sz in (-1, 0, 1) if (sa, sz) != (0, 0)]


def assemble(block, received):
    rim_a = received[(-1, 0)].shape[1]
    rim_z = received[(0, -1)].shape[2]
    corner = block.shape[:1] + (rim_a, rim_z) + block.shape[3:]
    bands = []
    for pz in (-1, 0, 1):
        row = []
        for pa in (-1, 0, 1):
            if (pa, pz) == (0, 0):
                row.append(block)
            elif (pa, pz) in received:
                row.append(received[(pa, pz)])
            else:
                row.append(jnp.zeros(corner, block.dtype))
        bands.append(jnp.concatenate(row, axis=1))
    return jnp.concatenate(bands, axis=2)


def shifted_2(shard, axis, by):
    length = lax.axis_size(axis)
    pairs = [(i, i + by) for i in range(length) if 0 <= i + by < length]
    return lax.ppermute(shard, axis, pairs)


def shifted_3(shard, axis, by):
    length = lax.axis_size(axis)
    return lax.ppermute(shard, axis, [(i, (i + by) % length) for i in range(length)])


def shifted(padded, rim_width, direction, step_by):
    selector = []
    total_dims = padded.ndim
    for dim_index in range(total_dims):
        extent = padded.shape[dim_index]
        if dim_index == total_dims - 3 + direction:
            selector.append(slice(rim_width + step_by, extent - rim_width + step_by))
        elif dim_index >= total_dims - 3:
            selector.append(slice(rim_width, extent - rim_width))
        else:
            selector.append(slice(None))
    return padded[tuple(selector)]


def clear_ends(padded, rim_width, axial_dim):
    extent = padded.shape[axial_dim]
    at_first = lax.axis_index("axial") == 0
    at_last = lax.axis_index("axial") == lax.axis_size("axial") - 1
    shape_list = [1] * padded.ndim
    shape_list[axial_dim] = extent
    position = lax.broadcasted_iota(jnp.int32, tuple(shape_list), axial_dim)
    dropped = at_first & (position < rim_width) | at_last & (position >= extent - rim_width)
    return jnp.where(dropped, jnp.float32(0.0), padded)


def radial_pad(values, rim_width, radial_mode):
    return jnp.pad(
        values, [(0, 0)] * (values.ndim - 1) + [(rim_width, rim_width)], mode=radial_mode
    )


def transport(scalar_pad, vel_pad, density_pad, density_rim, diffusion, step_size):
    center = shifted(scalar_pad, 2, 0, 0)
    density = shifted(density_pad, density_rim, 0, 0)
    change = jnp.zeros_like(center)
    for direction in range(3):
        carried = vel_pad[direction] * scalar_pad
        advect = (
            -shifted(carried, 2, direction, 2)
            + 8.0 * shifted(carried, 2, direction, 1)
            - 8.0 * shifted(carried, 2, direction, -1)
            + shifted(carried, 2, direction, -2)
        ) / 12.0
        upper_flux = (
            0.5
            * diffusion
            * (density + shifted(density_pad, density_rim, direction, 1))
            * (shifted(scalar_pad, 2, direction, 1) - center)
        )
        lower_flux = (
            0.5
            * diffusion
            * (density + shifted(density_pad, density_rim, direction, -1))
            * (center - shifted(scalar_pad, 2, direction, -1))
        )
        change = change - advect + upper_flux - lower_flux
    return center + step_size * change


def evaporate(attrs, gas_values, alive_mask, step_size):
    parcel_mass = attrs[0]
    parcel_temp = attrs[1]
    parcel_vel = attrs[2:5]
    offsets = attrs[5:8]
    gas_heat = gas_values[3]
    gas_fuel = gas_values[4]
    evap_rate = EVAP * jax.nn.softplus(gas_heat - parcel_temp) * (1.0 - gas_fuel)
    new_mass = parcel_mass * jnp.exp(-step_size * evap_rate)
    lost_mass = parcel_mass - new_mass
    new_temp = parcel_temp + step_size * RELAX * (gas_heat - parcel_temp)
    new_vel = parcel_vel + step_size * DRAG * (gas_values[0:3] - parcel_vel)
    new_offsets = offsets + step_size * new_vel
    heat_source = -LATENT * lost_mass - HEAT_CAP * new_mass * (new_temp - parcel_temp)
    new_attrs = (
        jnp.concatenate([new_mass[None], new_temp[None], new_vel, new_offsets], axis=0)
        * alive_mask[None]
    )
    sources = jnp.stack([heat_source * alive_mask, lost_mass * alive_mask])
    return (new_attrs, sources)


def pressure_pad(values):
    padded = extended(values, (("axial", 0), ("azim", 1)), 1)
    return radial_pad(clear_ends(padded, 1, 0), 1, "constant")


def operate(values):
    padded = pressure_pad(values)
    beside = shifted(padded, 1, 0, 1) + shifted(padded, 1, 0, -1)
    beside = beside + shifted(padded, 1, 1, 1) + shifted(padded, 1, 1, -1)
    beside = beside + shifted(padded, 1, 2, 1) + shifted(padded, 1, 2, -1)
    return (6.0 + SHIFT_PRESSURE) * values - beside


def reduce_groups():
    axial = lax.axis_size("axial")
    along_x = 4 if axial % 4 == 0 else 1
    groups = [("azim", 1, lax.axis_size("azim")), ("axial", 1, along_x), ("axial", along_x, axial // along_x)]
    return [group for group in groups if group[2] > 1]


def coefficient_cg(gram, size, shift, half_width):
    def apply_a(c):
        out = [shift * c[j] for j in range(size)]
        for j in range(size - 1):
            if j == 0:
                out[1] = out[1] + half_width * c[0]
            else:
                out[j + 1] = out[j + 1] + 0.5 * half_width * c[j]
                out[j - 1] = out[j - 1] + 0.5 * half_width * c[j]
        return out

    def inner(a, b):
        acc = None
        for i in range(size):
            for j in range(size):
                if isinstance(a[i], float) and a[i] == 0.0:
                    continue
                if isinstance(b[j], float) and b[j] == 0.0:
                    continue
                term = a[i] * gram[i][j] * b[j]
                acc = term if acc is None else acc + term
        return acc

    solution_c = [0.0] * size
    residual = [1.0] + [0.0] * (size - 1)
    search = list(residual)
    norm_now = inner(residual, residual)
    for iteration in range(ITERS):
        image = apply_a(search)
        alpha = norm_now / inner(search, image)
        solution_c = [solution_c[j] + alpha * search[j] for j in range(size)]
        residual = [residual[j] - alpha * image[j] for j in range(size)]
        if iteration == ITERS - 1:
            break
        norm_next = inner(residual, residual)
        search = [residual[j] + norm_next / norm_now * search[j] for j in range(size)]
        norm_now = norm_next
    return solution_c


def reduce_kernel(groups, shift, half_width, vel_ref, *refs):
    size = ITERS + 1
    basis_refs = refs[:size]
    o_ref, slots, send_sems, recv_sems = refs[size:]
    here = {"axial": lax.axis_index("axial"), "azim": lax.axis_index("azim")}

    def member(axis, stride, count, m):
        index = here[axis]
        base = index - ((index // stride) % count) * stride
        coords = dict(here)
        coords[axis] = base + m * stride
        return (coords["axial"], coords["azim"])

    def position(axis, stride, count):
        return (here[axis] // stride) % count

    barrier = pltpu.get_barrier_semaphore()
    greeted = 0
    for axis, stride, count in groups:
        mine = position(axis, stride, count)
        for m in range(1, count):
            pl.semaphore_signal(
                barrier,
                inc=1,
                device_id=member(axis, stride, count, (mine + m) % count),
                device_id_type=pl.DeviceIdType.MESH,
            )
            greeted += 1
    pl.semaphore_wait(barrier, greeted)
    row = lax.broadcasted_iota(jnp.int32, o_ref.shape, 0)
    lane = lax.broadcasted_iota(jnp.int32, o_ref.shape, 1)
    is_max = (row == 0) & (lane == 0)

    def total(x):
        return jnp.sum(jnp.sum(x, axis=0, keepdims=True), axis=1, keepdims=True)

    basis = [ref[...] for ref in basis_refs]
    pairs = [(i, j) for i in range(size) for j in range(i, size)]
    entries = [jnp.max(jnp.max(jnp.abs(vel_ref[...]), axis=0, keepdims=True), axis=1, keepdims=True)]
    entries += [total(basis[i] * basis[j]) for i, j in pairs]
    acc = jnp.zeros(o_ref.shape, jnp.float32)
    for n, entry in enumerate(entries):
        acc = jnp.where((row == 0) & (lane == n), entry, acc)
    offset = 0
    for axis, stride, count in groups:
        mine = position(axis, stride, count)
        slots[offset + mine] = acc
        copies = []
        for m in range(1, count):
            target = (mine + m) % count
            copy = pltpu.make_async_remote_copy(
                src_ref=slots.at[offset + mine],
                dst_ref=slots.at[offset + mine],
                send_sem=send_sems.at[offset + target],
                recv_sem=recv_sems.at[offset + mine],
                device_id=member(axis, stride, count, target),
                device_id_type=pl.DeviceIdType.MESH,
            )
            copy.start()
            copies.append(copy)
        for copy in copies:
            copy.wait_send()
        for m in range(count):
            incoming = pltpu.make_async_remote_copy(
                src_ref=slots.at[offset + m],
                dst_ref=slots.at[offset + m],
                send_sem=send_sems.at[offset + m],
                recv_sem=recv_sems.at[offset + m],
                device_id=member(axis, stride, count, m),
                device_id_type=pl.DeviceIdType.MESH,
            )

            @pl.when(m != mine)
            def _():
                incoming.wait_recv()

        combined = slots[offset]
        for m in range(1, count):
            other = slots[offset + m]
            combined = jnp.where(is_max, jnp.maximum(combined, other), combined + other)
        acc = combined
        offset += count
    first = acc[0:1, :]
    first_lane = lax.broadcasted_iota(jnp.int32, first.shape, 1)

    def entry_at(n):
        return jnp.sum(jnp.where(first_lane == n, first, 0.0), axis=1, keepdims=True)

    gram = [[None] * size for _ in range(size)]
    for n, (i, j) in enumerate(pairs):
        gram[i][j] = entry_at(n + 1)
        gram[j][i] = gram[i][j]
    coefficients = coefficient_cg(gram, size, shift, half_width)
    out = jnp.where(lane == ITERS, entry_at(0), 0.0)
    for j in range(ITERS):
        out = jnp.where((lane == j), coefficients[j], out)
    o_ref[...] = out


def pressure_coefficients(velocity, basis, shift, half_width):
    groups = reduce_groups()
    slot_count = sum(count for _, _, count in groups)
    flat = [v.reshape(-1, v.shape[-1]) for v in basis]
    out = pl.pallas_call(
        lambda *refs: reduce_kernel(groups, shift, half_width, *refs),
        out_shape=jax.ShapeDtypeStruct((8, 128), jnp.float32),
        in_specs=[pl.BlockSpec(memory_space=pltpu.VMEM)] * (1 + len(flat)),
        out_specs=pl.BlockSpec(memory_space=pltpu.VMEM),
        scratch_shapes=[
            pltpu.VMEM((slot_count, 8, 128), jnp.float32),
            pltpu.SemaphoreType.DMA((slot_count,)),
            pltpu.SemaphoreType.DMA((slot_count,)),
        ],
        compiler_params=pltpu.CompilerParams(collective_id=0, has_side_effects=True),
    )(velocity.reshape(-1, velocity.shape[-1]), *flat)
    return [out[0, j] for j in range(ITERS)], out[0, ITERS]


def neighbour_sum(padded):
    beside = shifted(padded, 1, 0, 1) + shifted(padded, 1, 0, -1)
    beside = beside + shifted(padded, 1, 1, 1) + shifted(padded, 1, 1, -1)
    return beside + shifted(padded, 1, 2, 1) + shifted(padded, 1, 2, -1)


def axial_valid(values, rim):
    extent = values.shape[0]
    inner_x = extent - 2 * rim
    first = lax.axis_index("axial") * inner_x - rim
    position = first + lax.broadcasted_iota(jnp.int32, (extent, 1, 1), 0)
    inside = (position >= 0) & (position < inner_x * lax.axis_size("axial"))
    return jnp.where(inside, values, jnp.float32(0.0))


def crop(values, by):
    if by == 0:
        return values
    return values[by:-by, by:-by]


def neighbour_sum_wide(values):
    padded = jnp.pad(values, [(0, 0), (0, 0), (1, 1)])
    nx, ny, nz = padded.shape

    def at(dx, dy, dz):
        return padded[1 + dx : nx - 1 + dx, 1 + dy : ny - 1 + dy, 1 + dz : nz - 1 + dz]

    beside = at(1, 0, 0) + at(-1, 0, 0)
    beside = beside + at(0, 1, 0) + at(0, -1, 0)
    return beside + at(0, 0, 1) + at(0, 0, -1)


def solve_pressure(wide_velocity, velocity):
    half_width = 6.0
    u = wide_velocity
    divergence = 0.5 * (u[0, 2:, 1:-1, 1:-1] - u[0, :-2, 1:-1, 1:-1])
    divergence = divergence + 0.5 * (u[1, 1:-1, 2:, 1:-1] - u[1, 1:-1, :-2, 1:-1])
    divergence = divergence + 0.5 * (u[2, 1:-1, 1:-1, 2:] - u[2, 1:-1, 1:-1, :-2])
    basis = [axial_valid(divergence, ITERS)]
    for j in range(ITERS):
        scaled = neighbour_sum_wide(basis[j]) * (-1.0 / half_width)
        if j == 0:
            fresh = scaled
        else:
            fresh = 2.0 * scaled - crop(basis[j - 1], 2)
        basis.append(axial_valid(fresh, ITERS - 1 - j))
    interior = [crop(basis[j], ITERS - j) for j in range(ITERS + 1)]
    coefficients, fastest = pressure_coefficients(
        velocity, interior, 6.0 + SHIFT_PRESSURE, half_width
    )
    padded_basis = [radial_pad(crop(basis[j], ITERS - j - 1), 1, "constant") for j in range(ITERS)]
    padded_pressure = coefficients[0] * padded_basis[0]
    for j in range(1, ITERS):
        padded_pressure = padded_pressure + coefficients[j] * padded_basis[j]
    return padded_pressure, fastest


def along_axial(buffer, step_by):
    return shifted_2(buffer, "axial", step_by)


def along_azim(buffer, step_by):
    return shifted_3(buffer, "azim", step_by)


def on_device(state, diff_coef, parcel_state, parcel_cell, parcel_dest, live_count):
    velocity = state[1:4]
    npar_local = parcel_cell.shape[0]
    cells_x, cells_y, cells_z = (state.shape[1], state.shape[2], state.shape[3])
    plane_count = cells_x * cells_y
    gas_table = jnp.transpose(state[1:6].reshape(5, plane_count, cells_z), (1, 0, 2)).reshape(
        plane_count, 5 * cells_z
    )
    live_now = live_count[0]
    slot_alive = jnp.arange(npar_local) < live_now
    alive_mask = slot_alive.astype(jnp.float32)
    plane_ids = parcel_cell // cells_z
    radial_ids = parcel_cell % cells_z
    plane_hot = (plane_ids[:, None] == jnp.arange(plane_count)[None, :]).astype(jnp.float32)
    radial_hot = (radial_ids[:, None] == jnp.arange(cells_z)[None, :]).astype(jnp.float32)
    gas_rows = jnp.dot(plane_hot, gas_table, precision=HIGHEST).reshape(npar_local, 5, cells_z)
    gas_values = jnp.sum(gas_rows * radial_hot[:, None, :], axis=2).T
    stacked = jnp.stack([(parcel_dest == d + 1) & slot_alive for d in range(4)]).astype(jnp.int32)
    ranks = jnp.cumsum(stacked, axis=1) - 1
    mover = jnp.sum(stacked, axis=0) > 0
    target = jnp.where(mover, jnp.sum(stacked * (jnp.arange(4)[:, None] * CAP + ranks), axis=0), -1)
    select = (target[:, None] == jnp.arange(4 * CAP)[None, :]).astype(jnp.float32)
    raw = jnp.concatenate([parcel_state, gas_values, alive_mask[None]], axis=0)
    leaving = jnp.transpose(
        jnp.dot(raw, select, precision=HIGHEST).reshape(raw.shape[0], 4, CAP), (1, 0, 2)
    )
    parcel_steps = [(-1, 0), (1, 0), (0, -1), (0, 1)]
    faces = [(sa, sz) for sa, sz in NEIGHBOURS if sa == 0 or sz == 0]
    items = [(rim_slab(state, 2, sa, sz), (sa, sz)) for sa, sz in faces]
    items += [(rim_slab(velocity, ITERS + 1, sa, sz), (sa, sz)) for sa, sz in NEIGHBOURS]
    items += [(leaving[d], parcel_steps[d]) for d in range(4)]
    got = neighbour_exchange(items)
    count = len(faces)
    state_rims = {(-sa, -sz): got[k] for k, (sa, sz) in enumerate(faces)}
    velocity_rims = {
        (-sa, -sz): got[count + k] for k, (sa, sz) in enumerate(NEIGHBOURS)
    }
    landed = got[count + len(NEIGHBOURS) :]
    whole_pad = assemble(state, state_rims)
    whole_pad = radial_pad(clear_ends(whole_pad, 2, 1), 2, "edge")
    moving = whole_pad[1:]
    density_pad = whole_pad[0]
    density_rim = 2
    vel_pad = moving[0:3]
    wide_velocity = assemble(velocity, velocity_rims)
    wide_velocity = radial_pad(clear_ends(wide_velocity, ITERS + 1, 1), 1, "edge")
    padded_pressure, fastest = solve_pressure(wide_velocity, velocity)
    step_size = CFL / (fastest + 1e-06)
    transported = transport(
        moving[3:], vel_pad, density_pad, density_rim, diff_coef[:, None, None, None], step_size
    )
    updated, sources = evaporate(parcel_state, gas_values, alive_mask, step_size)
    spread = (sources.T[:, :, None] * radial_hot[:, None, :]).reshape(npar_local, 2 * cells_z)
    deposit = lax.dot_general(plane_hot, spread, (((0,), (0,)), ((), ())), precision=HIGHEST)
    deposit = jnp.transpose(deposit.reshape(cells_x, cells_y, 2, cells_z), (2, 0, 1, 3))
    scalars_new = jnp.concatenate(
        [transported[:2] + deposit / state[0][None], transported[2:]], axis=0
    )
    at_first = lax.axis_index("axial") == 0
    at_last = lax.axis_index("axial") == lax.axis_size("axial") - 1
    arriving = []
    for d in range(4):
        payload = landed[d]
        if d == 0:
            payload = jnp.where(at_last, jnp.float32(0.0), payload)
        if d == 1:
            payload = jnp.where(at_first, jnp.float32(0.0), payload)
        moved, _ = evaporate(payload[:8], payload[8:13], payload[13], step_size)
        arriving.append(moved)
    arrived = jnp.stack(arriving)
    kept_parcels = jnp.where((parcel_dest == 0)[None], updated, jnp.float32(0.0))
    velocity_new = jnp.stack(
        [
            velocity[d]
            - 0.5 * (shifted(padded_pressure, 1, d, 1) - shifted(padded_pressure, 1, d, -1))
            for d in range(3)
        ]
    )
    return (scalars_new, velocity_new, kept_parcels, arrived)


def solution(mesh):
    in_specs = (
        P(None, "axial", "azim", None),
        P(),
        P(None, ("axial", "azim")),
        P(("axial", "azim")),
        P(("axial", "azim")),
        P(("axial", "azim")),
    )
    out_specs = (
        P(None, "axial", "azim", None),
        P(None, "axial", "azim", None),
        P(None, ("axial", "azim")),
        P(None, None, ("axial", "azim")),
    )
    return jax.shard_map(
        on_device, mesh=mesh, in_specs=in_specs, out_specs=out_specs, check_vma=False
    )
```

```python
import jax
import jax.numpy as jnp
from jax import lax
from jax.sharding import PartitionSpec as P
from jax.experimental import pallas as pl
from jax.experimental.pallas import tpu as pltpu

CAP = 64
ITERS = 4


CFL = 0.4
SHIFT_PRESSURE = 0.25
EVAP = 8.0
RELAX = 4.0
DRAG = 6.0
LATENT = 0.5
HEAT_CAP = 0.8
HIGHEST = lax.Precision.HIGHEST


def extended(block, sides, width):
    for axis, dim in sides:
        count = lax.axis_size(axis)
        forward = [(i, i + 1) for i in range(count - 1)]
        forward.append((count - 1, 0))
        backward = [(target, source) for source, target in forward]
        low = lax.ppermute(
            lax.slice_in_dim(block, block.shape[dim] - width, None, axis=dim), axis, forward
        )
        high = lax.ppermute(lax.slice_in_dim(block, 0, width, axis=dim), axis, backward)
        block = jnp.concatenate([low, block, high], axis=dim)
    return block


def exchange_kernel(offsets, *refs):
    count = len(offsets)
    sources = refs[:count]
    outs = refs[count : 2 * count]
    send_sems, recv_sems = refs[2 * count :]
    axial = lax.axis_index("axial")
    azim = lax.axis_index("azim")

    def device(step_axial, step_azim):
        return (
            (axial + step_axial + lax.axis_size("axial")) % lax.axis_size("axial"),
            (azim + step_azim + lax.axis_size("azim")) % lax.axis_size("azim"),
        )

    has_low = axial > 0
    has_high = axial < lax.axis_size("axial") - 1

    def reachable(step_axial):
        if step_axial < 0:
            return has_low
        if step_axial > 0:
            return has_high
        return None

    def guarded(condition, action):
        if condition is None:
            action()
        else:
            pl.when(condition)(action)

    neighbours = sorted(set(offsets))
    barrier = pltpu.get_barrier_semaphore()
    expected = 0
    for step in neighbours:

        def greet(step=step):
            pl.semaphore_signal(
                barrier, inc=1, device_id=device(*step), device_id_type=pl.DeviceIdType.MESH
            )

        guarded(reachable(step[0]), greet)
        condition = reachable(-step[0])
        expected = expected + (1 if condition is None else condition.astype(jnp.int32))
    pl.semaphore_wait(barrier, expected)
    copies = []
    for k, step in enumerate(offsets):
        copy = pltpu.make_async_remote_copy(
            src_ref=sources[k],
            dst_ref=outs[k],
            send_sem=send_sems.at[k],
            recv_sem=recv_sems.at[k],
            device_id=device(*step),
            device_id_type=pl.DeviceIdType.MESH,
        )
        guarded(reachable(step[0]), copy.start)
        copies.append((copy, step))
    for copy, step in copies:
        guarded(reachable(step[0]), copy.wait_send)
        guarded(reachable(-step[0]), copy.wait_recv)


def neighbour_exchange(items):
    offsets = [step for _, step in items]
    flat = [a for a, _ in items]
    count = len(flat)
    outs = pl.pallas_call(
        lambda *refs: exchange_kernel(offsets, *refs),
        out_shape=[jax.ShapeDtypeStruct(f.shape, f.dtype) for f in flat],
        in_specs=[pl.BlockSpec(memory_space=pl.ANY)] * count,
        out_specs=[pl.BlockSpec(memory_space=pl.ANY)] * count,
        scratch_shapes=[pltpu.SemaphoreType.DMA((count,)), pltpu.SemaphoreType.DMA((count,))],
        compiler_params=pltpu.CompilerParams(collective_id=1, has_side_effects=True),
    )(*flat)
    return list(outs)


def rim_slab(block, width, step_axial, step_azim):
    def pick(values, dim, step):
        if step > 0:
            return lax.slice_in_dim(values, values.shape[dim] - width, None, axis=dim)
        if step < 0:
            return lax.slice_in_dim(values, 0, width, axis=dim)
        return values

    return pick(pick(block, 1, step_axial), 2, step_azim)


NEIGHBOURS = [(sa, sz) for sa in (-1, 0, 1) for sz in (-1, 0, 1) if (sa, sz) != (0, 0)]


def assemble(block, received):
    rim_a = received[(-1, 0)].shape[1]
    rim_z = received[(0, -1)].shape[2]
    corner = block.shape[:1] + (rim_a, rim_z) + block.shape[3:]
    bands = []
    for pz in (-1, 0, 1):
        row = []
        for pa in (-1, 0, 1):
            if (pa, pz) == (0, 0):
                row.append(block)
            elif (pa, pz) in received:
                row.append(received[(pa, pz)])
            else:
                row.append(jnp.zeros(corner, block.dtype))
        bands.append(jnp.concatenate(row, axis=1))
    return jnp.concatenate(bands, axis=2)


def shifted_2(shard, axis, by):
    length = lax.axis_size(axis)
    pairs = [(i, i + by) for i in range(length) if 0 <= i + by < length]
    return lax.ppermute(shard, axis, pairs)


def shifted_3(shard, axis, by):
    length = lax.axis_size(axis)
    return lax.ppermute(shard, axis, [(i, (i + by) % length) for i in range(length)])


def shifted(padded, rim_width, direction, step_by):
    selector = []
    total_dims = padded.ndim
    for dim_index in range(total_dims):
        extent = padded.shape[dim_index]
        if dim_index == total_dims - 3 + direction:
            selector.append(slice(rim_width + step_by, extent - rim_width + step_by))
        elif dim_index >= total_dims - 3:
            selector.append(slice(rim_width, extent - rim_width))
        else:
            selector.append(slice(None))
    return padded[tuple(selector)]


def clear_ends(padded, rim_width, axial_dim):
    extent = padded.shape[axial_dim]
    at_first = lax.axis_index("axial") == 0
    at_last = lax.axis_index("axial") == lax.axis_size("axial") - 1
    shape_list = [1] * padded.ndim
    shape_list[axial_dim] = extent
    position = lax.broadcasted_iota(jnp.int32, tuple(shape_list), axial_dim)
    dropped = at_first & (position < rim_width) | at_last & (position >= extent - rim_width)
    return jnp.where(dropped, jnp.float32(0.0), padded)


def radial_pad(values, rim_width, radial_mode):
    return jnp.pad(
        values, [(0, 0)] * (values.ndim - 1) + [(rim_width, rim_width)], mode=radial_mode
    )


def transport(scalar_pad, vel_pad, density_pad, density_rim, diffusion, step_size):
    center = shifted(scalar_pad, 2, 0, 0)
    density = shifted(density_pad, density_rim, 0, 0)
    change = jnp.zeros_like(center)
    for direction in range(3):
        carried = vel_pad[direction] * scalar_pad
        advect = (
            -shifted(carried, 2, direction, 2)
            + 8.0 * shifted(carried, 2, direction, 1)
            - 8.0 * shifted(carried, 2, direction, -1)
            + shifted(carried, 2, direction, -2)
        ) / 12.0
        upper_flux = (
            0.5
            * diffusion
            * (density + shifted(density_pad, density_rim, direction, 1))
            * (shifted(scalar_pad, 2, direction, 1) - center)
        )
        lower_flux = (
            0.5
            * diffusion
            * (density + shifted(density_pad, density_rim, direction, -1))
            * (center - shifted(scalar_pad, 2, direction, -1))
        )
        change = change - advect + upper_flux - lower_flux
    return center + step_size * change


def evaporate(attrs, gas_values, alive_mask, step_size):
    parcel_mass = attrs[0]
    parcel_temp = attrs[1]
    parcel_vel = attrs[2:5]
    offsets = attrs[5:8]
    gas_heat = gas_values[3]
    gas_fuel = gas_values[4]
    evap_rate = EVAP * jax.nn.softplus(gas_heat - parcel_temp) * (1.0 - gas_fuel)
    new_mass = parcel_mass * jnp.exp(-step_size * evap_rate)
    lost_mass = parcel_mass - new_mass
    new_temp = parcel_temp + step_size * RELAX * (gas_heat - parcel_temp)
    new_vel = parcel_vel + step_size * DRAG * (gas_values[0:3] - parcel_vel)
    new_offsets = offsets + step_size * new_vel
    heat_source = -LATENT * lost_mass - HEAT_CAP * new_mass * (new_temp - parcel_temp)
    new_attrs = (
        jnp.concatenate([new_mass[None], new_temp[None], new_vel, new_offsets], axis=0)
        * alive_mask[None]
    )
    sources = jnp.stack([heat_source * alive_mask, lost_mass * alive_mask])
    return (new_attrs, sources)


def pressure_pad(values):
    padded = extended(values, (("axial", 0), ("azim", 1)), 1)
    return radial_pad(clear_ends(padded, 1, 0), 1, "constant")


def operate(values):
    padded = pressure_pad(values)
    beside = shifted(padded, 1, 0, 1) + shifted(padded, 1, 0, -1)
    beside = beside + shifted(padded, 1, 1, 1) + shifted(padded, 1, 1, -1)
    beside = beside + shifted(padded, 1, 2, 1) + shifted(padded, 1, 2, -1)
    return (6.0 + SHIFT_PRESSURE) * values - beside


def reduce_groups():
    axial = lax.axis_size("axial")
    along_x = 4 if axial % 4 == 0 else 1
    groups = [("azim", 1, lax.axis_size("azim")), ("axial", 1, along_x), ("axial", along_x, axial // along_x)]
    return [group for group in groups if group[2] > 1]


def coefficient_cg(gram, size, shift, half_width):
    def apply_a(c):
        out = [shift * c[j] for j in range(size)]
        for j in range(size - 1):
            if j == 0:
                out[1] = out[1] + half_width * c[0]
            else:
                out[j + 1] = out[j + 1] + 0.5 * half_width * c[j]
                out[j - 1] = out[j - 1] + 0.5 * half_width * c[j]
        return out

    def inner(a, b):
        acc = None
        for i in range(size):
            for j in range(size):
                if isinstance(a[i], float) and a[i] == 0.0:
                    continue
                if isinstance(b[j], float) and b[j] == 0.0:
                    continue
                term = a[i] * gram[i][j] * b[j]
                acc = term if acc is None else acc + term
        return acc

    solution_c = [0.0] * size
    residual = [1.0] + [0.0] * (size - 1)
    search = list(residual)
    norm_now = inner(residual, residual)
    for iteration in range(ITERS):
        image = apply_a(search)
        alpha = norm_now / inner(search, image)
        solution_c = [solution_c[j] + alpha * search[j] for j in range(size)]
        residual = [residual[j] - alpha * image[j] for j in range(size)]
        if iteration == ITERS - 1:
            break
        norm_next = inner(residual, residual)
        search = [residual[j] + norm_next / norm_now * search[j] for j in range(size)]
        norm_now = norm_next
    return solution_c


def reduce_kernel(groups, shift, half_width, vel_ref, *refs):
    size = ITERS + 1
    basis_refs = refs[:size]
    o_ref, slots, send_sems, recv_sems = refs[size:]
    here = {"axial": lax.axis_index("axial"), "azim": lax.axis_index("azim")}

    def member(axis, stride, count, m):
        index = here[axis]
        base = index - ((index // stride) % count) * stride
        coords = dict(here)
        coords[axis] = base + m * stride
        return (coords["axial"], coords["azim"])

    def position(axis, stride, count):
        return (here[axis] // stride) % count

    barrier = pltpu.get_barrier_semaphore()
    greeted = 0
    for axis, stride, count in groups:
        mine = position(axis, stride, count)
        for m in range(1, count):
            pl.semaphore_signal(
                barrier,
                inc=1,
                device_id=member(axis, stride, count, (mine + m) % count),
                device_id_type=pl.DeviceIdType.MESH,
            )
            greeted += 1
    pl.semaphore_wait(barrier, greeted)
    row = lax.broadcasted_iota(jnp.int32, o_ref.shape, 0)
    lane = lax.broadcasted_iota(jnp.int32, o_ref.shape, 1)
    is_max = (row == 0) & (lane == 0)

    def total(x):
        return jnp.sum(jnp.sum(x, axis=0, keepdims=True), axis=1, keepdims=True)

    basis = [ref[...] for ref in basis_refs]
    pairs = [(i, j) for i in range(size) for j in range(i, size)]
    entries = [jnp.max(jnp.max(jnp.abs(vel_ref[...]), axis=0, keepdims=True), axis=1, keepdims=True)]
    entries += [total(basis[i] * basis[j]) for i, j in pairs]
    acc = jnp.zeros(o_ref.shape, jnp.float32)
    for n, entry in enumerate(entries):
        acc = jnp.where((row == 0) & (lane == n), entry, acc)
    offset = 0
    for axis, stride, count in groups:
        mine = position(axis, stride, count)
        slots[offset + mine] = acc
        copies = []
        for m in range(1, count):
            target = (mine + m) % count
            copy = pltpu.make_async_remote_copy(
                src_ref=slots.at[offset + mine],
                dst_ref=slots.at[offset + mine],
                send_sem=send_sems.at[offset + target],
                recv_sem=recv_sems.at[offset + mine],
                device_id=member(axis, stride, count, target),
                device_id_type=pl.DeviceIdType.MESH,
            )
            copy.start()
            copies.append(copy)
        for copy in copies:
            copy.wait_send()
        for m in range(count):
            incoming = pltpu.make_async_remote_copy(
                src_ref=slots.at[offset + m],
                dst_ref=slots.at[offset + m],
                send_sem=send_sems.at[offset + m],
                recv_sem=recv_sems.at[offset + m],
                device_id=member(axis, stride, count, m),
                device_id_type=pl.DeviceIdType.MESH,
            )

            @pl.when(m != mine)
            def _():
                incoming.wait_recv()

        combined = slots[offset]
        for m in range(1, count):
            other = slots[offset + m]
            combined = jnp.where(is_max, jnp.maximum(combined, other), combined + other)
        acc = combined
        offset += count
    first = acc[0:1, :]
    first_lane = lax.broadcasted_iota(jnp.int32, first.shape, 1)

    def entry_at(n):
        return jnp.sum(jnp.where(first_lane == n, first, 0.0), axis=1, keepdims=True)

    gram = [[None] * size for _ in range(size)]
    for n, (i, j) in enumerate(pairs):
        gram[i][j] = entry_at(n + 1)
        gram[j][i] = gram[i][j]
    coefficients = coefficient_cg(gram, size, shift, half_width)
    out = jnp.where(lane == ITERS, entry_at(0), 0.0)
    for j in range(ITERS):
        out = jnp.where((lane == j), coefficients[j], out)
    o_ref[...] = out


def pressure_coefficients(velocity, basis, shift, half_width):
    groups = reduce_groups()
    slot_count = sum(count for _, _, count in groups)
    flat = [v.reshape(-1, v.shape[-1]) for v in basis]
    out = pl.pallas_call(
        lambda *refs: reduce_kernel(groups, shift, half_width, *refs),
        out_shape=jax.ShapeDtypeStruct((8, 128), jnp.float32),
        in_specs=[pl.BlockSpec(memory_space=pltpu.VMEM)] * (1 + len(flat)),
        out_specs=pl.BlockSpec(memory_space=pltpu.VMEM),
        scratch_shapes=[
            pltpu.VMEM((slot_count, 8, 128), jnp.float32),
            pltpu.SemaphoreType.DMA((slot_count,)),
            pltpu.SemaphoreType.DMA((slot_count,)),
        ],
        compiler_params=pltpu.CompilerParams(collective_id=0, has_side_effects=True),
    )(velocity.reshape(-1, velocity.shape[-1]), *flat)
    return [out[0, j] for j in range(ITERS)], out[0, ITERS]


def neighbour_sum(padded):
    beside = shifted(padded, 1, 0, 1) + shifted(padded, 1, 0, -1)
    beside = beside + shifted(padded, 1, 1, 1) + shifted(padded, 1, 1, -1)
    return beside + shifted(padded, 1, 2, 1) + shifted(padded, 1, 2, -1)


def axial_valid(values, rim):
    extent = values.shape[0]
    inner_x = extent - 2 * rim
    first = lax.axis_index("axial") * inner_x - rim
    position = first + lax.broadcasted_iota(jnp.int32, (extent, 1, 1), 0)
    inside = (position >= 0) & (position < inner_x * lax.axis_size("axial"))
    return jnp.where(inside, values, jnp.float32(0.0))


def crop(values, by):
    if by == 0:
        return values
    return values[by:-by, by:-by]


def neighbour_sum_wide(values):
    padded = jnp.pad(values, [(0, 0), (0, 0), (1, 1)])
    nx, ny, nz = padded.shape

    def at(dx, dy, dz):
        return padded[1 + dx : nx - 1 + dx, 1 + dy : ny - 1 + dy, 1 + dz : nz - 1 + dz]

    beside = at(1, 0, 0) + at(-1, 0, 0)
    beside = beside + at(0, 1, 0) + at(0, -1, 0)
    return beside + at(0, 0, 1) + at(0, 0, -1)


def solve_pressure(wide_velocity, velocity):
    half_width = 6.0
    u = wide_velocity
    divergence = 0.5 * (u[0, 2:, 1:-1, 1:-1] - u[0, :-2, 1:-1, 1:-1])
    divergence = divergence + 0.5 * (u[1, 1:-1, 2:, 1:-1] - u[1, 1:-1, :-2, 1:-1])
    divergence = divergence + 0.5 * (u[2, 1:-1, 1:-1, 2:] - u[2, 1:-1, 1:-1, :-2])
    basis = [axial_valid(divergence, ITERS)]
    for j in range(ITERS):
        scaled = neighbour_sum_wide(basis[j]) * (-1.0 / half_width)
        if j == 0:
            fresh = scaled
        else:
            fresh = 2.0 * scaled - crop(basis[j - 1], 2)
        basis.append(axial_valid(fresh, ITERS - 1 - j))
    interior = [crop(basis[j], ITERS - j) for j in range(ITERS + 1)]
    coefficients, fastest = pressure_coefficients(
        velocity, interior, 6.0 + SHIFT_PRESSURE, half_width
    )
    padded_basis = [radial_pad(crop(basis[j], ITERS - j - 1), 1, "constant") for j in range(ITERS)]
    padded_pressure = coefficients[0] * padded_basis[0]
    for j in range(1, ITERS):
        padded_pressure = padded_pressure + coefficients[j] * padded_basis[j]
    return padded_pressure, fastest


def along_axial(buffer, step_by):
    return shifted_2(buffer, "axial", step_by)


def along_azim(buffer, step_by):
    return shifted_3(buffer, "azim", step_by)


def on_device(state, diff_coef, parcel_state, parcel_cell, parcel_dest, live_count):
    velocity = state[1:4]
    npar_local = parcel_cell.shape[0]
    cells_x, cells_y, cells_z = (state.shape[1], state.shape[2], state.shape[3])
    plane_count = cells_x * cells_y
    gas_table = jnp.transpose(state[1:6].reshape(5, plane_count, cells_z), (1, 0, 2)).reshape(
        plane_count, 5 * cells_z
    )
    live_now = live_count[0]
    slot_alive = jnp.arange(npar_local) < live_now
    alive_mask = slot_alive.astype(jnp.float32)
    plane_ids = parcel_cell // cells_z
    radial_ids = parcel_cell % cells_z
    plane_hot = (plane_ids[:, None] == jnp.arange(plane_count)[None, :]).astype(jnp.float32)
    radial_hot = (radial_ids[:, None] == jnp.arange(cells_z)[None, :]).astype(jnp.float32)
    gas_rows = jnp.dot(plane_hot, gas_table, precision=HIGHEST).reshape(npar_local, 5, cells_z)
    gas_values = jnp.sum(gas_rows * radial_hot[:, None, :], axis=2).T
    stacked = jnp.stack([(parcel_dest == d + 1) & slot_alive for d in range(4)]).astype(jnp.int32)
    ranks = jnp.cumsum(stacked, axis=1) - 1
    mover = jnp.sum(stacked, axis=0) > 0
    target = jnp.where(mover, jnp.sum(stacked * (jnp.arange(4)[:, None] * CAP + ranks), axis=0), -1)
    select = (target[:, None] == jnp.arange(4 * CAP)[None, :]).astype(jnp.float32)
    raw = jnp.concatenate([parcel_state, gas_values, alive_mask[None]], axis=0)
    leaving = jnp.transpose(
        jnp.dot(raw, select, precision=HIGHEST).reshape(raw.shape[0], 4, CAP), (1, 0, 2)
    )
    parcel_steps = [(-1, 0), (1, 0), (0, -1), (0, 1)]
    faces = [(sa, sz) for sa, sz in NEIGHBOURS if sa == 0 or sz == 0]
    items = [(rim_slab(state, 2, sa, sz), (sa, sz)) for sa, sz in faces]
    items += [(rim_slab(velocity, ITERS + 1, sa, sz), (sa, sz)) for sa, sz in NEIGHBOURS]
    items += [(leaving[d], parcel_steps[d]) for d in range(4)]
    got = neighbour_exchange(items)
    count = len(faces)
    state_rims = {(-sa, -sz): got[k] for k, (sa, sz) in enumerate(faces)}
    velocity_rims = {
        (-sa, -sz): got[count + k] for k, (sa, sz) in enumerate(NEIGHBOURS)
    }
    landed = got[count + len(NEIGHBOURS) :]
    whole_pad = assemble(state, state_rims)
    whole_pad = radial_pad(clear_ends(whole_pad, 2, 1), 2, "edge")
    moving = whole_pad[1:]
    density_pad = whole_pad[0]
    density_rim = 2
    vel_pad = moving[0:3]
    wide_velocity = assemble(velocity, velocity_rims)
    wide_velocity = radial_pad(clear_ends(wide_velocity, ITERS + 1, 1), 1, "edge")
    padded_pressure, fastest = solve_pressure(wide_velocity, velocity)
    step_size = CFL / (fastest + 1e-06)
    transported = transport(
        moving[3:], vel_pad, density_pad, density_rim, diff_coef[:, None, None, None], step_size
    )
    updated, sources = evaporate(parcel_state, gas_values, alive_mask, step_size)
    spread = (sources.T[:, :, None] * radial_hot[:, None, :]).reshape(npar_local, 2 * cells_z)
    deposit = lax.dot_general(plane_hot, spread, (((0,), (0,)), ((), ())), precision=HIGHEST)
    deposit = jnp.transpose(deposit.reshape(cells_x, cells_y, 2, cells_z), (2, 0, 1, 3))
    scalars_new = jnp.concatenate(
        [transported[:2] + deposit / state[0][None], transported[2:]], axis=0
    )
    at_first = lax.axis_index("axial") == 0
    at_last = lax.axis_index("axial") == lax.axis_size("axial") - 1
    arriving = []
    for d in range(4):
        payload = landed[d]
        if d == 0:
            payload = jnp.where(at_last, jnp.float32(0.0), payload)
        if d == 1:
            payload = jnp.where(at_first, jnp.float32(0.0), payload)
        moved, _ = evaporate(payload[:8], payload[8:13], payload[13], step_size)
        arriving.append(moved)
    arrived = jnp.stack(arriving)
    kept_parcels = jnp.where((parcel_dest == 0)[None], updated, jnp.float32(0.0))
    velocity_new = jnp.stack(
        [
            velocity[d]
            - 0.5 * (shifted(padded_pressure, 1, d, 1) - shifted(padded_pressure, 1, d, -1))
            for d in range(3)
        ]
    )
    return (scalars_new, velocity_new, kept_parcels, arrived)


def solution(mesh):
    in_specs = (
        P(None, "axial", "azim", None),
        P(),
        P(None, ("axial", "azim")),
        P(("axial", "azim")),
        P(("axial", "azim")),
        P(("axial", "azim")),
    )
    out_specs = (
        P(None, "axial", "azim", None),
        P(None, "axial", "azim", None),
        P(None, ("axial", "azim")),
        P(None, None, ("axial", "azim")),
    )
    return jax.shard_map(
        on_device, mesh=mesh, in_specs=in_specs, out_specs=out_specs, check_vma=False
    )
```

```python
import jax
import jax.numpy as jnp
from jax import lax
from jax.sharding import PartitionSpec as P
from jax.experimental import pallas as pl
from jax.experimental.pallas import tpu as pltpu

CAP = 64
ITERS = 4


CFL = 0.4
SHIFT_PRESSURE = 0.25
EVAP = 8.0
RELAX = 4.0
DRAG = 6.0
LATENT = 0.5
HEAT_CAP = 0.8
HIGHEST = lax.Precision.HIGHEST


def extended(block, sides, width):
    for axis, dim in sides:
        count = lax.axis_size(axis)
        forward = [(i, i + 1) for i in range(count - 1)]
        forward.append((count - 1, 0))
        backward = [(target, source) for source, target in forward]
        low = lax.ppermute(
            lax.slice_in_dim(block, block.shape[dim] - width, None, axis=dim), axis, forward
        )
        high = lax.ppermute(lax.slice_in_dim(block, 0, width, axis=dim), axis, backward)
        block = jnp.concatenate([low, block, high], axis=dim)
    return block


def exchange_kernel(offsets, *refs):
    count = len(offsets)
    sources = refs[:count]
    outs = refs[count : 2 * count]
    send_sems, recv_sems = refs[2 * count :]
    axial = lax.axis_index("axial")
    azim = lax.axis_index("azim")

    def device(step_axial, step_azim):
        return (
            (axial + step_axial + lax.axis_size("axial")) % lax.axis_size("axial"),
            (azim + step_azim + lax.axis_size("azim")) % lax.axis_size("azim"),
        )

    has_low = axial > 0
    has_high = axial < lax.axis_size("axial") - 1

    def reachable(step_axial):
        if step_axial < 0:
            return has_low
        if step_axial > 0:
            return has_high
        return None

    def guarded(condition, action):
        if condition is None:
            action()
        else:
            pl.when(condition)(action)

    neighbours = sorted(set(offsets))
    barrier = pltpu.get_barrier_semaphore()
    expected = 0
    for step in neighbours:

        def greet(step=step):
            pl.semaphore_signal(
                barrier, inc=1, device_id=device(*step), device_id_type=pl.DeviceIdType.MESH
            )

        guarded(reachable(step[0]), greet)
        condition = reachable(-step[0])
        expected = expected + (1 if condition is None else condition.astype(jnp.int32))
    pl.semaphore_wait(barrier, expected)
    copies = []
    for k, step in enumerate(offsets):
        copy = pltpu.make_async_remote_copy(
            src_ref=sources[k],
            dst_ref=outs[k],
            send_sem=send_sems.at[k],
            recv_sem=recv_sems.at[k],
            device_id=device(*step),
            device_id_type=pl.DeviceIdType.MESH,
        )
        guarded(reachable(step[0]), copy.start)
        copies.append((copy, step))
    for copy, step in copies:
        guarded(reachable(step[0]), copy.wait_send)
        guarded(reachable(-step[0]), copy.wait_recv)


def neighbour_exchange(items):
    offsets = [step for _, step in items]
    flat = [a for a, _ in items]
    count = len(flat)
    outs = pl.pallas_call(
        lambda *refs: exchange_kernel(offsets, *refs),
        out_shape=[jax.ShapeDtypeStruct(f.shape, f.dtype) for f in flat],
        in_specs=[pl.BlockSpec(memory_space=pl.ANY)] * count,
        out_specs=[pl.BlockSpec(memory_space=pl.ANY)] * count,
        scratch_shapes=[pltpu.SemaphoreType.DMA((count,)), pltpu.SemaphoreType.DMA((count,))],
        compiler_params=pltpu.CompilerParams(collective_id=1, has_side_effects=True),
    )(*flat)
    return list(outs)


def rim_slab(block, width, step_axial, step_azim):
    def pick(values, dim, step):
        if step > 0:
            return lax.slice_in_dim(values, values.shape[dim] - width, None, axis=dim)
        if step < 0:
            return lax.slice_in_dim(values, 0, width, axis=dim)
        return values

    return pick(pick(block, 1, step_axial), 2, step_azim)


NEIGHBOURS = [(sa, sz) for sa in (-1, 0, 1) for sz in (-1, 0, 1) if (sa, sz) != (0, 0)]


def assemble(block, received):
    rim_a = received[(-1, 0)].shape[1]
    rim_z = received[(0, -1)].shape[2]
    corner = block.shape[:1] + (rim_a, rim_z) + block.shape[3:]
    bands = []
    for pz in (-1, 0, 1):
        row = []
        for pa in (-1, 0, 1):
            if (pa, pz) == (0, 0):
                row.append(block)
            elif (pa, pz) in received:
                row.append(received[(pa, pz)])
            else:
                row.append(jnp.zeros(corner, block.dtype))
        bands.append(jnp.concatenate(row, axis=1))
    return jnp.concatenate(bands, axis=2)


def shifted_2(shard, axis, by):
    length = lax.axis_size(axis)
    pairs = [(i, i + by) for i in range(length) if 0 <= i + by < length]
    return lax.ppermute(shard, axis, pairs)


def shifted_3(shard, axis, by):
    length = lax.axis_size(axis)
    return lax.ppermute(shard, axis, [(i, (i + by) % length) for i in range(length)])


def shifted(padded, rim_width, direction, step_by):
    selector = []
    total_dims = padded.ndim
    for dim_index in range(total_dims):
        extent = padded.shape[dim_index]
        if dim_index == total_dims - 3 + direction:
            selector.append(slice(rim_width + step_by, extent - rim_width + step_by))
        elif dim_index >= total_dims - 3:
            selector.append(slice(rim_width, extent - rim_width))
        else:
            selector.append(slice(None))
    return padded[tuple(selector)]


def clear_ends(padded, rim_width, axial_dim):
    extent = padded.shape[axial_dim]
    at_first = lax.axis_index("axial") == 0
    at_last = lax.axis_index("axial") == lax.axis_size("axial") - 1
    shape_list = [1] * padded.ndim
    shape_list[axial_dim] = extent
    position = lax.broadcasted_iota(jnp.int32, tuple(shape_list), axial_dim)
    dropped = at_first & (position < rim_width) | at_last & (position >= extent - rim_width)
    return jnp.where(dropped, jnp.float32(0.0), padded)


def radial_pad(values, rim_width, radial_mode):
    return jnp.pad(
        values, [(0, 0)] * (values.ndim - 1) + [(rim_width, rim_width)], mode=radial_mode
    )


def transport(scalar_pad, vel_pad, density_pad, density_rim, diffusion, step_size):
    center = shifted(scalar_pad, 2, 0, 0)
    density = shifted(density_pad, density_rim, 0, 0)
    change = jnp.zeros_like(center)
    for direction in range(3):
        carried = vel_pad[direction] * scalar_pad
        advect = (
            -shifted(carried, 2, direction, 2)
            + 8.0 * shifted(carried, 2, direction, 1)
            - 8.0 * shifted(carried, 2, direction, -1)
            + shifted(carried, 2, direction, -2)
        ) / 12.0
        upper_flux = (
            0.5
            * diffusion
            * (density + shifted(density_pad, density_rim, direction, 1))
            * (shifted(scalar_pad, 2, direction, 1) - center)
        )
        lower_flux = (
            0.5
            * diffusion
            * (density + shifted(density_pad, density_rim, direction, -1))
            * (center - shifted(scalar_pad, 2, direction, -1))
        )
        change = change - advect + upper_flux - lower_flux
    return center + step_size * change


def evaporate(attrs, gas_values, alive_mask, step_size):
    parcel_mass = attrs[0]
    parcel_temp = attrs[1]
    parcel_vel = attrs[2:5]
    offsets = attrs[5:8]
    gas_heat = gas_values[3]
    gas_fuel = gas_values[4]
    evap_rate = EVAP * jax.nn.softplus(gas_heat - parcel_temp) * (1.0 - gas_fuel)
    new_mass = parcel_mass * jnp.exp(-step_size * evap_rate)
    lost_mass = parcel_mass - new_mass
    new_temp = parcel_temp + step_size * RELAX * (gas_heat - parcel_temp)
    new_vel = parcel_vel + step_size * DRAG * (gas_values[0:3] - parcel_vel)
    new_offsets = offsets + step_size * new_vel
    heat_source = -LATENT * lost_mass - HEAT_CAP * new_mass * (new_temp - parcel_temp)
    new_attrs = (
        jnp.concatenate([new_mass[None], new_temp[None], new_vel, new_offsets], axis=0)
        * alive_mask[None]
    )
    sources = jnp.stack([heat_source * alive_mask, lost_mass * alive_mask])
    return (new_attrs, sources)


def pressure_pad(values):
    padded = extended(values, (("axial", 0), ("azim", 1)), 1)
    return radial_pad(clear_ends(padded, 1, 0), 1, "constant")


def operate(values):
    padded = pressure_pad(values)
    beside = shifted(padded, 1, 0, 1) + shifted(padded, 1, 0, -1)
    beside = beside + shifted(padded, 1, 1, 1) + shifted(padded, 1, 1, -1)
    beside = beside + shifted(padded, 1, 2, 1) + shifted(padded, 1, 2, -1)
    return (6.0 + SHIFT_PRESSURE) * values - beside


def reduce_groups():
    axial = lax.axis_size("axial")
    along_x = 4 if axial % 4 == 0 else 1
    groups = [
        (("azim", 1, lax.axis_size("azim")), ("axial", 1, along_x)),
        (("axial", along_x, axial // along_x),),
    ]
    return [tuple(d for d in g if d[2] > 1) for g in groups if any(d[2] > 1 for d in g)]


def group_size(group):
    size = 1
    for _, _, count in group:
        size *= count
    return size


def coefficient_cg(gram, size, shift, half_width):
    def apply_a(c):
        out = [shift * c[j] for j in range(size)]
        for j in range(size - 1):
            if j == 0:
                out[1] = out[1] + half_width * c[0]
            else:
                out[j + 1] = out[j + 1] + 0.5 * half_width * c[j]
                out[j - 1] = out[j - 1] + 0.5 * half_width * c[j]
        return out

    def inner(a, b):
        acc = None
        for i in range(size):
            for j in range(size):
                if isinstance(a[i], float) and a[i] == 0.0:
                    continue
                if isinstance(b[j], float) and b[j] == 0.0:
                    continue
                term = a[i] * gram[i][j] * b[j]
                acc = term if acc is None else acc + term
        return acc

    solution_c = [0.0] * size
    residual = [1.0] + [0.0] * (size - 1)
    search = list(residual)
    norm_now = inner(residual, residual)
    for iteration in range(ITERS):
        image = apply_a(search)
        alpha = norm_now / inner(search, image)
        solution_c = [solution_c[j] + alpha * search[j] for j in range(size)]
        residual = [residual[j] - alpha * image[j] for j in range(size)]
        if iteration == ITERS - 1:
            break
        norm_next = inner(residual, residual)
        search = [residual[j] + norm_next / norm_now * search[j] for j in range(size)]
        norm_now = norm_next
    return solution_c


def reduce_kernel(groups, shift, half_width, vel_ref, *refs):
    size = ITERS + 1
    basis_refs = refs[:size]
    o_ref, slots, send_sems, recv_sems = refs[size:]
    here = {"axial": lax.axis_index("axial"), "azim": lax.axis_index("azim")}

    def member(group, m):
        coords = dict(here)
        for axis, stride, count in group:
            index = here[axis]
            base = index - ((index // stride) % count) * stride
            coords[axis] = base + (m % count) * stride
            m = m // count
        return (coords["axial"], coords["azim"])

    def position(group):
        place = 0
        weight = 1
        for axis, stride, count in group:
            place = place + ((here[axis] // stride) % count) * weight
            weight *= count
        return place

    barrier = pltpu.get_barrier_semaphore()
    greeted = 0
    for group in groups:
        count = group_size(group)
        mine = position(group)
        for m in range(1, count):
            pl.semaphore_signal(
                barrier,
                inc=1,
                device_id=member(group, (mine + m) % count),
                device_id_type=pl.DeviceIdType.MESH,
            )
            greeted += 1
    pl.semaphore_wait(barrier, greeted)
    row = lax.broadcasted_iota(jnp.int32, o_ref.shape, 0)
    lane = lax.broadcasted_iota(jnp.int32, o_ref.shape, 1)
    is_max = (row == 0) & (lane == 0)

    def total(x):
        return jnp.sum(jnp.sum(x, axis=0, keepdims=True), axis=1, keepdims=True)

    basis = [ref[...] for ref in basis_refs]
    pairs = [(i, j) for i in range(size) for j in range(i, size)]
    entries = [jnp.max(jnp.max(jnp.abs(vel_ref[...]), axis=0, keepdims=True), axis=1, keepdims=True)]
    entries += [total(basis[i] * basis[j]) for i, j in pairs]
    acc = jnp.zeros(o_ref.shape, jnp.float32)
    for n, entry in enumerate(entries):
        acc = jnp.where((row == 0) & (lane == n), entry, acc)
    offset = 0
    for group in groups:
        count = group_size(group)
        mine = position(group)
        slots[offset + mine] = acc
        copies = []
        for m in range(1, count):
            target = (mine + m) % count
            copy = pltpu.make_async_remote_copy(
                src_ref=slots.at[offset + mine],
                dst_ref=slots.at[offset + mine],
                send_sem=send_sems.at[offset + target],
                recv_sem=recv_sems.at[offset + mine],
                device_id=member(group, target),
                device_id_type=pl.DeviceIdType.MESH,
            )
            copy.start()
            copies.append(copy)
        for copy in copies:
            copy.wait_send()
        for m in range(count):
            incoming = pltpu.make_async_remote_copy(
                src_ref=slots.at[offset + m],
                dst_ref=slots.at[offset + m],
                send_sem=send_sems.at[offset + m],
                recv_sem=recv_sems.at[offset + m],
                device_id=member(group, m),
                device_id_type=pl.DeviceIdType.MESH,
            )

            @pl.when(m != mine)
            def _():
                incoming.wait_recv()

        combined = slots[offset]
        for m in range(1, count):
            other = slots[offset + m]
            combined = jnp.where(is_max, jnp.maximum(combined, other), combined + other)
        acc = combined
        offset += count
    first = acc[0:1, :]
    first_lane = lax.broadcasted_iota(jnp.int32, first.shape, 1)

    def entry_at(n):
        return jnp.sum(jnp.where(first_lane == n, first, 0.0), axis=1, keepdims=True)

    gram = [[None] * size for _ in range(size)]
    for n, (i, j) in enumerate(pairs):
        gram[i][j] = entry_at(n + 1)
        gram[j][i] = gram[i][j]
    coefficients = coefficient_cg(gram, size, shift, half_width)
    out = jnp.where(lane == ITERS, entry_at(0), 0.0)
    for j in range(ITERS):
        out = jnp.where((lane == j), coefficients[j], out)
    o_ref[...] = out


def pressure_coefficients(velocity, basis, shift, half_width):
    groups = reduce_groups()
    slot_count = sum(group_size(group) for group in groups)
    flat = [v.reshape(-1, v.shape[-1]) for v in basis]
    out = pl.pallas_call(
        lambda *refs: reduce_kernel(groups, shift, half_width, *refs),
        out_shape=jax.ShapeDtypeStruct((8, 128), jnp.float32),
        in_specs=[pl.BlockSpec(memory_space=pltpu.VMEM)] * (1 + len(flat)),
        out_specs=pl.BlockSpec(memory_space=pltpu.VMEM),
        scratch_shapes=[
            pltpu.VMEM((slot_count, 8, 128), jnp.float32),
            pltpu.SemaphoreType.DMA((slot_count,)),
            pltpu.SemaphoreType.DMA((slot_count,)),
        ],
        compiler_params=pltpu.CompilerParams(collective_id=0, has_side_effects=True),
    )(velocity.reshape(-1, velocity.shape[-1]), *flat)
    return [out[0, j] for j in range(ITERS)], out[0, ITERS]


def neighbour_sum(padded):
    beside = shifted(padded, 1, 0, 1) + shifted(padded, 1, 0, -1)
    beside = beside + shifted(padded, 1, 1, 1) + shifted(padded, 1, 1, -1)
    return beside + shifted(padded, 1, 2, 1) + shifted(padded, 1, 2, -1)


def axial_valid(values, rim):
    extent = values.shape[0]
    inner_x = extent - 2 * rim
    first = lax.axis_index("axial") * inner_x - rim
    position = first + lax.broadcasted_iota(jnp.int32, (extent, 1, 1), 0)
    inside = (position >= 0) & (position < inner_x * lax.axis_size("axial"))
    return jnp.where(inside, values, jnp.float32(0.0))


def crop(values, by):
    if by == 0:
        return values
    return values[by:-by, by:-by]


def neighbour_sum_wide(values):
    padded = jnp.pad(values, [(0, 0), (0, 0), (1, 1)])
    nx, ny, nz = padded.shape

    def at(dx, dy, dz):
        return padded[1 + dx : nx - 1 + dx, 1 + dy : ny - 1 + dy, 1 + dz : nz - 1 + dz]

    beside = at(1, 0, 0) + at(-1, 0, 0)
    beside = beside + at(0, 1, 0) + at(0, -1, 0)
    return beside + at(0, 0, 1) + at(0, 0, -1)


def solve_pressure(wide_velocity, velocity):
    half_width = 6.0
    u = wide_velocity
    divergence = 0.5 * (u[0, 2:, 1:-1, 1:-1] - u[0, :-2, 1:-1, 1:-1])
    divergence = divergence + 0.5 * (u[1, 1:-1, 2:, 1:-1] - u[1, 1:-1, :-2, 1:-1])
    divergence = divergence + 0.5 * (u[2, 1:-1, 1:-1, 2:] - u[2, 1:-1, 1:-1, :-2])
    basis = [axial_valid(divergence, ITERS)]
    for j in range(ITERS):
        scaled = neighbour_sum_wide(basis[j]) * (-1.0 / half_width)
        if j == 0:
            fresh = scaled
        else:
            fresh = 2.0 * scaled - crop(basis[j - 1], 2)
        basis.append(axial_valid(fresh, ITERS - 1 - j))
    interior = [crop(basis[j], ITERS - j) for j in range(ITERS + 1)]
    coefficients, fastest = pressure_coefficients(
        velocity, interior, 6.0 + SHIFT_PRESSURE, half_width
    )
    padded_basis = [radial_pad(crop(basis[j], ITERS - j - 1), 1, "constant") for j in range(ITERS)]
    padded_pressure = coefficients[0] * padded_basis[0]
    for j in range(1, ITERS):
        padded_pressure = padded_pressure + coefficients[j] * padded_basis[j]
    return padded_pressure, fastest


def along_axial(buffer, step_by):
    return shifted_2(buffer, "axial", step_by)


def along_azim(buffer, step_by):
    return shifted_3(buffer, "azim", step_by)


def on_device(state, diff_coef, parcel_state, parcel_cell, parcel_dest, live_count):
    velocity = state[1:4]
    npar_local = parcel_cell.shape[0]
    cells_x, cells_y, cells_z = (state.shape[1], state.shape[2], state.shape[3])
    plane_count = cells_x * cells_y
    gas_table = jnp.transpose(state[1:6].reshape(5, plane_count, cells_z), (1, 0, 2)).reshape(
        plane_count, 5 * cells_z
    )
    live_now = live_count[0]
    slot_alive = jnp.arange(npar_local) < live_now
    alive_mask = slot_alive.astype(jnp.float32)
    plane_ids = parcel_cell // cells_z
    radial_ids = parcel_cell % cells_z
    plane_hot = (plane_ids[:, None] == jnp.arange(plane_count)[None, :]).astype(jnp.float32)
    radial_hot = (radial_ids[:, None] == jnp.arange(cells_z)[None, :]).astype(jnp.float32)
    gas_rows = jnp.dot(plane_hot, gas_table, precision=HIGHEST).reshape(npar_local, 5, cells_z)
    gas_values = jnp.sum(gas_rows * radial_hot[:, None, :], axis=2).T
    stacked = jnp.stack([(parcel_dest == d + 1) & slot_alive for d in range(4)]).astype(jnp.int32)
    ranks = jnp.cumsum(stacked, axis=1) - 1
    mover = jnp.sum(stacked, axis=0) > 0
    target = jnp.where(mover, jnp.sum(stacked * (jnp.arange(4)[:, None] * CAP + ranks), axis=0), -1)
    select = (target[:, None] == jnp.arange(4 * CAP)[None, :]).astype(jnp.float32)
    raw = jnp.concatenate([parcel_state, gas_values, alive_mask[None]], axis=0)
    leaving = jnp.transpose(
        jnp.dot(raw, select, precision=HIGHEST).reshape(raw.shape[0], 4, CAP), (1, 0, 2)
    )
    parcel_steps = [(-1, 0), (1, 0), (0, -1), (0, 1)]
    faces = [(sa, sz) for sa, sz in NEIGHBOURS if sa == 0 or sz == 0]
    items = [(rim_slab(state, 2, sa, sz), (sa, sz)) for sa, sz in faces]
    items += [(rim_slab(velocity, ITERS + 1, sa, sz), (sa, sz)) for sa, sz in NEIGHBOURS]
    items += [(leaving[d], parcel_steps[d]) for d in range(4)]
    got = neighbour_exchange(items)
    count = len(faces)
    state_rims = {(-sa, -sz): got[k] for k, (sa, sz) in enumerate(faces)}
    velocity_rims = {
        (-sa, -sz): got[count + k] for k, (sa, sz) in enumerate(NEIGHBOURS)
    }
    landed = got[count + len(NEIGHBOURS) :]
    whole_pad = assemble(state, state_rims)
    whole_pad = radial_pad(clear_ends(whole_pad, 2, 1), 2, "edge")
    moving = whole_pad[1:]
    density_pad = whole_pad[0]
    density_rim = 2
    vel_pad = moving[0:3]
    wide_velocity = assemble(velocity, velocity_rims)
    wide_velocity = radial_pad(clear_ends(wide_velocity, ITERS + 1, 1), 1, "edge")
    padded_pressure, fastest = solve_pressure(wide_velocity, velocity)
    step_size = CFL / (fastest + 1e-06)
    transported = transport(
        moving[3:], vel_pad, density_pad, density_rim, diff_coef[:, None, None, None], step_size
    )
    updated, sources = evaporate(parcel_state, gas_values, alive_mask, step_size)
    spread = (sources.T[:, :, None] * radial_hot[:, None, :]).reshape(npar_local, 2 * cells_z)
    deposit = lax.dot_general(plane_hot, spread, (((0,), (0,)), ((), ())), precision=HIGHEST)
    deposit = jnp.transpose(deposit.reshape(cells_x, cells_y, 2, cells_z), (2, 0, 1, 3))
    scalars_new = jnp.concatenate(
        [transported[:2] + deposit / state[0][None], transported[2:]], axis=0
    )
    at_first = lax.axis_index("axial") == 0
    at_last = lax.axis_index("axial") == lax.axis_size("axial") - 1
    arriving = []
    for d in range(4):
        payload = landed[d]
        if d == 0:
            payload = jnp.where(at_last, jnp.float32(0.0), payload)
        if d == 1:
            payload = jnp.where(at_first, jnp.float32(0.0), payload)
        moved, _ = evaporate(payload[:8], payload[8:13], payload[13], step_size)
        arriving.append(moved)
    arrived = jnp.stack(arriving)
    kept_parcels = jnp.where((parcel_dest == 0)[None], updated, jnp.float32(0.0))
    velocity_new = jnp.stack(
        [
            velocity[d]
            - 0.5 * (shifted(padded_pressure, 1, d, 1) - shifted(padded_pressure, 1, d, -1))
            for d in range(3)
        ]
    )
    return (scalars_new, velocity_new, kept_parcels, arrived)


def solution(mesh):
    in_specs = (
        P(None, "axial", "azim", None),
        P(),
        P(None, ("axial", "azim")),
        P(("axial", "azim")),
        P(("axial", "azim")),
        P(("axial", "azim")),
    )
    out_specs = (
        P(None, "axial", "azim", None),
        P(None, "axial", "azim", None),
        P(None, ("axial", "azim")),
        P(None, None, ("axial", "azim")),
    )
    return jax.shard_map(
        on_device, mesh=mesh, in_specs=in_specs, out_specs=out_specs, check_vma=False
    )
```

```python
import jax
import jax.numpy as jnp
from jax import lax
from jax.sharding import PartitionSpec as P
from jax.experimental import pallas as pl
from jax.experimental.pallas import tpu as pltpu

CAP = 64
ITERS = 4


CFL = 0.4
SHIFT_PRESSURE = 0.25
EVAP = 8.0
RELAX = 4.0
DRAG = 6.0
LATENT = 0.5
HEAT_CAP = 0.8
HIGHEST = lax.Precision.HIGHEST


def extended(block, sides, width):
    for axis, dim in sides:
        count = lax.axis_size(axis)
        forward = [(i, i + 1) for i in range(count - 1)]
        forward.append((count - 1, 0))
        backward = [(target, source) for source, target in forward]
        low = lax.ppermute(
            lax.slice_in_dim(block, block.shape[dim] - width, None, axis=dim), axis, forward
        )
        high = lax.ppermute(lax.slice_in_dim(block, 0, width, axis=dim), axis, backward)
        block = jnp.concatenate([low, block, high], axis=dim)
    return block


def exchange_kernel(offsets, *refs):
    count = len(offsets)
    sources = refs[:count]
    outs = refs[count : 2 * count]
    send_sems, recv_sems = refs[2 * count :]
    axial = lax.axis_index("axial")
    azim = lax.axis_index("azim")

    def device(step_axial, step_azim):
        return (
            (axial + step_axial + lax.axis_size("axial")) % lax.axis_size("axial"),
            (azim + step_azim + lax.axis_size("azim")) % lax.axis_size("azim"),
        )

    has_low = axial > 0
    has_high = axial < lax.axis_size("axial") - 1

    def reachable(step_axial):
        if step_axial < 0:
            return has_low
        if step_axial > 0:
            return has_high
        return None

    def guarded(condition, action):
        if condition is None:
            action()
        else:
            pl.when(condition)(action)

    neighbours = sorted(set(offsets))
    barrier = pltpu.get_barrier_semaphore()
    expected = 0
    for step in neighbours:

        def greet(step=step):
            pl.semaphore_signal(
                barrier, inc=1, device_id=device(*step), device_id_type=pl.DeviceIdType.MESH
            )

        guarded(reachable(step[0]), greet)
        condition = reachable(-step[0])
        expected = expected + (1 if condition is None else condition.astype(jnp.int32))
    pl.semaphore_wait(barrier, expected)
    copies = []
    for k, step in enumerate(offsets):
        copy = pltpu.make_async_remote_copy(
            src_ref=sources[k],
            dst_ref=outs[k],
            send_sem=send_sems.at[k],
            recv_sem=recv_sems.at[k],
            device_id=device(*step),
            device_id_type=pl.DeviceIdType.MESH,
        )
        guarded(reachable(step[0]), copy.start)
        copies.append((copy, step))
    for copy, step in copies:
        guarded(reachable(step[0]), copy.wait_send)
        guarded(reachable(-step[0]), copy.wait_recv)


def neighbour_exchange(items):
    offsets = [step for _, step in items]
    flat = [a for a, _ in items]
    count = len(flat)
    outs = pl.pallas_call(
        lambda *refs: exchange_kernel(offsets, *refs),
        out_shape=[jax.ShapeDtypeStruct(f.shape, f.dtype) for f in flat],
        in_specs=[pl.BlockSpec(memory_space=pl.ANY)] * count,
        out_specs=[pl.BlockSpec(memory_space=pl.ANY)] * count,
        scratch_shapes=[pltpu.SemaphoreType.DMA((count,)), pltpu.SemaphoreType.DMA((count,))],
        compiler_params=pltpu.CompilerParams(collective_id=1, has_side_effects=True),
    )(*flat)
    return list(outs)


def rim_slab(block, width, step_axial, step_azim):
    def pick(values, dim, step):
        if step > 0:
            return lax.slice_in_dim(values, values.shape[dim] - width, None, axis=dim)
        if step < 0:
            return lax.slice_in_dim(values, 0, width, axis=dim)
        return values

    return pick(pick(block, 1, step_axial), 2, step_azim)


NEIGHBOURS = [(sa, sz) for sa in (-1, 0, 1) for sz in (-1, 0, 1) if (sa, sz) != (0, 0)]


def assemble(block, received):
    rim_a = received[(-1, 0)].shape[1]
    rim_z = received[(0, -1)].shape[2]
    corner = block.shape[:1] + (rim_a, rim_z) + block.shape[3:]
    bands = []
    for pz in (-1, 0, 1):
        row = []
        for pa in (-1, 0, 1):
            if (pa, pz) == (0, 0):
                row.append(block)
            elif (pa, pz) in received:
                row.append(received[(pa, pz)])
            else:
                row.append(jnp.zeros(corner, block.dtype))
        bands.append(jnp.concatenate(row, axis=1))
    return jnp.concatenate(bands, axis=2)


def shifted_2(shard, axis, by):
    length = lax.axis_size(axis)
    pairs = [(i, i + by) for i in range(length) if 0 <= i + by < length]
    return lax.ppermute(shard, axis, pairs)


def shifted_3(shard, axis, by):
    length = lax.axis_size(axis)
    return lax.ppermute(shard, axis, [(i, (i + by) % length) for i in range(length)])


def shifted(padded, rim_width, direction, step_by):
    selector = []
    total_dims = padded.ndim
    for dim_index in range(total_dims):
        extent = padded.shape[dim_index]
        if dim_index == total_dims - 3 + direction:
            selector.append(slice(rim_width + step_by, extent - rim_width + step_by))
        elif dim_index >= total_dims - 3:
            selector.append(slice(rim_width, extent - rim_width))
        else:
            selector.append(slice(None))
    return padded[tuple(selector)]


def clear_ends(padded, rim_width, axial_dim):
    extent = padded.shape[axial_dim]
    at_first = lax.axis_index("axial") == 0
    at_last = lax.axis_index("axial") == lax.axis_size("axial") - 1
    shape_list = [1] * padded.ndim
    shape_list[axial_dim] = extent
    position = lax.broadcasted_iota(jnp.int32, tuple(shape_list), axial_dim)
    dropped = at_first & (position < rim_width) | at_last & (position >= extent - rim_width)
    return jnp.where(dropped, jnp.float32(0.0), padded)


def radial_pad(values, rim_width, radial_mode):
    return jnp.pad(
        values, [(0, 0)] * (values.ndim - 1) + [(rim_width, rim_width)], mode=radial_mode
    )


def transport(scalar_pad, vel_pad, density_pad, density_rim, diffusion, step_size):
    center = shifted(scalar_pad, 2, 0, 0)
    density = shifted(density_pad, density_rim, 0, 0)
    change = jnp.zeros_like(center)
    for direction in range(3):
        carried = vel_pad[direction] * scalar_pad
        advect = (
            -shifted(carried, 2, direction, 2)
            + 8.0 * shifted(carried, 2, direction, 1)
            - 8.0 * shifted(carried, 2, direction, -1)
            + shifted(carried, 2, direction, -2)
        ) / 12.0
        upper_flux = (
            0.5
            * diffusion
            * (density + shifted(density_pad, density_rim, direction, 1))
            * (shifted(scalar_pad, 2, direction, 1) - center)
        )
        lower_flux = (
            0.5
            * diffusion
            * (density + shifted(density_pad, density_rim, direction, -1))
            * (center - shifted(scalar_pad, 2, direction, -1))
        )
        change = change - advect + upper_flux - lower_flux
    return center + step_size * change


def evaporate(attrs, gas_values, alive_mask, step_size):
    parcel_mass = attrs[0]
    parcel_temp = attrs[1]
    parcel_vel = attrs[2:5]
    offsets = attrs[5:8]
    gas_heat = gas_values[3]
    gas_fuel = gas_values[4]
    evap_rate = EVAP * jax.nn.softplus(gas_heat - parcel_temp) * (1.0 - gas_fuel)
    new_mass = parcel_mass * jnp.exp(-step_size * evap_rate)
    lost_mass = parcel_mass - new_mass
    new_temp = parcel_temp + step_size * RELAX * (gas_heat - parcel_temp)
    new_vel = parcel_vel + step_size * DRAG * (gas_values[0:3] - parcel_vel)
    new_offsets = offsets + step_size * new_vel
    heat_source = -LATENT * lost_mass - HEAT_CAP * new_mass * (new_temp - parcel_temp)
    new_attrs = (
        jnp.concatenate([new_mass[None], new_temp[None], new_vel, new_offsets], axis=0)
        * alive_mask[None]
    )
    sources = jnp.stack([heat_source * alive_mask, lost_mass * alive_mask])
    return (new_attrs, sources)


def pressure_pad(values):
    padded = extended(values, (("axial", 0), ("azim", 1)), 1)
    return radial_pad(clear_ends(padded, 1, 0), 1, "constant")


def operate(values):
    padded = pressure_pad(values)
    beside = shifted(padded, 1, 0, 1) + shifted(padded, 1, 0, -1)
    beside = beside + shifted(padded, 1, 1, 1) + shifted(padded, 1, 1, -1)
    beside = beside + shifted(padded, 1, 2, 1) + shifted(padded, 1, 2, -1)
    return (6.0 + SHIFT_PRESSURE) * values - beside


def reduce_groups():
    axial = lax.axis_size("axial")
    along_x = 4 if axial % 4 == 0 else 1
    groups = [("azim", 1, lax.axis_size("azim")), ("axial", 1, along_x), ("axial", along_x, axial // along_x)]
    return [group for group in groups if group[2] > 1]


def coefficient_cg(gram, size, shift, half_width):
    def apply_a(c):
        out = [shift * c[j] for j in range(size)]
        for j in range(size - 1):
            if j == 0:
                out[1] = out[1] + half_width * c[0]
            else:
                out[j + 1] = out[j + 1] + 0.5 * half_width * c[j]
                out[j - 1] = out[j - 1] + 0.5 * half_width * c[j]
        return out

    def inner(a, b):
        acc = None
        for i in range(size):
            for j in range(size):
                if isinstance(a[i], float) and a[i] == 0.0:
                    continue
                if isinstance(b[j], float) and b[j] == 0.0:
                    continue
                term = a[i] * gram[i][j] * b[j]
                acc = term if acc is None else acc + term
        return acc

    solution_c = [0.0] * size
    residual = [1.0] + [0.0] * (size - 1)
    search = list(residual)
    norm_now = inner(residual, residual)
    for iteration in range(ITERS):
        image = apply_a(search)
        alpha = norm_now / inner(search, image)
        solution_c = [solution_c[j] + alpha * search[j] for j in range(size)]
        residual = [residual[j] - alpha * image[j] for j in range(size)]
        if iteration == ITERS - 1:
            break
        norm_next = inner(residual, residual)
        search = [residual[j] + norm_next / norm_now * search[j] for j in range(size)]
        norm_now = norm_next
    return solution_c


def reduce_kernel(groups, extra_steps, shift, half_width, vel_ref, *refs):
    size = ITERS + 1
    extras = len(extra_steps)
    basis_refs = refs[:size]
    extra_sources = refs[size : size + extras]
    o_ref = refs[size + extras]
    extra_outs = refs[size + extras + 1 : size + 2 * extras + 1]
    slots, send_sems, recv_sems, extra_send, extra_recv = refs[size + 2 * extras + 1 :]
    here = {"axial": lax.axis_index("axial"), "azim": lax.axis_index("azim")}
    has_low = here["axial"] > 0
    has_high = here["axial"] < lax.axis_size("axial") - 1

    def reachable(step_axial):
        if step_axial < 0:
            return has_low
        if step_axial > 0:
            return has_high
        return None

    def guarded(condition, action):
        if condition is None:
            action()
        else:
            pl.when(condition)(action)

    def neighbour(step_axial, step_azim):
        return (
            (here["axial"] + step_axial + lax.axis_size("axial")) % lax.axis_size("axial"),
            (here["azim"] + step_azim + lax.axis_size("azim")) % lax.axis_size("azim"),
        )

    def member(axis, stride, count, m):
        index = here[axis]
        base = index - ((index // stride) % count) * stride
        coords = dict(here)
        coords[axis] = base + m * stride
        return (coords["axial"], coords["azim"])

    def position(axis, stride, count):
        return (here[axis] // stride) % count

    barrier = pltpu.get_barrier_semaphore()
    greeted = 0
    for axis, stride, count in groups:
        mine = position(axis, stride, count)
        for m in range(1, count):
            pl.semaphore_signal(
                barrier,
                inc=1,
                device_id=member(axis, stride, count, (mine + m) % count),
                device_id_type=pl.DeviceIdType.MESH,
            )
            greeted += 1
    for step in sorted(set(extra_steps)):

        def greet(step=step):
            pl.semaphore_signal(
                barrier, inc=1, device_id=neighbour(*step), device_id_type=pl.DeviceIdType.MESH
            )

        guarded(reachable(step[0]), greet)
        condition = reachable(-step[0])
        greeted = greeted + (1 if condition is None else condition.astype(jnp.int32))
    pl.semaphore_wait(barrier, greeted)
    extra_copies = []
    for k, step in enumerate(extra_steps):
        copy = pltpu.make_async_remote_copy(
            src_ref=extra_sources[k],
            dst_ref=extra_outs[k],
            send_sem=extra_send.at[k],
            recv_sem=extra_recv.at[k],
            device_id=neighbour(*step),
            device_id_type=pl.DeviceIdType.MESH,
        )
        guarded(reachable(step[0]), copy.start)
        extra_copies.append((copy, step))
    row = lax.broadcasted_iota(jnp.int32, o_ref.shape, 0)
    lane = lax.broadcasted_iota(jnp.int32, o_ref.shape, 1)
    is_max = (row == 0) & (lane == 0)

    def total(x):
        return jnp.sum(jnp.sum(x, axis=0, keepdims=True), axis=1, keepdims=True)

    basis = [ref[...] for ref in basis_refs]
    pairs = [(i, j) for i in range(size) for j in range(i, size)]
    entries = [jnp.max(jnp.max(jnp.abs(vel_ref[...]), axis=0, keepdims=True), axis=1, keepdims=True)]
    entries += [total(basis[i] * basis[j]) for i, j in pairs]
    acc = jnp.zeros(o_ref.shape, jnp.float32)
    for n, entry in enumerate(entries):
        acc = jnp.where((row == 0) & (lane == n), entry, acc)
    offset = 0
    for axis, stride, count in groups:
        mine = position(axis, stride, count)
        slots[offset + mine] = acc
        copies = []
        for m in range(1, count):
            target = (mine + m) % count
            copy = pltpu.make_async_remote_copy(
                src_ref=slots.at[offset + mine],
                dst_ref=slots.at[offset + mine],
                send_sem=send_sems.at[offset + target],
                recv_sem=recv_sems.at[offset + mine],
                device_id=member(axis, stride, count, target),
                device_id_type=pl.DeviceIdType.MESH,
            )
            copy.start()
            copies.append(copy)
        for copy in copies:
            copy.wait_send()
        for m in range(count):
            incoming = pltpu.make_async_remote_copy(
                src_ref=slots.at[offset + m],
                dst_ref=slots.at[offset + m],
                send_sem=send_sems.at[offset + m],
                recv_sem=recv_sems.at[offset + m],
                device_id=member(axis, stride, count, m),
                device_id_type=pl.DeviceIdType.MESH,
            )

            @pl.when(m != mine)
            def _():
                incoming.wait_recv()

        combined = slots[offset]
        for m in range(1, count):
            other = slots[offset + m]
            combined = jnp.where(is_max, jnp.maximum(combined, other), combined + other)
        acc = combined
        offset += count
    first = acc[0:1, :]
    first_lane = lax.broadcasted_iota(jnp.int32, first.shape, 1)

    def entry_at(n):
        return jnp.sum(jnp.where(first_lane == n, first, 0.0), axis=1, keepdims=True)

    gram = [[None] * size for _ in range(size)]
    for n, (i, j) in enumerate(pairs):
        gram[i][j] = entry_at(n + 1)
        gram[j][i] = gram[i][j]
    coefficients = coefficient_cg(gram, size, shift, half_width)
    out = jnp.where(lane == ITERS, entry_at(0), 0.0)
    for j in range(ITERS):
        out = jnp.where((lane == j), coefficients[j], out)
    o_ref[...] = out
    for copy, step in extra_copies:
        guarded(reachable(step[0]), copy.wait_send)
        guarded(reachable(-step[0]), copy.wait_recv)


def pressure_coefficients(velocity, basis, shift, half_width, extra_items):
    groups = reduce_groups()
    slot_count = sum(count for _, _, count in groups)
    flat = [v.reshape(-1, v.shape[-1]) for v in basis]
    extra_steps = [step for _, step in extra_items]
    extra_arrays = [a for a, _ in extra_items]
    extras = len(extra_arrays)
    vmem = pl.BlockSpec(memory_space=pltpu.VMEM)
    anywhere = pl.BlockSpec(memory_space=pl.ANY)
    outs = pl.pallas_call(
        lambda *refs: reduce_kernel(groups, extra_steps, shift, half_width, *refs),
        out_shape=[jax.ShapeDtypeStruct((8, 128), jnp.float32)]
        + [jax.ShapeDtypeStruct(a.shape, a.dtype) for a in extra_arrays],
        in_specs=[vmem] * (1 + len(flat)) + [anywhere] * extras,
        out_specs=[vmem] + [anywhere] * extras,
        scratch_shapes=[
            pltpu.VMEM((slot_count, 8, 128), jnp.float32),
            pltpu.SemaphoreType.DMA((slot_count,)),
            pltpu.SemaphoreType.DMA((slot_count,)),
            pltpu.SemaphoreType.DMA((extras,)),
            pltpu.SemaphoreType.DMA((extras,)),
        ],
        compiler_params=pltpu.CompilerParams(collective_id=0, has_side_effects=True),
    )(velocity.reshape(-1, velocity.shape[-1]), *flat, *extra_arrays)
    out = outs[0]
    return [out[0, j] for j in range(ITERS)], out[0, ITERS], list(outs[1:])


def neighbour_sum(padded):
    beside = shifted(padded, 1, 0, 1) + shifted(padded, 1, 0, -1)
    beside = beside + shifted(padded, 1, 1, 1) + shifted(padded, 1, 1, -1)
    return beside + shifted(padded, 1, 2, 1) + shifted(padded, 1, 2, -1)


def axial_valid(values, rim):
    extent = values.shape[0]
    inner_x = extent - 2 * rim
    first = lax.axis_index("axial") * inner_x - rim
    position = first + lax.broadcasted_iota(jnp.int32, (extent, 1, 1), 0)
    inside = (position >= 0) & (position < inner_x * lax.axis_size("axial"))
    return jnp.where(inside, values, jnp.float32(0.0))


def crop(values, by):
    if by == 0:
        return values
    return values[by:-by, by:-by]


def neighbour_sum_wide(values):
    padded = jnp.pad(values, [(0, 0), (0, 0), (1, 1)])
    nx, ny, nz = padded.shape

    def at(dx, dy, dz):
        return padded[1 + dx : nx - 1 + dx, 1 + dy : ny - 1 + dy, 1 + dz : nz - 1 + dz]

    beside = at(1, 0, 0) + at(-1, 0, 0)
    beside = beside + at(0, 1, 0) + at(0, -1, 0)
    return beside + at(0, 0, 1) + at(0, 0, -1)


def solve_pressure(wide_velocity, velocity, extra_items):
    half_width = 6.0
    u = wide_velocity
    divergence = 0.5 * (u[0, 2:, 1:-1, 1:-1] - u[0, :-2, 1:-1, 1:-1])
    divergence = divergence + 0.5 * (u[1, 1:-1, 2:, 1:-1] - u[1, 1:-1, :-2, 1:-1])
    divergence = divergence + 0.5 * (u[2, 1:-1, 1:-1, 2:] - u[2, 1:-1, 1:-1, :-2])
    basis = [axial_valid(divergence, ITERS)]
    for j in range(ITERS):
        scaled = neighbour_sum_wide(basis[j]) * (-1.0 / half_width)
        if j == 0:
            fresh = scaled
        else:
            fresh = 2.0 * scaled - crop(basis[j - 1], 2)
        basis.append(axial_valid(fresh, ITERS - 1 - j))
    interior = [crop(basis[j], ITERS - j) for j in range(ITERS + 1)]
    coefficients, fastest, received = pressure_coefficients(
        velocity, interior, 6.0 + SHIFT_PRESSURE, half_width, extra_items
    )
    padded_basis = [radial_pad(crop(basis[j], ITERS - j - 1), 1, "constant") for j in range(ITERS)]
    padded_pressure = coefficients[0] * padded_basis[0]
    for j in range(1, ITERS):
        padded_pressure = padded_pressure + coefficients[j] * padded_basis[j]
    return padded_pressure, fastest, received


def along_axial(buffer, step_by):
    return shifted_2(buffer, "axial", step_by)


def along_azim(buffer, step_by):
    return shifted_3(buffer, "azim", step_by)


def on_device(state, diff_coef, parcel_state, parcel_cell, parcel_dest, live_count):
    velocity = state[1:4]
    npar_local = parcel_cell.shape[0]
    cells_x, cells_y, cells_z = (state.shape[1], state.shape[2], state.shape[3])
    plane_count = cells_x * cells_y
    gas_table = jnp.transpose(state[1:6].reshape(5, plane_count, cells_z), (1, 0, 2)).reshape(
        plane_count, 5 * cells_z
    )
    live_now = live_count[0]
    slot_alive = jnp.arange(npar_local) < live_now
    alive_mask = slot_alive.astype(jnp.float32)
    plane_ids = parcel_cell // cells_z
    radial_ids = parcel_cell % cells_z
    plane_hot = (plane_ids[:, None] == jnp.arange(plane_count)[None, :]).astype(jnp.float32)
    radial_hot = (radial_ids[:, None] == jnp.arange(cells_z)[None, :]).astype(jnp.float32)
    gas_rows = jnp.dot(plane_hot, gas_table, precision=HIGHEST).reshape(npar_local, 5, cells_z)
    gas_values = jnp.sum(gas_rows * radial_hot[:, None, :], axis=2).T
    stacked = jnp.stack([(parcel_dest == d + 1) & slot_alive for d in range(4)]).astype(jnp.int32)
    ranks = jnp.cumsum(stacked, axis=1) - 1
    mover = jnp.sum(stacked, axis=0) > 0
    target = jnp.where(mover, jnp.sum(stacked * (jnp.arange(4)[:, None] * CAP + ranks), axis=0), -1)
    select = (target[:, None] == jnp.arange(4 * CAP)[None, :]).astype(jnp.float32)
    raw = jnp.concatenate([parcel_state, gas_values, alive_mask[None]], axis=0)
    leaving = jnp.transpose(
        jnp.dot(raw, select, precision=HIGHEST).reshape(raw.shape[0], 4, CAP), (1, 0, 2)
    )
    parcel_steps = [(-1, 0), (1, 0), (0, -1), (0, 1)]
    faces = [(sa, sz) for sa, sz in NEIGHBOURS if sa == 0 or sz == 0]
    items = [(rim_slab(state, 2, sa, sz), (sa, sz)) for sa, sz in faces]
    items += [(rim_slab(velocity, ITERS + 1, sa, sz), (sa, sz)) for sa, sz in NEIGHBOURS]
    got = neighbour_exchange(items)
    count = len(faces)
    state_rims = {(-sa, -sz): got[k] for k, (sa, sz) in enumerate(faces)}
    velocity_rims = {
        (-sa, -sz): got[count + k] for k, (sa, sz) in enumerate(NEIGHBOURS)
    }
    whole_pad = assemble(state, state_rims)
    whole_pad = radial_pad(clear_ends(whole_pad, 2, 1), 2, "edge")
    moving = whole_pad[1:]
    density_pad = whole_pad[0]
    density_rim = 2
    vel_pad = moving[0:3]
    wide_velocity = assemble(velocity, velocity_rims)
    wide_velocity = radial_pad(clear_ends(wide_velocity, ITERS + 1, 1), 1, "edge")
    parcel_items = [(leaving[d], parcel_steps[d]) for d in range(4)]
    padded_pressure, fastest, landed = solve_pressure(wide_velocity, velocity, parcel_items)
    step_size = CFL / (fastest + 1e-06)
    transported = transport(
        moving[3:], vel_pad, density_pad, density_rim, diff_coef[:, None, None, None], step_size
    )
    updated, sources = evaporate(parcel_state, gas_values, alive_mask, step_size)
    spread = (sources.T[:, :, None] * radial_hot[:, None, :]).reshape(npar_local, 2 * cells_z)
    deposit = lax.dot_general(plane_hot, spread, (((0,), (0,)), ((), ())), precision=HIGHEST)
    deposit = jnp.transpose(deposit.reshape(cells_x, cells_y, 2, cells_z), (2, 0, 1, 3))
    scalars_new = jnp.concatenate(
        [transported[:2] + deposit / state[0][None], transported[2:]], axis=0
    )
    at_first = lax.axis_index("axial") == 0
    at_last = lax.axis_index("axial") == lax.axis_size("axial") - 1
    arriving = []
    for d in range(4):
        payload = landed[d]
        if d == 0:
            payload = jnp.where(at_last, jnp.float32(0.0), payload)
        if d == 1:
            payload = jnp.where(at_first, jnp.float32(0.0), payload)
        moved, _ = evaporate(payload[:8], payload[8:13], payload[13], step_size)
        arriving.append(moved)
    arrived = jnp.stack(arriving)
    kept_parcels = jnp.where((parcel_dest == 0)[None], updated, jnp.float32(0.0))
    velocity_new = jnp.stack(
        [
            velocity[d]
            - 0.5 * (shifted(padded_pressure, 1, d, 1) - shifted(padded_pressure, 1, d, -1))
            for d in range(3)
        ]
    )
    return (scalars_new, velocity_new, kept_parcels, arrived)


def solution(mesh):
    in_specs = (
        P(None, "axial", "azim", None),
        P(),
        P(None, ("axial", "azim")),
        P(("axial", "azim")),
        P(("axial", "azim")),
        P(("axial", "azim")),
    )
    out_specs = (
        P(None, "axial", "azim", None),
        P(None, "axial", "azim", None),
        P(None, ("axial", "azim")),
        P(None, None, ("axial", "azim")),
    )
    return jax.shard_map(
        on_device, mesh=mesh, in_specs=in_specs, out_specs=out_specs, check_vma=False
    )
```

```python
import jax
import jax.numpy as jnp
from jax import lax
from jax.sharding import PartitionSpec as P
from jax.experimental import pallas as pl
from jax.experimental.pallas import tpu as pltpu

CAP = 64
ITERS = 4


CFL = 0.4
SHIFT_PRESSURE = 0.25
EVAP = 8.0
RELAX = 4.0
DRAG = 6.0
LATENT = 0.5
HEAT_CAP = 0.8
HIGHEST = lax.Precision.HIGHEST


def extended(block, sides, width):
    for axis, dim in sides:
        count = lax.axis_size(axis)
        forward = [(i, i + 1) for i in range(count - 1)]
        forward.append((count - 1, 0))
        backward = [(target, source) for source, target in forward]
        low = lax.ppermute(
            lax.slice_in_dim(block, block.shape[dim] - width, None, axis=dim), axis, forward
        )
        high = lax.ppermute(lax.slice_in_dim(block, 0, width, axis=dim), axis, backward)
        block = jnp.concatenate([low, block, high], axis=dim)
    return block


def exchange_kernel(offsets, *refs):
    count = len(offsets)
    sources = refs[:count]
    outs = refs[count : 2 * count]
    send_sems, recv_sems = refs[2 * count :]
    axial = lax.axis_index("axial")
    azim = lax.axis_index("azim")

    def device(step_axial, step_azim):
        return (
            (axial + step_axial + lax.axis_size("axial")) % lax.axis_size("axial"),
            (azim + step_azim + lax.axis_size("azim")) % lax.axis_size("azim"),
        )

    has_low = axial > 0
    has_high = axial < lax.axis_size("axial") - 1

    def reachable(step_axial):
        if step_axial < 0:
            return has_low
        if step_axial > 0:
            return has_high
        return None

    def guarded(condition, action):
        if condition is None:
            action()
        else:
            pl.when(condition)(action)

    neighbours = sorted(set(offsets))
    barrier = pltpu.get_barrier_semaphore()
    expected = 0
    for step in neighbours:

        def greet(step=step):
            pl.semaphore_signal(
                barrier, inc=1, device_id=device(*step), device_id_type=pl.DeviceIdType.MESH
            )

        guarded(reachable(step[0]), greet)
        condition = reachable(-step[0])
        expected = expected + (1 if condition is None else condition.astype(jnp.int32))
    pl.semaphore_wait(barrier, expected)
    copies = []
    order = sorted(range(count), key=lambda k: -abs(offsets[k][0]) - abs(offsets[k][1]))
    for k in order:
        step = offsets[k]
        copy = pltpu.make_async_remote_copy(
            src_ref=sources[k],
            dst_ref=outs[k],
            send_sem=send_sems.at[k],
            recv_sem=recv_sems.at[k],
            device_id=device(*step),
            device_id_type=pl.DeviceIdType.MESH,
        )
        guarded(reachable(step[0]), copy.start)
        copies.append((copy, step))
    for copy, step in copies:
        guarded(reachable(step[0]), copy.wait_send)
        guarded(reachable(-step[0]), copy.wait_recv)


def neighbour_exchange(items):
    offsets = [step for _, step in items]
    flat = [a for a, _ in items]
    count = len(flat)
    outs = pl.pallas_call(
        lambda *refs: exchange_kernel(offsets, *refs),
        out_shape=[jax.ShapeDtypeStruct(f.shape, f.dtype) for f in flat],
        in_specs=[pl.BlockSpec(memory_space=pl.ANY)] * count,
        out_specs=[pl.BlockSpec(memory_space=pl.ANY)] * count,
        scratch_shapes=[pltpu.SemaphoreType.DMA((count,)), pltpu.SemaphoreType.DMA((count,))],
        compiler_params=pltpu.CompilerParams(collective_id=1, has_side_effects=True),
    )(*flat)
    return list(outs)


def rim_slab(block, width, step_axial, step_azim):
    def pick(values, dim, step):
        if step > 0:
            return lax.slice_in_dim(values, values.shape[dim] - width, None, axis=dim)
        if step < 0:
            return lax.slice_in_dim(values, 0, width, axis=dim)
        return values

    return pick(pick(block, 1, step_axial), 2, step_azim)


NEIGHBOURS = [(sa, sz) for sa in (-1, 0, 1) for sz in (-1, 0, 1) if (sa, sz) != (0, 0)]


def assemble(block, received):
    rim_a = received[(-1, 0)].shape[1]
    rim_z = received[(0, -1)].shape[2]
    corner = block.shape[:1] + (rim_a, rim_z) + block.shape[3:]
    bands = []
    for pz in (-1, 0, 1):
        row = []
        for pa in (-1, 0, 1):
            if (pa, pz) == (0, 0):
                row.append(block)
            elif (pa, pz) in received:
                row.append(received[(pa, pz)])
            else:
                row.append(jnp.zeros(corner, block.dtype))
        bands.append(jnp.concatenate(row, axis=1))
    return jnp.concatenate(bands, axis=2)


def shifted_2(shard, axis, by):
    length = lax.axis_size(axis)
    pairs = [(i, i + by) for i in range(length) if 0 <= i + by < length]
    return lax.ppermute(shard, axis, pairs)


def shifted_3(shard, axis, by):
    length = lax.axis_size(axis)
    return lax.ppermute(shard, axis, [(i, (i + by) % length) for i in range(length)])


def shifted(padded, rim_width, direction, step_by):
    selector = []
    total_dims = padded.ndim
    for dim_index in range(total_dims):
        extent = padded.shape[dim_index]
        if dim_index == total_dims - 3 + direction:
            selector.append(slice(rim_width + step_by, extent - rim_width + step_by))
        elif dim_index >= total_dims - 3:
            selector.append(slice(rim_width, extent - rim_width))
        else:
            selector.append(slice(None))
    return padded[tuple(selector)]


def clear_ends(padded, rim_width, axial_dim):
    extent = padded.shape[axial_dim]
    at_first = lax.axis_index("axial") == 0
    at_last = lax.axis_index("axial") == lax.axis_size("axial") - 1
    shape_list = [1] * padded.ndim
    shape_list[axial_dim] = extent
    position = lax.broadcasted_iota(jnp.int32, tuple(shape_list), axial_dim)
    dropped = at_first & (position < rim_width) | at_last & (position >= extent - rim_width)
    return jnp.where(dropped, jnp.float32(0.0), padded)


def radial_pad(values, rim_width, radial_mode):
    return jnp.pad(
        values, [(0, 0)] * (values.ndim - 1) + [(rim_width, rim_width)], mode=radial_mode
    )


def transport(scalar_pad, vel_pad, density_pad, density_rim, diffusion, step_size):
    center = shifted(scalar_pad, 2, 0, 0)
    density = shifted(density_pad, density_rim, 0, 0)
    change = jnp.zeros_like(center)
    for direction in range(3):
        carried = vel_pad[direction] * scalar_pad
        advect = (
            -shifted(carried, 2, direction, 2)
            + 8.0 * shifted(carried, 2, direction, 1)
            - 8.0 * shifted(carried, 2, direction, -1)
            + shifted(carried, 2, direction, -2)
        ) / 12.0
        upper_flux = (
            0.5
            * diffusion
            * (density + shifted(density_pad, density_rim, direction, 1))
            * (shifted(scalar_pad, 2, direction, 1) - center)
        )
        lower_flux = (
            0.5
            * diffusion
            * (density + shifted(density_pad, density_rim, direction, -1))
            * (center - shifted(scalar_pad, 2, direction, -1))
        )
        change = change - advect + upper_flux - lower_flux
    return center + step_size * change


def evaporate(attrs, gas_values, alive_mask, step_size):
    parcel_mass = attrs[0]
    parcel_temp = attrs[1]
    parcel_vel = attrs[2:5]
    offsets = attrs[5:8]
    gas_heat = gas_values[3]
    gas_fuel = gas_values[4]
    evap_rate = EVAP * jax.nn.softplus(gas_heat - parcel_temp) * (1.0 - gas_fuel)
    new_mass = parcel_mass * jnp.exp(-step_size * evap_rate)
    lost_mass = parcel_mass - new_mass
    new_temp = parcel_temp + step_size * RELAX * (gas_heat - parcel_temp)
    new_vel = parcel_vel + step_size * DRAG * (gas_values[0:3] - parcel_vel)
    new_offsets = offsets + step_size * new_vel
    heat_source = -LATENT * lost_mass - HEAT_CAP * new_mass * (new_temp - parcel_temp)
    new_attrs = (
        jnp.concatenate([new_mass[None], new_temp[None], new_vel, new_offsets], axis=0)
        * alive_mask[None]
    )
    sources = jnp.stack([heat_source * alive_mask, lost_mass * alive_mask])
    return (new_attrs, sources)


def pressure_pad(values):
    padded = extended(values, (("axial", 0), ("azim", 1)), 1)
    return radial_pad(clear_ends(padded, 1, 0), 1, "constant")


def operate(values):
    padded = pressure_pad(values)
    beside = shifted(padded, 1, 0, 1) + shifted(padded, 1, 0, -1)
    beside = beside + shifted(padded, 1, 1, 1) + shifted(padded, 1, 1, -1)
    beside = beside + shifted(padded, 1, 2, 1) + shifted(padded, 1, 2, -1)
    return (6.0 + SHIFT_PRESSURE) * values - beside


def reduce_groups():
    axial = lax.axis_size("axial")
    along_x = 4 if axial % 4 == 0 else 1
    groups = [
        (("azim", 1, lax.axis_size("azim")), ("axial", 1, along_x)),
        (("axial", along_x, axial // along_x),),
    ]
    return [tuple(d for d in g if d[2] > 1) for g in groups if any(d[2] > 1 for d in g)]


def group_size(group):
    size = 1
    for _, _, count in group:
        size *= count
    return size


def coefficient_cg(gram, size, shift, half_width):
    def apply_a(c):
        out = [shift * c[j] for j in range(size)]
        for j in range(size - 1):
            if j == 0:
                out[1] = out[1] + half_width * c[0]
            else:
                out[j + 1] = out[j + 1] + 0.5 * half_width * c[j]
                out[j - 1] = out[j - 1] + 0.5 * half_width * c[j]
        return out

    def inner(a, b):
        acc = None
        for i in range(size):
            for j in range(size):
                if isinstance(a[i], float) and a[i] == 0.0:
                    continue
                if isinstance(b[j], float) and b[j] == 0.0:
                    continue
                term = a[i] * gram[i][j] * b[j]
                acc = term if acc is None else acc + term
        return acc

    solution_c = [0.0] * size
    residual = [1.0] + [0.0] * (size - 1)
    search = list(residual)
    norm_now = inner(residual, residual)
    for iteration in range(ITERS):
        image = apply_a(search)
        alpha = norm_now / inner(search, image)
        solution_c = [solution_c[j] + alpha * search[j] for j in range(size)]
        residual = [residual[j] - alpha * image[j] for j in range(size)]
        if iteration == ITERS - 1:
            break
        norm_next = inner(residual, residual)
        search = [residual[j] + norm_next / norm_now * search[j] for j in range(size)]
        norm_now = norm_next
    return solution_c


def reduce_kernel(groups, shift, half_width, vel_ref, *refs):
    size = ITERS + 1
    basis_refs = refs[:size]
    o_ref, slots, send_sems, recv_sems = refs[size:]
    here = {"axial": lax.axis_index("axial"), "azim": lax.axis_index("azim")}

    def member(group, m):
        coords = dict(here)
        for axis, stride, count in group:
            index = here[axis]
            base = index - ((index // stride) % count) * stride
            coords[axis] = base + (m % count) * stride
            m = m // count
        return (coords["axial"], coords["azim"])

    def position(group):
        place = 0
        weight = 1
        for axis, stride, count in group:
            place = place + ((here[axis] // stride) % count) * weight
            weight *= count
        return place

    barrier = pltpu.get_barrier_semaphore()
    greeted = 0
    for group in groups:
        count = group_size(group)
        mine = position(group)
        for m in range(1, count):
            pl.semaphore_signal(
                barrier,
                inc=1,
                device_id=member(group, (mine + m) % count),
                device_id_type=pl.DeviceIdType.MESH,
            )
            greeted += 1
    pl.semaphore_wait(barrier, greeted)
    row = lax.broadcasted_iota(jnp.int32, o_ref.shape, 0)
    lane = lax.broadcasted_iota(jnp.int32, o_ref.shape, 1)
    is_max = (row == 0) & (lane == 0)

    def total(x):
        return jnp.sum(jnp.sum(x, axis=0, keepdims=True), axis=1, keepdims=True)

    basis = [ref[...] for ref in basis_refs]
    pairs = [(i, j) for i in range(size) for j in range(i, size)]
    entries = [jnp.max(jnp.max(jnp.abs(vel_ref[...]), axis=0, keepdims=True), axis=1, keepdims=True)]
    entries += [total(basis[i] * basis[j]) for i, j in pairs]
    acc = jnp.zeros(o_ref.shape, jnp.float32)
    for n, entry in enumerate(entries):
        acc = jnp.where((row == 0) & (lane == n), entry, acc)
    offset = 0
    for group in groups:
        count = group_size(group)
        mine = position(group)
        slots[offset + mine] = acc
        copies = []
        for m in range(1, count):
            target = (mine + m) % count
            copy = pltpu.make_async_remote_copy(
                src_ref=slots.at[offset + mine],
                dst_ref=slots.at[offset + mine],
                send_sem=send_sems.at[offset + target],
                recv_sem=recv_sems.at[offset + mine],
                device_id=member(group, target),
                device_id_type=pl.DeviceIdType.MESH,
            )
            copy.start()
            copies.append(copy)
        for copy in copies:
            copy.wait_send()
        for m in range(count):
            incoming = pltpu.make_async_remote_copy(
                src_ref=slots.at[offset + m],
                dst_ref=slots.at[offset + m],
                send_sem=send_sems.at[offset + m],
                recv_sem=recv_sems.at[offset + m],
                device_id=member(group, m),
                device_id_type=pl.DeviceIdType.MESH,
            )

            @pl.when(m != mine)
            def _():
                incoming.wait_recv()

        combined = slots[offset]
        for m in range(1, count):
            other = slots[offset + m]
            combined = jnp.where(is_max, jnp.maximum(combined, other), combined + other)
        acc = combined
        offset += count
    first = acc[0:1, :]
    first_lane = lax.broadcasted_iota(jnp.int32, first.shape, 1)

    def entry_at(n):
        return jnp.sum(jnp.where(first_lane == n, first, 0.0), axis=1, keepdims=True)

    gram = [[None] * size for _ in range(size)]
    for n, (i, j) in enumerate(pairs):
        gram[i][j] = entry_at(n + 1)
        gram[j][i] = gram[i][j]
    coefficients = coefficient_cg(gram, size, shift, half_width)
    out = jnp.where(lane == ITERS, entry_at(0), 0.0)
    for j in range(ITERS):
        out = jnp.where((lane == j), coefficients[j], out)
    o_ref[...] = out


def pressure_coefficients(velocity, basis, shift, half_width):
    groups = reduce_groups()
    slot_count = sum(group_size(group) for group in groups)
    flat = [v.reshape(-1, v.shape[-1]) for v in basis]
    out = pl.pallas_call(
        lambda *refs: reduce_kernel(groups, shift, half_width, *refs),
        out_shape=jax.ShapeDtypeStruct((8, 128), jnp.float32),
        in_specs=[pl.BlockSpec(memory_space=pltpu.VMEM)] * (1 + len(flat)),
        out_specs=pl.BlockSpec(memory_space=pltpu.VMEM),
        scratch_shapes=[
            pltpu.VMEM((slot_count, 8, 128), jnp.float32),
            pltpu.SemaphoreType.DMA((slot_count,)),
            pltpu.SemaphoreType.DMA((slot_count,)),
        ],
        compiler_params=pltpu.CompilerParams(collective_id=0, has_side_effects=True),
    )(velocity.reshape(-1, velocity.shape[-1]), *flat)
    return [out[0, j] for j in range(ITERS)], out[0, ITERS]


def neighbour_sum(padded):
    beside = shifted(padded, 1, 0, 1) + shifted(padded, 1, 0, -1)
    beside = beside + shifted(padded, 1, 1, 1) + shifted(padded, 1, 1, -1)
    return beside + shifted(padded, 1, 2, 1) + shifted(padded, 1, 2, -1)


def axial_valid(values, rim):
    extent = values.shape[0]
    inner_x = extent - 2 * rim
    first = lax.axis_index("axial") * inner_x - rim
    position = first + lax.broadcasted_iota(jnp.int32, (extent, 1, 1), 0)
    inside = (position >= 0) & (position < inner_x * lax.axis_size("axial"))
    return jnp.where(inside, values, jnp.float32(0.0))


def crop(values, by):
    if by == 0:
        return values
    return values[by:-by, by:-by]


def neighbour_sum_wide(values):
    padded = jnp.pad(values, [(0, 0), (0, 0), (1, 1)])
    nx, ny, nz = padded.shape

    def at(dx, dy, dz):
        return padded[1 + dx : nx - 1 + dx, 1 + dy : ny - 1 + dy, 1 + dz : nz - 1 + dz]

    beside = at(1, 0, 0) + at(-1, 0, 0)
    beside = beside + at(0, 1, 0) + at(0, -1, 0)
    return beside + at(0, 0, 1) + at(0, 0, -1)


def solve_pressure(wide_velocity, velocity):
    half_width = 6.0
    u = wide_velocity
    divergence = 0.5 * (u[0, 2:, 1:-1, 1:-1] - u[0, :-2, 1:-1, 1:-1])
    divergence = divergence + 0.5 * (u[1, 1:-1, 2:, 1:-1] - u[1, 1:-1, :-2, 1:-1])
    divergence = divergence + 0.5 * (u[2, 1:-1, 1:-1, 2:] - u[2, 1:-1, 1:-1, :-2])
    basis = [axial_valid(divergence, ITERS)]
    for j in range(ITERS):
        scaled = neighbour_sum_wide(basis[j]) * (-1.0 / half_width)
        if j == 0:
            fresh = scaled
        else:
            fresh = 2.0 * scaled - crop(basis[j - 1], 2)
        basis.append(axial_valid(fresh, ITERS - 1 - j))
    interior = [crop(basis[j], ITERS - j) for j in range(ITERS + 1)]
    coefficients, fastest = pressure_coefficients(
        velocity, interior, 6.0 + SHIFT_PRESSURE, half_width
    )
    padded_basis = [radial_pad(crop(basis[j], ITERS - j - 1), 1, "constant") for j in range(ITERS)]
    padded_pressure = coefficients[0] * padded_basis[0]
    for j in range(1, ITERS):
        padded_pressure = padded_pressure + coefficients[j] * padded_basis[j]
    return padded_pressure, fastest


def along_axial(buffer, step_by):
    return shifted_2(buffer, "axial", step_by)


def along_azim(buffer, step_by):
    return shifted_3(buffer, "azim", step_by)


def on_device(state, diff_coef, parcel_state, parcel_cell, parcel_dest, live_count):
    velocity = state[1:4]
    npar_local = parcel_cell.shape[0]
    cells_x, cells_y, cells_z = (state.shape[1], state.shape[2], state.shape[3])
    plane_count = cells_x * cells_y
    gas_table = jnp.transpose(state[1:6].reshape(5, plane_count, cells_z), (1, 0, 2)).reshape(
        plane_count, 5 * cells_z
    )
    live_now = live_count[0]
    slot_alive = jnp.arange(npar_local) < live_now
    alive_mask = slot_alive.astype(jnp.float32)
    plane_ids = parcel_cell // cells_z
    radial_ids = parcel_cell % cells_z
    plane_hot = (plane_ids[:, None] == jnp.arange(plane_count)[None, :]).astype(jnp.float32)
    radial_hot = (radial_ids[:, None] == jnp.arange(cells_z)[None, :]).astype(jnp.float32)
    gas_rows = jnp.dot(plane_hot, gas_table, precision=HIGHEST).reshape(npar_local, 5, cells_z)
    gas_values = jnp.sum(gas_rows * radial_hot[:, None, :], axis=2).T
    stacked = jnp.stack([(parcel_dest == d + 1) & slot_alive for d in range(4)]).astype(jnp.int32)
    ranks = jnp.cumsum(stacked, axis=1) - 1
    mover = jnp.sum(stacked, axis=0) > 0
    target = jnp.where(mover, jnp.sum(stacked * (jnp.arange(4)[:, None] * CAP + ranks), axis=0), -1)
    select = (target[:, None] == jnp.arange(4 * CAP)[None, :]).astype(jnp.float32)
    raw = jnp.concatenate([parcel_state, gas_values, alive_mask[None]], axis=0)
    leaving = jnp.transpose(
        jnp.dot(raw, select, precision=HIGHEST).reshape(raw.shape[0], 4, CAP), (1, 0, 2)
    )
    parcel_steps = [(-1, 0), (1, 0), (0, -1), (0, 1)]
    faces = [(sa, sz) for sa, sz in NEIGHBOURS if sa == 0 or sz == 0]
    items = [(rim_slab(state, 2, sa, sz), (sa, sz)) for sa, sz in faces]
    items += [(rim_slab(velocity, ITERS + 1, sa, sz), (sa, sz)) for sa, sz in NEIGHBOURS]
    items += [(leaving[d], parcel_steps[d]) for d in range(4)]
    got = neighbour_exchange(items)
    count = len(faces)
    state_rims = {(-sa, -sz): got[k] for k, (sa, sz) in enumerate(faces)}
    velocity_rims = {
        (-sa, -sz): got[count + k] for k, (sa, sz) in enumerate(NEIGHBOURS)
    }
    landed = got[count + len(NEIGHBOURS) :]
    whole_pad = assemble(state, state_rims)
    whole_pad = radial_pad(clear_ends(whole_pad, 2, 1), 2, "edge")
    moving = whole_pad[1:]
    density_pad = whole_pad[0]
    density_rim = 2
    vel_pad = moving[0:3]
    wide_velocity = assemble(velocity, velocity_rims)
    wide_velocity = radial_pad(clear_ends(wide_velocity, ITERS + 1, 1), 1, "edge")
    padded_pressure, fastest = solve_pressure(wide_velocity, velocity)
    step_size = CFL / (fastest + 1e-06)
    transported = transport(
        moving[3:], vel_pad, density_pad, density_rim, diff_coef[:, None, None, None], step_size
    )
    updated, sources = evaporate(parcel_state, gas_values, alive_mask, step_size)
    spread = (sources.T[:, :, None] * radial_hot[:, None, :]).reshape(npar_local, 2 * cells_z)
    deposit = lax.dot_general(plane_hot, spread, (((0,), (0,)), ((), ())), precision=HIGHEST)
    deposit = jnp.transpose(deposit.reshape(cells_x, cells_y, 2, cells_z), (2, 0, 1, 3))
    scalars_new = jnp.concatenate(
        [transported[:2] + deposit / state[0][None], transported[2:]], axis=0
    )
    at_first = lax.axis_index("axial") == 0
    at_last = lax.axis_index("axial") == lax.axis_size("axial") - 1
    arriving = []
    for d in range(4):
        payload = landed[d]
        if d == 0:
            payload = jnp.where(at_last, jnp.float32(0.0), payload)
        if d == 1:
            payload = jnp.where(at_first, jnp.float32(0.0), payload)
        moved, _ = evaporate(payload[:8], payload[8:13], payload[13], step_size)
        arriving.append(moved)
    arrived = jnp.stack(arriving)
    kept_parcels = jnp.where((parcel_dest == 0)[None], updated, jnp.float32(0.0))
    velocity_new = jnp.stack(
        [
            velocity[d]
            - 0.5 * (shifted(padded_pressure, 1, d, 1) - shifted(padded_pressure, 1, d, -1))
            for d in range(3)
        ]
    )
    return (scalars_new, velocity_new, kept_parcels, arrived)


def solution(mesh):
    in_specs = (
        P(None, "axial", "azim", None),
        P(),
        P(None, ("axial", "azim")),
        P(("axial", "azim")),
        P(("axial", "azim")),
        P(("axial", "azim")),
    )
    out_specs = (
        P(None, "axial", "azim", None),
        P(None, "axial", "azim", None),
        P(None, ("axial", "azim")),
        P(None, None, ("axial", "azim")),
    )
    return jax.shard_map(
        on_device, mesh=mesh, in_specs=in_specs, out_specs=out_specs, check_vma=False
    )
```

```python
import jax
import jax.numpy as jnp
from jax import lax
from jax.sharding import PartitionSpec as P
from jax.experimental import pallas as pl
from jax.experimental.pallas import tpu as pltpu

CAP = 64
ITERS = 4


CFL = 0.4
SHIFT_PRESSURE = 0.25
EVAP = 8.0
RELAX = 4.0
DRAG = 6.0
LATENT = 0.5
HEAT_CAP = 0.8
HIGHEST = lax.Precision.HIGHEST


def extended(block, sides, width):
    for axis, dim in sides:
        count = lax.axis_size(axis)
        forward = [(i, i + 1) for i in range(count - 1)]
        forward.append((count - 1, 0))
        backward = [(target, source) for source, target in forward]
        low = lax.ppermute(
            lax.slice_in_dim(block, block.shape[dim] - width, None, axis=dim), axis, forward
        )
        high = lax.ppermute(lax.slice_in_dim(block, 0, width, axis=dim), axis, backward)
        block = jnp.concatenate([low, block, high], axis=dim)
    return block


def exchange_kernel(offsets, *refs):
    count = len(offsets)
    sources = refs[:count]
    outs = refs[count : 2 * count]
    send_sems, recv_sems = refs[2 * count :]
    axial = lax.axis_index("axial")
    azim = lax.axis_index("azim")

    def device(step_axial, step_azim):
        return (
            (axial + step_axial + lax.axis_size("axial")) % lax.axis_size("axial"),
            (azim + step_azim + lax.axis_size("azim")) % lax.axis_size("azim"),
        )

    has_low = axial > 0
    has_high = axial < lax.axis_size("axial") - 1

    def reachable(step_axial):
        if step_axial < 0:
            return has_low
        if step_axial > 0:
            return has_high
        return None

    def guarded(condition, action):
        if condition is None:
            action()
        else:
            pl.when(condition)(action)

    neighbours = sorted(set(offsets))
    barrier = pltpu.get_barrier_semaphore()
    expected = 0
    for step in neighbours:

        def greet(step=step):
            pl.semaphore_signal(
                barrier, inc=1, device_id=device(*step), device_id_type=pl.DeviceIdType.MESH
            )

        guarded(reachable(step[0]), greet)
        condition = reachable(-step[0])
        expected = expected + (1 if condition is None else condition.astype(jnp.int32))
    pl.semaphore_wait(barrier, expected)
    copies = []
    order = sorted(range(count), key=lambda k: -abs(offsets[k][0]) - abs(offsets[k][1]))
    for k in order:
        step = offsets[k]
        copy = pltpu.make_async_remote_copy(
            src_ref=sources[k],
            dst_ref=outs[k],
            send_sem=send_sems.at[k],
            recv_sem=recv_sems.at[k],
            device_id=device(*step),
            device_id_type=pl.DeviceIdType.MESH,
        )
        guarded(reachable(step[0]), copy.start)
        copies.append((copy, step))
    for copy, step in copies:
        guarded(reachable(step[0]), copy.wait_send)
        guarded(reachable(-step[0]), copy.wait_recv)


def neighbour_exchange(items):
    offsets = [step for _, step in items]
    flat = [a for a, _ in items]
    count = len(flat)
    outs = pl.pallas_call(
        lambda *refs: exchange_kernel(offsets, *refs),
        out_shape=[jax.ShapeDtypeStruct(f.shape, f.dtype) for f in flat],
        in_specs=[pl.BlockSpec(memory_space=pl.ANY)] * count,
        out_specs=[pl.BlockSpec(memory_space=pl.ANY)] * count,
        scratch_shapes=[pltpu.SemaphoreType.DMA((count,)), pltpu.SemaphoreType.DMA((count,))],
        compiler_params=pltpu.CompilerParams(collective_id=1, has_side_effects=True),
    )(*flat)
    return list(outs)


def rim_slab(block, width, step_axial, step_azim):
    def pick(values, dim, step):
        if step > 0:
            return lax.slice_in_dim(values, values.shape[dim] - width, None, axis=dim)
        if step < 0:
            return lax.slice_in_dim(values, 0, width, axis=dim)
        return values

    return pick(pick(block, 1, step_axial), 2, step_azim)


NEIGHBOURS = [(sa, sz) for sa in (-1, 0, 1) for sz in (-1, 0, 1) if (sa, sz) != (0, 0)]


def assemble(block, received):
    rim_a = received[(-1, 0)].shape[1]
    rim_z = received[(0, -1)].shape[2]
    corner = block.shape[:1] + (rim_a, rim_z) + block.shape[3:]
    bands = []
    for pz in (-1, 0, 1):
        row = []
        for pa in (-1, 0, 1):
            if (pa, pz) == (0, 0):
                row.append(block)
            elif (pa, pz) in received:
                row.append(received[(pa, pz)])
            else:
                row.append(jnp.zeros(corner, block.dtype))
        bands.append(jnp.concatenate(row, axis=1))
    return jnp.concatenate(bands, axis=2)


def shifted_2(shard, axis, by):
    length = lax.axis_size(axis)
    pairs = [(i, i + by) for i in range(length) if 0 <= i + by < length]
    return lax.ppermute(shard, axis, pairs)


def shifted_3(shard, axis, by):
    length = lax.axis_size(axis)
    return lax.ppermute(shard, axis, [(i, (i + by) % length) for i in range(length)])


def shifted(padded, rim_width, direction, step_by):
    selector = []
    total_dims = padded.ndim
    for dim_index in range(total_dims):
        extent = padded.shape[dim_index]
        if dim_index == total_dims - 3 + direction:
            selector.append(slice(rim_width + step_by, extent - rim_width + step_by))
        elif dim_index >= total_dims - 3:
            selector.append(slice(rim_width, extent - rim_width))
        else:
            selector.append(slice(None))
    return padded[tuple(selector)]


def clear_ends(padded, rim_width, axial_dim):
    extent = padded.shape[axial_dim]
    at_first = lax.axis_index("axial") == 0
    at_last = lax.axis_index("axial") == lax.axis_size("axial") - 1
    shape_list = [1] * padded.ndim
    shape_list[axial_dim] = extent
    position = lax.broadcasted_iota(jnp.int32, tuple(shape_list), axial_dim)
    dropped = at_first & (position < rim_width) | at_last & (position >= extent - rim_width)
    return jnp.where(dropped, jnp.float32(0.0), padded)


def radial_pad(values, rim_width, radial_mode):
    return jnp.pad(
        values, [(0, 0)] * (values.ndim - 1) + [(rim_width, rim_width)], mode=radial_mode
    )


def transport(scalar_pad, vel_pad, density_pad, density_rim, diffusion, step_size):
    center = shifted(scalar_pad, 2, 0, 0)
    density = shifted(density_pad, density_rim, 0, 0)
    change = jnp.zeros_like(center)
    for direction in range(3):
        carried = vel_pad[direction] * scalar_pad
        advect = (
            -shifted(carried, 2, direction, 2)
            + 8.0 * shifted(carried, 2, direction, 1)
            - 8.0 * shifted(carried, 2, direction, -1)
            + shifted(carried, 2, direction, -2)
        ) / 12.0
        upper_flux = (
            0.5
            * diffusion
            * (density + shifted(density_pad, density_rim, direction, 1))
            * (shifted(scalar_pad, 2, direction, 1) - center)
        )
        lower_flux = (
            0.5
            * diffusion
            * (density + shifted(density_pad, density_rim, direction, -1))
            * (center - shifted(scalar_pad, 2, direction, -1))
        )
        change = change - advect + upper_flux - lower_flux
    return center + step_size * change


def evaporate(attrs, gas_values, alive_mask, step_size):
    parcel_mass = attrs[0]
    parcel_temp = attrs[1]
    parcel_vel = attrs[2:5]
    offsets = attrs[5:8]
    gas_heat = gas_values[3]
    gas_fuel = gas_values[4]
    evap_rate = EVAP * jax.nn.softplus(gas_heat - parcel_temp) * (1.0 - gas_fuel)
    new_mass = parcel_mass * jnp.exp(-step_size * evap_rate)
    lost_mass = parcel_mass - new_mass
    new_temp = parcel_temp + step_size * RELAX * (gas_heat - parcel_temp)
    new_vel = parcel_vel + step_size * DRAG * (gas_values[0:3] - parcel_vel)
    new_offsets = offsets + step_size * new_vel
    heat_source = -LATENT * lost_mass - HEAT_CAP * new_mass * (new_temp - parcel_temp)
    new_attrs = (
        jnp.concatenate([new_mass[None], new_temp[None], new_vel, new_offsets], axis=0)
        * alive_mask[None]
    )
    sources = jnp.stack([heat_source * alive_mask, lost_mass * alive_mask])
    return (new_attrs, sources)


def pressure_pad(values):
    padded = extended(values, (("axial", 0), ("azim", 1)), 1)
    return radial_pad(clear_ends(padded, 1, 0), 1, "constant")


def operate(values):
    padded = pressure_pad(values)
    beside = shifted(padded, 1, 0, 1) + shifted(padded, 1, 0, -1)
    beside = beside + shifted(padded, 1, 1, 1) + shifted(padded, 1, 1, -1)
    beside = beside + shifted(padded, 1, 2, 1) + shifted(padded, 1, 2, -1)
    return (6.0 + SHIFT_PRESSURE) * values - beside


def reduce_groups():
    axial = lax.axis_size("axial")
    along_x = 4 if axial % 4 == 0 else 1
    groups = [
        (("azim", 1, lax.axis_size("azim")), ("axial", 1, along_x)),
        (("axial", along_x, axial // along_x),),
    ]
    return [tuple(d for d in g if d[2] > 1) for g in groups if any(d[2] > 1 for d in g)]


def group_size(group):
    size = 1
    for _, _, count in group:
        size *= count
    return size


def coefficient_cg(gram, size, shift, half_width):
    def apply_a(c):
        out = [shift * c[j] for j in range(size)]
        for j in range(size - 1):
            if j == 0:
                out[1] = out[1] + half_width * c[0]
            else:
                out[j + 1] = out[j + 1] + 0.5 * half_width * c[j]
                out[j - 1] = out[j - 1] + 0.5 * half_width * c[j]
        return out

    def inner(a, b):
        acc = None
        for i in range(size):
            for j in range(size):
                if isinstance(a[i], float) and a[i] == 0.0:
                    continue
                if isinstance(b[j], float) and b[j] == 0.0:
                    continue
                term = a[i] * gram[i][j] * b[j]
                acc = term if acc is None else acc + term
        return acc

    solution_c = [0.0] * size
    residual = [1.0] + [0.0] * (size - 1)
    search = list(residual)
    norm_now = inner(residual, residual)
    for iteration in range(ITERS):
        image = apply_a(search)
        alpha = norm_now / inner(search, image)
        solution_c = [solution_c[j] + alpha * search[j] for j in range(size)]
        residual = [residual[j] - alpha * image[j] for j in range(size)]
        if iteration == ITERS - 1:
            break
        norm_next = inner(residual, residual)
        search = [residual[j] + norm_next / norm_now * search[j] for j in range(size)]
        norm_now = norm_next
    return solution_c


def reduce_kernel(groups, shift, half_width, vel_ref, *refs):
    size = ITERS + 1
    basis_refs = refs[:size]
    o_ref, slots, send_sems, recv_sems = refs[size:]
    here = {"axial": lax.axis_index("axial"), "azim": lax.axis_index("azim")}

    def member(group, m):
        coords = dict(here)
        for axis, stride, count in group:
            index = here[axis]
            base = index - ((index // stride) % count) * stride
            coords[axis] = base + (m % count) * stride
            m = m // count
        return (coords["axial"], coords["azim"])

    def position(group):
        place = 0
        weight = 1
        for axis, stride, count in group:
            place = place + ((here[axis] // stride) % count) * weight
            weight *= count
        return place

    barrier = pltpu.get_barrier_semaphore()
    greeted = 0
    for group in groups:
        count = group_size(group)
        mine = position(group)
        for m in range(1, count):
            pl.semaphore_signal(
                barrier,
                inc=1,
                device_id=member(group, (mine + m) % count),
                device_id_type=pl.DeviceIdType.MESH,
            )
            greeted += 1
    row = lax.broadcasted_iota(jnp.int32, o_ref.shape, 0)
    lane = lax.broadcasted_iota(jnp.int32, o_ref.shape, 1)
    is_max = (row == 0) & (lane == 0)

    def total(x):
        return jnp.sum(jnp.sum(x, axis=0, keepdims=True), axis=1, keepdims=True)

    basis = [ref[...] for ref in basis_refs]
    pairs = [(i, j) for i in range(size) for j in range(i, size)]
    entries = [jnp.max(jnp.max(jnp.abs(vel_ref[...]), axis=0, keepdims=True), axis=1, keepdims=True)]
    entries += [total(basis[i] * basis[j]) for i, j in pairs]
    acc = jnp.zeros(o_ref.shape, jnp.float32)
    for n, entry in enumerate(entries):
        acc = jnp.where((row == 0) & (lane == n), entry, acc)
    pl.semaphore_wait(barrier, greeted)
    offset = 0
    for group in groups:
        count = group_size(group)
        mine = position(group)
        slots[offset + mine] = acc
        copies = []
        for m in range(1, count):
            target = (mine + m) % count
            copy = pltpu.make_async_remote_copy(
                src_ref=slots.at[offset + mine],
                dst_ref=slots.at[offset + mine],
                send_sem=send_sems.at[offset + target],
                recv_sem=recv_sems.at[offset + mine],
                device_id=member(group, target),
                device_id_type=pl.DeviceIdType.MESH,
            )
            copy.start()
            copies.append(copy)
        for copy in copies:
            copy.wait_send()
        for m in range(count):
            incoming = pltpu.make_async_remote_copy(
                src_ref=slots.at[offset + m],
                dst_ref=slots.at[offset + m],
                send_sem=send_sems.at[offset + m],
                recv_sem=recv_sems.at[offset + m],
                device_id=member(group, m),
                device_id_type=pl.DeviceIdType.MESH,
            )

            @pl.when(m != mine)
            def _():
                incoming.wait_recv()

        combined = slots[offset]
        for m in range(1, count):
            other = slots[offset + m]
            combined = jnp.where(is_max, jnp.maximum(combined, other), combined + other)
        acc = combined
        offset += count
    first = acc[0:1, :]
    first_lane = lax.broadcasted_iota(jnp.int32, first.shape, 1)

    def entry_at(n):
        return jnp.sum(jnp.where(first_lane == n, first, 0.0), axis=1, keepdims=True)

    gram = [[None] * size for _ in range(size)]
    for n, (i, j) in enumerate(pairs):
        gram[i][j] = entry_at(n + 1)
        gram[j][i] = gram[i][j]
    coefficients = coefficient_cg(gram, size, shift, half_width)
    out = jnp.where(lane == ITERS, entry_at(0), 0.0)
    for j in range(ITERS):
        out = jnp.where((lane == j), coefficients[j], out)
    o_ref[...] = out


def pressure_coefficients(velocity, basis, shift, half_width):
    groups = reduce_groups()
    slot_count = sum(group_size(group) for group in groups)
    flat = [v.reshape(-1, v.shape[-1]) for v in basis]
    out = pl.pallas_call(
        lambda *refs: reduce_kernel(groups, shift, half_width, *refs),
        out_shape=jax.ShapeDtypeStruct((8, 128), jnp.float32),
        in_specs=[pl.BlockSpec(memory_space=pltpu.VMEM)] * (1 + len(flat)),
        out_specs=pl.BlockSpec(memory_space=pltpu.VMEM),
        scratch_shapes=[
            pltpu.VMEM((slot_count, 8, 128), jnp.float32),
            pltpu.SemaphoreType.DMA((slot_count,)),
            pltpu.SemaphoreType.DMA((slot_count,)),
        ],
        compiler_params=pltpu.CompilerParams(collective_id=0, has_side_effects=True),
    )(velocity.reshape(-1, velocity.shape[-1]), *flat)
    return [out[0, j] for j in range(ITERS)], out[0, ITERS]


def neighbour_sum(padded):
    beside = shifted(padded, 1, 0, 1) + shifted(padded, 1, 0, -1)
    beside = beside + shifted(padded, 1, 1, 1) + shifted(padded, 1, 1, -1)
    return beside + shifted(padded, 1, 2, 1) + shifted(padded, 1, 2, -1)


def axial_valid(values, rim):
    extent = values.shape[0]
    inner_x = extent - 2 * rim
    first = lax.axis_index("axial") * inner_x - rim
    position = first + lax.broadcasted_iota(jnp.int32, (extent, 1, 1), 0)
    inside = (position >= 0) & (position < inner_x * lax.axis_size("axial"))
    return jnp.where(inside, values, jnp.float32(0.0))


def crop(values, by):
    if by == 0:
        return values
    return values[by:-by, by:-by]


def neighbour_sum_wide(values):
    padded = jnp.pad(values, [(0, 0), (0, 0), (1, 1)])
    nx, ny, nz = padded.shape

    def at(dx, dy, dz):
        return padded[1 + dx : nx - 1 + dx, 1 + dy : ny - 1 + dy, 1 + dz : nz - 1 + dz]

    beside = at(1, 0, 0) + at(-1, 0, 0)
    beside = beside + at(0, 1, 0) + at(0, -1, 0)
    return beside + at(0, 0, 1) + at(0, 0, -1)


def solve_pressure(wide_velocity, velocity):
    half_width = 6.0
    u = wide_velocity
    divergence = 0.5 * (u[0, 2:, 1:-1, 1:-1] - u[0, :-2, 1:-1, 1:-1])
    divergence = divergence + 0.5 * (u[1, 1:-1, 2:, 1:-1] - u[1, 1:-1, :-2, 1:-1])
    divergence = divergence + 0.5 * (u[2, 1:-1, 1:-1, 2:] - u[2, 1:-1, 1:-1, :-2])
    basis = [axial_valid(divergence, ITERS)]
    for j in range(ITERS):
        scaled = neighbour_sum_wide(basis[j]) * (-1.0 / half_width)
        if j == 0:
            fresh = scaled
        else:
            fresh = 2.0 * scaled - crop(basis[j - 1], 2)
        basis.append(axial_valid(fresh, ITERS - 1 - j))
    interior = [crop(basis[j], ITERS - j) for j in range(ITERS + 1)]
    coefficients, fastest = pressure_coefficients(
        velocity, interior, 6.0 + SHIFT_PRESSURE, half_width
    )
    padded_basis = [radial_pad(crop(basis[j], ITERS - j - 1), 1, "constant") for j in range(ITERS)]
    padded_pressure = coefficients[0] * padded_basis[0]
    for j in range(1, ITERS):
        padded_pressure = padded_pressure + coefficients[j] * padded_basis[j]
    return padded_pressure, fastest


def along_axial(buffer, step_by):
    return shifted_2(buffer, "axial", step_by)


def along_azim(buffer, step_by):
    return shifted_3(buffer, "azim", step_by)


def on_device(state, diff_coef, parcel_state, parcel_cell, parcel_dest, live_count):
    velocity = state[1:4]
    npar_local = parcel_cell.shape[0]
    cells_x, cells_y, cells_z = (state.shape[1], state.shape[2], state.shape[3])
    plane_count = cells_x * cells_y
    gas_table = jnp.transpose(state[1:6].reshape(5, plane_count, cells_z), (1, 0, 2)).reshape(
        plane_count, 5 * cells_z
    )
    live_now = live_count[0]
    slot_alive = jnp.arange(npar_local) < live_now
    alive_mask = slot_alive.astype(jnp.float32)
    plane_ids = parcel_cell // cells_z
    radial_ids = parcel_cell % cells_z
    plane_hot = (plane_ids[:, None] == jnp.arange(plane_count)[None, :]).astype(jnp.float32)
    radial_hot = (radial_ids[:, None] == jnp.arange(cells_z)[None, :]).astype(jnp.float32)
    gas_rows = jnp.dot(plane_hot, gas_table, precision=HIGHEST).reshape(npar_local, 5, cells_z)
    gas_values = jnp.sum(gas_rows * radial_hot[:, None, :], axis=2).T
    stacked = jnp.stack([(parcel_dest == d + 1) & slot_alive for d in range(4)]).astype(jnp.int32)
    ranks = jnp.cumsum(stacked, axis=1) - 1
    mover = jnp.sum(stacked, axis=0) > 0
    target = jnp.where(mover, jnp.sum(stacked * (jnp.arange(4)[:, None] * CAP + ranks), axis=0), -1)
    select = (target[:, None] == jnp.arange(4 * CAP)[None, :]).astype(jnp.float32)
    raw = jnp.concatenate([parcel_state, gas_values, alive_mask[None]], axis=0)
    leaving = jnp.transpose(
        jnp.dot(raw, select, precision=HIGHEST).reshape(raw.shape[0], 4, CAP), (1, 0, 2)
    )
    parcel_steps = [(-1, 0), (1, 0), (0, -1), (0, 1)]
    faces = [(sa, sz) for sa, sz in NEIGHBOURS if sa == 0 or sz == 0]
    items = [(rim_slab(state, 2, sa, sz), (sa, sz)) for sa, sz in faces]
    items += [(rim_slab(velocity, ITERS + 1, sa, sz), (sa, sz)) for sa, sz in NEIGHBOURS]
    items += [(leaving[d], parcel_steps[d]) for d in range(4)]
    got = neighbour_exchange(items)
    count = len(faces)
    state_rims = {(-sa, -sz): got[k] for k, (sa, sz) in enumerate(faces)}
    velocity_rims = {
        (-sa, -sz): got[count + k] for k, (sa, sz) in enumerate(NEIGHBOURS)
    }
    landed = got[count + len(NEIGHBOURS) :]
    whole_pad = assemble(state, state_rims)
    whole_pad = radial_pad(clear_ends(whole_pad, 2, 1), 2, "edge")
    moving = whole_pad[1:]
    density_pad = whole_pad[0]
    density_rim = 2
    vel_pad = moving[0:3]
    wide_velocity = assemble(velocity, velocity_rims)
    wide_velocity = radial_pad(clear_ends(wide_velocity, ITERS + 1, 1), 1, "edge")
    padded_pressure, fastest = solve_pressure(wide_velocity, velocity)
    step_size = CFL / (fastest + 1e-06)
    transported = transport(
        moving[3:], vel_pad, density_pad, density_rim, diff_coef[:, None, None, None], step_size
    )
    updated, sources = evaporate(parcel_state, gas_values, alive_mask, step_size)
    spread = (sources.T[:, :, None] * radial_hot[:, None, :]).reshape(npar_local, 2 * cells_z)
    deposit = lax.dot_general(plane_hot, spread, (((0,), (0,)), ((), ())), precision=HIGHEST)
    deposit = jnp.transpose(deposit.reshape(cells_x, cells_y, 2, cells_z), (2, 0, 1, 3))
    scalars_new = jnp.concatenate(
        [transported[:2] + deposit / state[0][None], transported[2:]], axis=0
    )
    at_first = lax.axis_index("axial") == 0
    at_last = lax.axis_index("axial") == lax.axis_size("axial") - 1
    arriving = []
    for d in range(4):
        payload = landed[d]
        if d == 0:
            payload = jnp.where(at_last, jnp.float32(0.0), payload)
        if d == 1:
            payload = jnp.where(at_first, jnp.float32(0.0), payload)
        moved, _ = evaporate(payload[:8], payload[8:13], payload[13], step_size)
        arriving.append(moved)
    arrived = jnp.stack(arriving)
    kept_parcels = jnp.where((parcel_dest == 0)[None], updated, jnp.float32(0.0))
    velocity_new = jnp.stack(
        [
            velocity[d]
            - 0.5 * (shifted(padded_pressure, 1, d, 1) - shifted(padded_pressure, 1, d, -1))
            for d in range(3)
        ]
    )
    return (scalars_new, velocity_new, kept_parcels, arrived)


def solution(mesh):
    in_specs = (
        P(None, "axial", "azim", None),
        P(),
        P(None, ("axial", "azim")),
        P(("axial", "azim")),
        P(("axial", "azim")),
        P(("axial", "azim")),
    )
    out_specs = (
        P(None, "axial", "azim", None),
        P(None, "axial", "azim", None),
        P(None, ("axial", "azim")),
        P(None, None, ("axial", "azim")),
    )
    return jax.shard_map(
        on_device, mesh=mesh, in_specs=in_specs, out_specs=out_specs, check_vma=False
    )
```
